256 devices in a mesh: dp: 8 (over y, core), tower: 32 (over x, z).
Axes of the slice: x: 4, y: 4, z: 8, core: 2. Of those that a mesh axis runs over, the one named last changes fastest.
Arguments:
- attn_out: bfloat16 [32768, 4096], P(('dp', 'tower')), may hold values from -0.375 to 0.375
- out_cot: bfloat16 [32768, 4096], P(('dp', 'tower')), may hold values from -6 to 6
- modality: int32 [32768], P(('dp', 'tower')), may hold values from 0 to 2, as said below
- group_modality: int32 [8], replicated, may hold values from 0 to 2, as said below
- o_weight: bfloat16 [32768, 4096], P('tower'), as said below
Outputs:
- attn_grad: bfloat16 [32768, 4096], P(('dp', 'tower'))
- weight_grad: bfloat16 [32768, 4096], P('tower', 'dp')
The draws below stay inside these ranges and needn't reach their ends.
Inputs may be any that keep to these rules, and one draw needn't show every extreme that they name: `group_modality`: every modality is served by at least one group. In each block of 128 tokens (one device's tokens), a modality served by k groups appears at most k * 24 times; in every block the modality served by the fewest groups (the lowest such id on a tie) appears exactly that often. `o_weight`: groups that serve the same modality hold equal rows.
All inputs are finite; a program needn't handle non-finite values.
Results may differ from the reference program's by a relative error of at most 0.014.
Values may be sent and summed in bfloat16 or wider, within the bound.
A program may use at most 128 MiB of HBM per device.

```python
import math
import jax
import jax.numpy as jnp
from jax import lax

D = 4096
TOK_DEV = 128
NGROUP = 8
CAP = 24
TOKENS = 32768
N_DP = 8
N_TOWER = 32


def group_table(key):
    first_key = jax.random.fold_in(key, 11)
    second_key = jax.random.fold_in(key, 12)
    extra = jax.random.randint(first_key, (NGROUP - 3,), 0, 3, dtype=jnp.int32)
    listed = jnp.concatenate([jnp.arange(3, dtype=jnp.int32), extra])
    return jax.random.permutation(second_key, listed)


def draw_group_modality(key, part):
    return group_table(key)


def draw_modality(key, part):
    table = group_table(key)
    modal_ids = jnp.arange(3, dtype=jnp.int32)
    per_kind = jnp.sum((table[:, None] == modal_ids[None, :]).astype(jnp.int32), axis=0)
    fewest = jnp.argmin(per_kind).astype(jnp.int32)
    slot_total = NGROUP * CAP
    slot_ids = jnp.arange(slot_total, dtype=jnp.int32)
    slot_kind = table[slot_ids // CAP]
    forced = slot_kind == fewest
    block_count = TOKENS // TOK_DEV
    block_keys = jax.random.split(jax.random.fold_in(key, 13), block_count)

    def one_block(block_key):
        score_key, order_key = jax.random.split(block_key)
        scores = jax.random.randint(score_key, (slot_total,), 0, 65536, dtype=jnp.int32) * slot_total + slot_ids
        scores = jnp.where(forced, 1073741824 + slot_ids, scores)
        _, picked = lax.top_k(scores, TOK_DEV)
        return jax.random.permutation(order_key, slot_kind[picked])
    return jax.vmap(one_block)(block_keys).reshape(-1).astype(jnp.int32)


def draw_o_weight(key, part):
    table = group_table(key)
    weight_key = jax.random.fold_in(key, 21)
    towers = jax.random.normal(weight_key, (3, D, D), jnp.float32) / math.sqrt(D)
    return towers[table].reshape(NGROUP * D, D).astype(jnp.bfloat16)


def level_of(own_key, shape, pieces, low, high):
    gain, own = 1.0, jax.random.fold_in(own_key, 6)
    for dim, blocks in pieces:
        steps = jnp.exp(jax.random.uniform(jax.random.fold_in(own, dim), (blocks,), jnp.float32, low / len(pieces), high / len(pieces)))
        gain = gain * jnp.repeat(steps, shape[dim] // blocks).reshape([-1 if axis == dim else 1 for axis in range(len(shape))])
    return gain


def scatter_about(key, shape, deviation, limit, pieces=(), kind=jnp.bfloat16):
    result = jax.random.normal(key, shape, jnp.float32) * deviation
    if len(pieces) > 0:
        result = level_of(key, shape, pieces, -0.22, 0.18) * result
    return jnp.clip(result, min=-limit, max=limit).astype(kind)


def setup_inputs(seed: int = 0) -> dict:
    key_of = jax.random.split(jax.random.key(seed), 6)
    attn_out = scatter_about(key_of[0], (TOKENS, D), 0.0625, 0.375, ((0, 256),))
    out_cot = scatter_about(key_of[1], (TOKENS, D), 1.0, 6.0, ((0, 256),))
    modality = draw_modality(jax.random.fold_in(key_of[5], 71), 0)
    group_modality = draw_group_modality(jax.random.fold_in(key_of[5], 71), 0)
    o_weight = draw_o_weight(jax.random.fold_in(key_of[5], 71), 0)
    return {"attn_out": attn_out, "out_cot": out_cot, "modality": modality, "group_modality": group_modality, "o_weight": o_weight}


def routing(modal_rows, tower_idx, group_modality):
    modal_ids = jnp.arange(3, dtype=jnp.int32)
    member = (modal_rows[:, None] == modal_ids[None, :]).astype(jnp.int32)
    before = jnp.cumsum(member, axis=0) - member
    order_in = jnp.sum(before * member, axis=1)
    group_of = (group_modality[:, None] == modal_ids[None, :]).astype(jnp.int32)
    per_kind = jnp.sum(group_of, axis=0)
    group_rank = jnp.sum((jnp.cumsum(group_of, axis=0) - group_of) * group_of, axis=1)
    how_many = jnp.sum(member * per_kind[None, :], axis=1)
    target = (order_in + tower_idx) % how_many
    chosen = (group_modality[None, :] == modal_rows[:, None]) & (group_rank[None, :] == target[:, None])
    group_ids = jnp.arange(group_modality.shape[0], dtype=jnp.int32)
    routed = jnp.sum(chosen.astype(jnp.int32) * group_ids[None, :], axis=1)
    slot_idx = order_in // how_many
    return routed, slot_idx


def reference(attn_out, out_cot, modality, group_modality, o_weight):
    blocks = N_DP * N_TOWER
    modal_rows = modality.reshape(blocks, TOK_DEV)
    towers = jnp.arange(blocks, dtype=jnp.int32) % N_TOWER
    routed, slot_idx = jax.vmap(routing, in_axes=(0, 0, None))(modal_rows, towers, group_modality)
    rows_per = N_TOWER * TOK_DEV
    slots_all = NGROUP * N_TOWER * CAP
    source = jnp.arange(N_TOWER, dtype=jnp.int32)[:, None]
    totals_init = jnp.zeros((NGROUP * D, D), jnp.float32)

    def row_step(totals, row_idx):
        route_row = lax.dynamic_slice_in_dim(routed, row_idx * N_TOWER, N_TOWER, 0)
        slot_row = lax.dynamic_slice_in_dim(slot_idx, row_idx * N_TOWER, N_TOWER, 0)
        landing = ((route_row * N_TOWER + source) * CAP + slot_row).reshape(-1).astype(jnp.int32)
        slot_table = jnp.full((slots_all,), rows_per, jnp.int32).at[landing].set(jnp.arange(rows_per, dtype=jnp.int32))
        slot_table = slot_table.reshape(NGROUP, N_TOWER * CAP)
        attn_row = lax.dynamic_slice_in_dim(attn_out, row_idx * rows_per, rows_per, 0)
        cot_row = lax.dynamic_slice_in_dim(out_cot, row_idx * rows_per, rows_per, 0)
        attn_pad = jnp.concatenate([attn_row, jnp.zeros((1, D), attn_row.dtype)], axis=0)
        cot_pad = jnp.concatenate([cot_row, jnp.zeros((1, D), cot_row.dtype)], axis=0)

        def group_step(carried, group_idx):
            grad_rows, totals_now = carried
            take_rows = slot_table[group_idx]
            attn_buf = attn_pad[take_rows]
            cot_buf = cot_pad[take_rows]
            weight = lax.dynamic_slice_in_dim(o_weight, group_idx * D, D, 0)
            grads = jnp.dot(cot_buf, weight.T, preferred_element_type=jnp.float32).astype(jnp.bfloat16)
            grad_rows = grad_rows.at[take_rows].set(grads, mode="drop")
            partial_value = jnp.dot(attn_buf.T, cot_buf, preferred_element_type=jnp.float32).astype(jnp.bfloat16)
            current = lax.dynamic_slice_in_dim(totals_now, group_idx * D, D, 0)
            totals_now = lax.dynamic_update_slice_in_dim(totals_now, current + partial_value.astype(jnp.float32), group_idx * D, 0)
            return (grad_rows, totals_now), None

        grad_init = jnp.zeros((rows_per, D), jnp.bfloat16)
        (grad_rows, totals), _ = lax.scan(group_step, (grad_init, totals), jnp.arange(NGROUP, dtype=jnp.int32))
        return totals, grad_rows

    totals, grad_all = lax.scan(row_step, totals_init, jnp.arange(N_DP, dtype=jnp.int32))
    return grad_all.reshape(TOKENS, D), totals.astype(jnp.bfloat16)
```

```python
import jax
import jax.numpy as jnp
from jax import lax
from jax.sharding import PartitionSpec as P

NGROUP = 8
CAP = 24


def routing(modal_rows, tower_idx, group_modality):
    modal_ids = jnp.arange(3, dtype=jnp.int32)
    member = (modal_rows[:, None] == modal_ids[None, :]).astype(jnp.int32)
    before = jnp.cumsum(member, axis=0) - member
    order_in = jnp.sum(before * member, axis=1)
    group_of = (group_modality[:, None] == modal_ids[None, :]).astype(jnp.int32)
    per_kind = jnp.sum(group_of, axis=0)
    group_rank = jnp.sum((jnp.cumsum(group_of, axis=0) - group_of) * group_of, axis=1)
    how_many = jnp.sum(member * per_kind[None, :], axis=1)
    target = (order_in + tower_idx) % how_many
    chosen = (group_modality[None, :] == modal_rows[:, None]) & (
        group_rank[None, :] == target[:, None]
    )
    group_ids = jnp.arange(group_modality.shape[0], dtype=jnp.int32)
    routed = jnp.sum(chosen.astype(jnp.int32) * group_ids[None, :], axis=1)
    slot_idx = order_in // how_many
    return (routed, slot_idx)


def per_device(attn_out, out_cot, modality, group_modality, o_weight):
    tower_idx = lax.axis_index("tower")
    tower_count = lax.axis_size("tower")
    group_size = tower_count // NGROUP
    piece_rows = o_weight.shape[0]
    model_width = attn_out.shape[1]
    tok_count = attn_out.shape[0]
    routed, slot_idx = routing(modality, tower_idx, group_modality)
    group_ids = jnp.arange(NGROUP, dtype=jnp.int32)
    slot_ids = jnp.arange(CAP, dtype=jnp.int32)
    dispatch = (
        (routed[None, None, :] == group_ids[:, None, None])
        & (slot_idx[None, None, :] == slot_ids[None, :, None])
    ).astype(jnp.bfloat16)
    cot_group = jnp.einsum(
        "gct,te->gce", dispatch, out_cot, preferred_element_type=jnp.float32
    ).astype(jnp.bfloat16)
    cot_send = jnp.broadcast_to(cot_group[:, None], (NGROUP, group_size, CAP, model_width)).reshape(
        tower_count, CAP, model_width
    )
    attn_send = jnp.einsum(
        "gct,tpe->gpce",
        dispatch,
        attn_out.reshape(tok_count, group_size, piece_rows),
        preferred_element_type=jnp.float32,
    ).astype(jnp.bfloat16).reshape(tower_count, CAP, piece_rows)
    attn_got = lax.all_to_all(attn_send, "tower", split_axis=0, concat_axis=0, tiled=True)
    cot_got = lax.all_to_all(cot_send, "tower", split_axis=0, concat_axis=0, tiled=True)
    grad_piece = lax.dot_general(
        cot_got, o_weight, (((2,), (1,)), ((), ())), preferred_element_type=jnp.float32
    ).astype(jnp.bfloat16)
    returned = lax.all_to_all(grad_piece, "tower", split_axis=0, concat_axis=0, tiled=True)
    returned_groups = returned.reshape(NGROUP, group_size, CAP, piece_rows)
    attn_grad = jnp.einsum(
        "gct,gpce->tpe", dispatch, returned_groups, preferred_element_type=jnp.float32
    )
    attn_grad = attn_grad.reshape(tok_count, model_width).astype(jnp.bfloat16)
    attn_rows = attn_got.reshape(tower_count * CAP, piece_rows)
    cot_rows = cot_got.reshape(tower_count * CAP, model_width)
    summed = lax.psum_scatter(
        lax.dot_general(
            cot_rows, attn_rows, (((0,), (0,)), ((), ())), preferred_element_type=jnp.float32
        ).astype(jnp.bfloat16),
        "dp",
        scatter_dimension=0,
        tiled=True,
    ).astype(jnp.float32)
    weight_grad = summed.T.astype(jnp.bfloat16)
    return (attn_grad, weight_grad)


def solution(mesh):
    return jax.shard_map(
        per_device,
        mesh=mesh,
        in_specs=(
            P(("dp", "tower"), None),
            P(("dp", "tower"), None),
            P(("dp", "tower")),
            P(),
            P("tower", None),
        ),
        out_specs=(P(("dp", "tower"), None), P("tower", "dp")),
        check_vma=False,
    )
```

```python
import functools

import jax
import jax.numpy as jnp
from jax import lax
from jax.experimental import pallas as pl
from jax.experimental.pallas import tpu as pltpu
from jax.sharding import PartitionSpec as P

NGROUP = 8
CAP = 24
NX = 4
NZ = 8
NC = 4
MESH = pl.DeviceIdType.MESH


def routing(modal_rows, tower_idx, group_modality):
    modal_ids = jnp.arange(3, dtype=jnp.int32)
    member = (modal_rows[:, None] == modal_ids[None, :]).astype(jnp.int32)
    before = jnp.cumsum(member, axis=0) - member
    order_in = jnp.sum(before * member, axis=1)
    group_of = (group_modality[:, None] == modal_ids[None, :]).astype(jnp.int32)
    per_kind = jnp.sum(group_of, axis=0)
    group_rank = jnp.sum((jnp.cumsum(group_of, axis=0) - group_of) * group_of, axis=1)
    how_many = jnp.sum(member * per_kind[None, :], axis=1)
    target = (order_in + tower_idx) % how_many
    chosen = (group_modality[None, :] == modal_rows[:, None]) & (
        group_rank[None, :] == target[:, None]
    )
    group_ids = jnp.arange(group_modality.shape[0], dtype=jnp.int32)
    routed = jnp.sum(chosen.astype(jnp.int32) * group_ids[None, :], axis=1)
    slot_idx = order_in // how_many
    return (routed, slot_idx)


def dispatch_kernel(
    dest_ref, cot_ref, out_ref, ring, dests, staged,
    dest_send, dest_recv, right_send, right_recv, left_send, left_recv, x_send, x_recv, own_sem,
):
    width = cot_ref.shape[1] // NC
    half = width // 2
    me = lax.axis_index("tower")
    my_x, my_z = me // NZ, me % NZ
    my_half = my_z // (NZ // 2)

    def at_z(z):
        return my_x * NZ + (z + NZ) % NZ

    def at_x(x):
        return ((x + NX) % NX) * NZ + my_z

    barrier = pltpu.get_barrier_semaphore()
    for k in range(1, NZ):
        pl.semaphore_signal(barrier, inc=1, device_id={"tower": at_z(my_z + k)}, device_id_type=MESH)
    for k in range(1, NX):
        pl.semaphore_signal(barrier, inc=1, device_id={"tower": at_x(my_x + k)}, device_id_type=MESH)
    pl.semaphore_wait(barrier, NZ - 1 + NX - 1)

    def dest_copy(k):
        return pltpu.make_async_remote_copy(
            src_ref=dest_ref,
            dst_ref=dests.at[NZ - k],
            send_sem=dest_send.at[k],
            recv_sem=dest_recv.at[NZ - k],
            device_id={"tower": at_z(my_z + k)},
            device_id_type=MESH,
        )

    def block(c, off):
        return cot_ref.at[:, pl.ds(c * width, width)] if off == 0 else ring.at[c, off % NZ]

    def ring_copy(c, s, right):
        off = -s if right else s
        src = block(c, off)
        dst = ring.at[c, (off - 1 if right else off + 1) % NZ]
        if s == NZ // 2 - 1:
            cols = pl.ds(0, half) if right else pl.ds(half, half)
            src, dst = src.at[:, cols], dst.at[:, cols]
        return pltpu.make_async_remote_copy(
            src_ref=src,
            dst_ref=dst,
            send_sem=(right_send if right else left_send).at[c, s],
            recv_sem=(right_recv if right else left_recv).at[c, s],
            device_id={"tower": at_z(my_z + (1 if right else -1))},
            device_id_type=MESH,
        )

    rows = lax.broadcasted_iota(jnp.int32, (NX * CAP, 128), 0)
    x_of = sum((rows >= CAP * k).astype(jnp.int32) for k in range(1, NX))
    wanted = rows + CAP * x_of + CAP * my_half

    def deliver(c, off):
        d = dest_ref[0:1, :] if off == 0 else dests[off % NZ, 0:1, :]
        pick = jnp.where(wanted == d, 1.0, 0.0).astype(jnp.bfloat16)
        got = jnp.dot(pick, block(c, off)[...], preferred_element_type=jnp.float32)
        got = got.astype(jnp.bfloat16)
        slot = off % NZ
        z_from = (my_z + off + NZ) % NZ
        for x in range(NX):
            staged[x, c, slot] = got[x * CAP:(x + 1) * CAP]

        for k in range(NX):
            x = (my_x + k) % NX
            src = staged.at[x, c, slot]
            dst = out_ref.at[my_x * NZ + z_from, :, pl.ds(c * width, width)]
            if k == 0:
                pltpu.make_async_copy(src, dst, own_sem).start()
            else:
                pltpu.make_async_remote_copy(
                    src_ref=src, dst_ref=dst, send_sem=x_send.at[k], recv_sem=x_recv.at[NX - k],
                    device_id={"tower": at_x(my_x + k)}, device_id_type=MESH,
                ).start()

    for k in range(1, NZ):
        dest_copy(k).start()

    for c0 in range(0, NC, 2):
        for s in range(NZ // 2):
            for c in (c0, c0 + 1):
                if s > 0:
                    ring_copy(c, s - 1, True).wait_recv()
                    ring_copy(c, s - 1, False).wait_recv()
                ring_copy(c, s, True).start()
                ring_copy(c, s, False).start()
                if c == 0 and s == 0:
                    for k in range(1, NZ):
                        dest_copy(k).wait_recv()
                if s == 0:
                    deliver(c, 0)
                else:
                    deliver(c, -s)
                    deliver(c, s)
        for c in (c0, c0 + 1):
            ring_copy(c, NZ // 2 - 1, True).wait_recv()
            ring_copy(c, NZ // 2 - 1, False).wait_recv()
            deliver(c, NZ // 2)

    for k in range(1, NZ):
        dest_copy(k).wait_send()
    for c in range(NC):
        for s in range(NZ // 2):
            ring_copy(c, s, True).wait_send()
            ring_copy(c, s, False).wait_send()
    for k in range(NX):
        x = (my_x + k) % NX
        src = staged.at[x]
        if k == 0:
            pltpu.make_async_copy(src, src, own_sem).wait()
        else:
            pltpu.make_async_copy(src, src, x_send.at[k]).wait()
            pltpu.make_async_copy(src, src, x_recv.at[k]).wait()


def dispatch_cot(dest, cot):
    tok, width = cot.shape[0], cot.shape[1] // NC
    return pl.pallas_call(
        dispatch_kernel,
        out_shape=jax.ShapeDtypeStruct((NX * NZ, CAP, NC * width), jnp.bfloat16),
        in_specs=[pl.BlockSpec(memory_space=pltpu.VMEM)] * 2,
        out_specs=pl.BlockSpec(memory_space=pl.ANY),
        scratch_shapes=[
            pltpu.VMEM((NC, NZ, tok, width), jnp.bfloat16),
            pltpu.VMEM((NZ, 8, 128), jnp.int32),
            pltpu.VMEM((NX, NC, NZ, CAP, width), jnp.bfloat16),
            pltpu.SemaphoreType.DMA((NZ,)),
            pltpu.SemaphoreType.DMA((NZ,)),
            pltpu.SemaphoreType.DMA((NC, NZ // 2)),
            pltpu.SemaphoreType.DMA((NC, NZ // 2)),
            pltpu.SemaphoreType.DMA((NC, NZ // 2)),
            pltpu.SemaphoreType.DMA((NC, NZ // 2)),
            pltpu.SemaphoreType.DMA((NX,)),
            pltpu.SemaphoreType.DMA((NX,)),
            pltpu.SemaphoreType.DMA,
        ],
        compiler_params=pltpu.CompilerParams(
            collective_id=0, has_side_effects=True, vmem_limit_bytes=40 * 1024 * 1024
        ),
        cost_estimate=pl.CostEstimate(flops=6_000_000_000, bytes_accessed=250_000_000, transcendentals=0),
        name="dispatch_cot",
    )(dest, cot)


def per_device(attn_out, out_cot, modality, group_modality, o_weight):
    tower_idx = lax.axis_index("tower")
    tower_count = lax.axis_size("tower")
    group_size = tower_count // NGROUP
    piece_rows = o_weight.shape[0]
    tok_count, model_width = attn_out.shape
    routed, slot_idx = routing(modality, tower_idx, group_modality)
    group_ids = jnp.arange(NGROUP, dtype=jnp.int32)
    slot_ids = jnp.arange(CAP, dtype=jnp.int32)
    dispatch = (
        (routed[None, None, :] == group_ids[:, None, None])
        & (slot_idx[None, None, :] == slot_ids[None, :, None])
    ).astype(jnp.bfloat16)
    attn_send = jnp.einsum(
        "gct,tpe->gpce",
        dispatch,
        attn_out.reshape(tok_count, group_size, piece_rows),
        preferred_element_type=jnp.float32,
    ).astype(jnp.bfloat16).reshape(tower_count, CAP, piece_rows)
    attn_got = lax.all_to_all(attn_send, "tower", split_axis=0, concat_axis=0, tiled=True)

    dest = jnp.broadcast_to((routed * CAP + slot_idx)[None, :], (8, tok_count))
    cot_got = dispatch_cot(dest, out_cot)

    grad_piece = lax.dot_general(
        cot_got, o_weight, (((2,), (1,)), ((), ())), preferred_element_type=jnp.float32
    ).astype(jnp.bfloat16)
    returned = lax.all_to_all(grad_piece, "tower", split_axis=0, concat_axis=0, tiled=True)
    returned_groups = returned.reshape(NGROUP, group_size, CAP, piece_rows)
    attn_grad = jnp.einsum(
        "gct,gpce->tpe", dispatch, returned_groups, preferred_element_type=jnp.float32
    )
    attn_grad = attn_grad.reshape(tok_count, model_width).astype(jnp.bfloat16)
    attn_rows = attn_got.reshape(tower_count * CAP, piece_rows)
    cot_rows = cot_got.reshape(tower_count * CAP, model_width)
    summed = lax.psum_scatter(
        lax.dot_general(
            cot_rows, attn_rows, (((0,), (0,)), ((), ())), preferred_element_type=jnp.float32
        ).astype(jnp.bfloat16),
        "dp",
        scatter_dimension=0,
        tiled=True,
    )
    weight_grad = summed.T
    return (attn_grad, weight_grad)


def solution(mesh):
    return jax.shard_map(
        per_device,
        mesh=mesh,
        in_specs=(
            P(("dp", "tower"), None),
            P(("dp", "tower"), None),
            P(("dp", "tower")),
            P(),
            P("tower", None),
        ),
        out_specs=(P(("dp", "tower"), None), P("tower", "dp")),
        check_vma=False,
    )
```

```python
import jax
import jax.numpy as jnp
from jax import lax
from jax.experimental import pallas as pl
from jax.experimental.pallas import tpu as pltpu
from jax.sharding import PartitionSpec as P

NGROUP = 8
CAP = 24
NX = 4
NZ = 8
HALVES = NGROUP // NX
PIECES = NZ // HALVES
NDP = 8
NC = 4
LAST = NZ // 2
TILE = 256
MESH = pl.DeviceIdType.MESH
F32 = jnp.float32
BF16 = jnp.bfloat16


def kernel(
    mod_ref, gm_ref, attn_ref, cot_ref, w_ref, grad_ref, wgrad_ref,
    ring, dests, staged, cot_got, w_chunk, partial, terms, acc,
    attn_own, attn_x, attn_got, attn_t, grads, ret_z, ret_x,
    dest_send, dest_recv, right_send, right_recv, left_send, left_recv,
    x_send, x_recv, x_own, ax_send, ax_recv, ax_own, az_send, az_recv, az_own,
    w_sem, rs_send, rs_recv, rs_own, rz_send, rz_recv, rz_own, rx_send, rx_recv, rx_own,
):
    tok = cot_ref.shape[0]
    width = cot_ref.shape[1] // NC
    cols = width // NDP
    own_cols = wgrad_ref.shape[1]
    feats = w_ref.shape[0]
    half = width // 2
    me, my_d = lax.axis_index("tower"), lax.axis_index("dp")
    my_x, my_z = me // NZ, me % NZ
    my_half, my_piece = my_z // PIECES, my_z % PIECES

    def at_z(k):
        return {"tower": my_x * NZ + (my_z + k + NZ) % NZ}

    def at_x(k):
        return {"tower": ((my_x + k) % NX) * NZ + my_z}

    def at_d(k):
        return {"dp": (my_d + k) % NDP}

    def remote(src, dst, send, recv, device):
        return pltpu.make_async_remote_copy(
            src_ref=src, dst_ref=dst, send_sem=send, recv_sem=recv,
            device_id=device, device_id_type=MESH,
        )

    def wait_bytes(ref, sem):
        pltpu.make_async_copy(ref, ref, sem).wait()

    def w_load(c, d):
        return pltpu.make_async_copy(
            w_ref.at[:, pl.ds(d * own_cols + c * cols, cols)],
            w_chunk.at[c % 2, :, pl.ds(d * cols, cols)],
            w_sem.at[c],
        )

    barrier = pltpu.get_barrier_semaphore()
    for k in range(1, NZ):
        pl.semaphore_signal(barrier, inc=1, device_id=at_z(k), device_id_type=MESH)
    for k in range(1, NX):
        pl.semaphore_signal(barrier, inc=1, device_id=at_x(k), device_id_type=MESH)
    for k in range(1, NDP):
        pl.semaphore_signal(barrier, inc=1, device_id=at_d(k), device_id_type=MESH)

    for c in range(NC):
        for d in range(NDP):
            ring[c, 0, :, d * cols:(d + 1) * cols] = cot_ref[
                :, d * own_cols + c * cols:d * own_cols + (c + 1) * cols
            ]
    for c in range(2):
        for d in range(NDP):
            w_load(c, d).start()
    pl.semaphore_wait(barrier, NZ - 1 + NX - 1 + NDP - 1)

    def ring_copy(c, s, right):
        off = -s if right else s
        src = ring.at[c, off % NZ]
        dst = ring.at[c, (off - 1 if right else off + 1) % NZ]
        if s == LAST - 1:
            part = pl.ds(0, half) if right else pl.ds(half, half)
            src, dst = src.at[:, part], dst.at[:, part]
        return remote(
            src, dst,
            (right_send if right else left_send).at[c, s],
            (right_recv if right else left_recv).at[c, s],
            at_z(1 if right else -1),
        )

    ring_copy(0, 0, True).start()
    ring_copy(0, 0, False).start()

    mod = jnp.broadcast_to(mod_ref[...], (8, tok))
    kinds = [(mod == m).astype(F32) for m in range(3)]
    t_from = lax.broadcasted_iota(jnp.int32, (tok, tok), 0)
    t_to = lax.broadcasted_iota(jnp.int32, (tok, tok), 1)
    earlier = (t_from < t_to).astype(F32).astype(BF16)
    before = jnp.dot(jnp.concatenate(kinds, 0).astype(BF16), earlier, preferred_element_type=F32)
    order = sum(before[8 * m:8 * m + 8] * kinds[m] for m in range(3))
    serves = [gm_ref[g] for g in range(NGROUP)]
    how_many = jnp.ones_like(mod)
    for m in range(3):
        count = sum((s == m).astype(jnp.int32) for s in serves)
        how_many = jnp.where(mod == m, count, how_many)
    per = how_many.astype(F32)
    turn = (order.astype(jnp.int32) + me).astype(F32)
    target = (turn - jnp.floor((turn + 0.5) / per) * per).astype(jnp.int32)
    routed = jnp.zeros_like(mod)
    for g in range(NGROUP):
        rank = sum(((s == serves[g]).astype(jnp.int32) for s in serves[:g]), jnp.int32(0))
        routed = jnp.where((mod == serves[g]) & (target == rank), g, routed)
    dest = routed * CAP + jnp.floor((order + 0.5) / per).astype(jnp.int32)
    dests[0] = dest

    def dest_copy(k):
        return remote(dests.at[0], dests.at[NZ - k], dest_send.at[k], dest_recv.at[NZ - k], at_z(k))

    for k in range(1, NZ):
        dest_copy(k).start()

    slots = lax.broadcasted_iota(jnp.int32, (NGROUP * CAP, tok), 0)
    pick_own = jnp.where(slots == dest[0:1], 1.0, 0.0).astype(BF16)
    for p in range(PIECES):
        got = jnp.dot(pick_own, attn_ref[:, p * feats:(p + 1) * feats], preferred_element_type=F32)
        attn_own[:, :, :, p * feats:(p + 1) * feats] = got.astype(BF16).reshape(NX, HALVES, CAP, feats)

    def attn_x_copy(k):
        return remote(
            attn_own.at[(my_x + k) % NX], attn_x.at[my_x], ax_send.at[k], ax_recv.at[NX - k], at_x(k)
        )

    own_ax = pltpu.make_async_copy(attn_own.at[my_x], attn_x.at[my_x], ax_own)
    own_ax.start()
    for k in range(1, NX):
        attn_x_copy(k).start()

    def attn_z_src(k):
        z = (my_z + k) % NZ
        start = pl.multiple_of((z % PIECES) * feats, feats)
        return attn_x.at[:, z // PIECES, :, pl.ds(start, feats)]

    def attn_z_copy(k):
        return remote(
            attn_z_src(k), attn_got.at[:, my_z], az_send.at[k], az_recv.at[NZ - k], at_z(k)
        )

    def attn_along_z():
        own_ax.wait()
        for k in range(1, NX):
            attn_x_copy(k).wait_recv()
        pltpu.make_async_copy(attn_z_src(0), attn_got.at[:, my_z], az_own).start()
        for k in range(1, NZ):
            attn_z_copy(k).start()

    def attn_arrived():
        pltpu.make_async_copy(attn_z_src(0), attn_got.at[:, my_z], az_own).wait()
        for k in range(1, NZ):
            attn_z_copy(k).wait_recv()

        @pl.loop(0, feats // TILE)
        def _(j):
            at = pl.ds(pl.multiple_of(j * TILE, TILE), TILE)
            attn_t[at, :] = jnp.transpose(attn_got[:, :, :, at].reshape(NX * NZ * CAP, TILE))

    rows = lax.broadcasted_iota(jnp.int32, (NX * CAP, tok), 0)
    x_of = sum((rows >= CAP * k).astype(jnp.int32) for k in range(1, NX))
    wanted = rows + CAP * (HALVES - 1) * x_of + CAP * my_half

    def deliver(c, off):
        slot = off % NZ
        pick = jnp.where(wanted == dests[slot, 0:1, :], 1.0, 0.0).astype(BF16)
        got = jnp.dot(pick, ring[c, slot], preferred_element_type=F32).astype(BF16)
        for x in range(NX):
            staged[c % 2, x, slot] = got[x * CAP:(x + 1) * CAP]
        lands = cot_got.at[c, my_x, (my_z + off + NZ) % NZ]
        for k in range(NX):
            src = staged.at[c % 2, (my_x + k) % NX, slot]
            if k == 0:
                pltpu.make_async_copy(src, lands, x_own.at[c]).start()
            else:
                remote(src, lands, x_send.at[c, k], x_recv.at[c, NX - k], at_x(k)).start()

    def chunk_arrived(c):
        wait_bytes(staged.at[c % 2, 0], x_own.at[c])
        for k in range(1, NX):
            wait_bytes(staged.at[c % 2, k], x_recv.at[c, k])

    def x_sends_done(c):
        for k in range(1, NX):
            wait_bytes(staged.at[c % 2, k], x_send.at[c, k])

    def input_grad(c):
        wait_bytes(w_chunk.at[c % 2], w_sem.at[c])

        @pl.loop(0, feats // TILE)
        def _(j):
            at = pl.ds(pl.multiple_of(j * TILE, TILE), TILE)
            term = lax.dot_general(
                cot_got[c].reshape(NX * NZ * CAP, width), w_chunk[c % 2, at, :],
                (((1,), (1,)), ((), ())), preferred_element_type=F32,
            )
            if c > 0:
                term += acc[:, at]
            if c < NC - 1:
                acc[:, at] = term
            else:
                grads[:, :, :, at] = term.astype(BF16).reshape(NX, NZ, CAP, TILE)

        if c + 2 < NC:
            for d in range(NDP):
                w_load(c + 2, d).start()

    def rs_copy(c, k):
        return remote(
            partial.at[c % 2, (my_d + k) % NDP], terms.at[c, my_d],
            rs_send.at[c, k], rs_recv.at[c, NDP - k], at_d(k),
        )

    def rs_own_copy(c):
        return pltpu.make_async_copy(partial.at[c % 2, my_d], terms.at[c, my_d], rs_own.at[c])

    def weight_grad(c):
        if c >= 2:
            for k in range(1, NDP):
                rs_copy(c - 2, k).wait_send()
            rs_own_copy(c - 2).wait()

        per_tile = TILE // cols

        @pl.loop(0, width // TILE)
        def _(j):
            at = pl.ds(pl.multiple_of(j * TILE, TILE), TILE)
            term = jnp.dot(
                attn_t[...], cot_got[c, :, :, :, at].reshape(NX * NZ * CAP, TILE),
                preferred_element_type=F32,
            ).astype(BF16)
            for i in range(per_tile):
                partial[c % 2, j * per_tile + i] = term[:, i * cols:(i + 1) * cols]

        rs_own_copy(c).start()
        for k in range(1, NDP):
            rs_copy(c, k).start()

    def weight_grad_sum(c):
        if c >= NC - 2:
            rs_own_copy(c).wait()
        for k in range(1, NDP):
            rs_copy(c, k).wait_recv()

        @pl.loop(0, feats // TILE)
        def _(j):
            at = pl.ds(pl.multiple_of(j * TILE, TILE), TILE)
            total = terms[c, 0, at, :].astype(F32)
            for d in range(1, NDP):
                total += terms[c, d, at, :].astype(F32)
            wgrad_ref[at, c * cols:(c + 1) * cols] = total.astype(BF16)

    def ret_z_copy(k):
        return remote(
            grads.at[:, (my_z + k) % NZ], ret_z.at[my_z], rz_send.at[k], rz_recv.at[NZ - k], at_z(k)
        )

    for tick in range(2 * NC + LAST):
        live = [(c, tick - 2 * c) for c in range(NC) if 0 <= tick - 2 * c < 8]
        for c, s in live:
            if s in range(1, LAST + 1):
                ring_copy(c, s - 1, True).wait_recv()
                ring_copy(c, s - 1, False).wait_recv()
            if s < LAST and (c, s) != (0, 0):
                ring_copy(c, s, True).start()
                ring_copy(c, s, False).start()
        if tick == 1:
            for k in range(1, NZ):
                dest_copy(k).wait_recv()
        if tick == 2:
            attn_along_z()
        for c, s in live:
            if s == 0:
                if c < 2:
                    deliver(c, 0)
            elif s < LAST:
                if s == 1 and c >= 2:
                    x_sends_done(c - 2)
                    deliver(c, 0)
                deliver(c, -s)
                deliver(c, s)
            elif s == LAST:
                deliver(c, LAST)
            elif s == LAST + 1:
                chunk_arrived(c)
                if c == 0:
                    attn_arrived()
                input_grad(c)
                if c == NC - 1:
                    pltpu.make_async_copy(grads.at[:, my_z], ret_z.at[my_z], rz_own).start()
                    for k in range(1, NZ):
                        ret_z_copy(k).start()
                weight_grad(c)
                if c == 2:
                    weight_grad_sum(0)

    for c in range(1, NC - 1):
        weight_grad_sum(c)

    def ret_x_start(z):
        for k in range(NX):
            src, dst = ret_z.at[z, (my_x + k) % NX], ret_x.at[my_x, z]
            if k == 0:
                pltpu.make_async_copy(src, dst, rx_own).start()
            else:
                remote(src, dst, rx_send.at[k], rx_recv.at[NX - k], at_x(k)).start()

    pltpu.make_async_copy(grads.at[:, my_z], ret_z.at[my_z], rz_own).wait()
    ret_x_start(my_z)
    for k in (1, 7, 2, 6, 3, 5, 4):
        ret_z_copy(k).wait_recv()
        ret_x_start((my_z - k + NZ) % NZ)
    weight_grad_sum(NC - 1)
    for k in range(NX):
        wait_bytes(ret_x.at[k], rx_own if k == 0 else rx_recv.at[k])

    back = jnp.where(slots == dests[0, 0:1, :], 1.0, 0.0).astype(BF16)
    for p in range(PIECES):
        pieces = jnp.concatenate(
            [ret_x[g // HALVES, (g % HALVES) * PIECES + p] for g in range(NGROUP)], 0
        )
        grad_ref[:, p * feats:(p + 1) * feats] = lax.dot_general(
            back, pieces, (((0,), (0,)), ((), ())), preferred_element_type=F32
        ).astype(BF16)

    for k in range(1, NZ):
        dest_copy(k).wait_send()
        attn_z_copy(k).wait_send()
        ret_z_copy(k).wait_send()
    for k in range(1, NX):
        attn_x_copy(k).wait_send()
        wait_bytes(ret_x.at[k], rx_send.at[k])
    for c in range(NC):
        for s in range(LAST):
            ring_copy(c, s, True).wait_send()
            ring_copy(c, s, False).wait_send()
    for c in range(NC - 2, NC):
        x_sends_done(c)
        for k in range(1, NDP):
            rs_copy(c, k).wait_send()


def backward(mod, gm, attn, cot, w):
    tok, model = cot.shape
    width = model // NC
    feats = w.shape[0]
    dma = pltpu.SemaphoreType.DMA
    vmem = pl.BlockSpec(memory_space=pltpu.VMEM)
    return pl.pallas_call(
        kernel,
        out_shape=(
            jax.ShapeDtypeStruct((tok, model), BF16),
            jax.ShapeDtypeStruct((feats, model // NDP), BF16),
        ),
        in_specs=[
            vmem, pl.BlockSpec(memory_space=pltpu.SMEM), vmem, vmem,
            pl.BlockSpec(memory_space=pl.ANY),
        ],
        out_specs=(vmem, vmem),
        scratch_shapes=[
            pltpu.VMEM((NC, NZ, tok, width), BF16),
            pltpu.VMEM((NZ, 8, tok), jnp.int32),
            pltpu.VMEM((2, NX, NZ, CAP, width), BF16),
            pltpu.VMEM((NC, NX, NZ, CAP, width), BF16),
            pltpu.VMEM((2, feats, width), BF16),
            pltpu.VMEM((2, NDP, feats, width // NDP), BF16),
            pltpu.VMEM((NC, NDP, feats, width // NDP), BF16),
            pltpu.VMEM((NX * NZ * CAP, feats), F32),
            pltpu.VMEM((NX, HALVES, CAP, model), BF16),
            pltpu.VMEM((NX, HALVES, CAP, model), BF16),
            pltpu.VMEM((NX, NZ, CAP, feats), BF16),
            pltpu.VMEM((feats, NX * NZ * CAP), BF16),
            pltpu.VMEM((NX, NZ, CAP, feats), BF16),
            pltpu.VMEM((NZ, NX, CAP, feats), BF16),
            pltpu.VMEM((NX, NZ, CAP, feats), BF16),
            dma((NZ,)), dma((NZ,)),
            dma((NC, LAST)), dma((NC, LAST)), dma((NC, LAST)), dma((NC, LAST)),
            dma((NC, NX)), dma((NC, NX)), dma((NC,)),
            dma((NX,)), dma((NX,)), dma,
            dma((NZ,)), dma((NZ,)), dma,
            dma((NC,)),
            dma((NC, NDP)), dma((NC, NDP)), dma((NC,)),
            dma((NZ,)), dma((NZ,)), dma,
            dma((NX,)), dma((NX,)), dma,
        ],
        compiler_params=pltpu.CompilerParams(
            collective_id=0, has_side_effects=True, vmem_limit_bytes=63 * 1024 * 1024
        ),
        name="moe_proj_backward",
    )(mod, gm, attn, cot, w)


def per_device(attn_out, out_cot, modality, group_modality, o_weight):
    return backward(modality.reshape(1, -1), group_modality, attn_out, out_cot, o_weight)


def solution(mesh):
    return jax.shard_map(
        per_device,
        mesh=mesh,
        in_specs=(
            P(("dp", "tower"), None),
            P(("dp", "tower"), None),
            P(("dp", "tower")),
            P(),
            P("tower", None),
        ),
        out_specs=(P(("dp", "tower"), None), P("tower", "dp")),
        check_vma=False,
    )
```

```python
import jax
import jax.numpy as jnp
from jax import lax
from jax.experimental import pallas as pl
from jax.experimental.pallas import tpu as pltpu
from jax.sharding import PartitionSpec as P

NGROUP = 8
CAP = 24
NX = 4
NZ = 8
HALVES = NGROUP // NX
PIECES = NZ // HALVES
NDP = 8
CORES = 2
NY = NDP // CORES
NC = 4
LAST = NZ // 2
TILE = 256
MESH = pl.DeviceIdType.MESH
F32 = jnp.float32
BF16 = jnp.bfloat16


def kernel(
    mod_ref, gm_ref, attn_ref, cot_ref, w_ref, grad_ref, wgrad_ref,
    ring, dests, staged, cot_got, w_chunk, partial, other, terms, acc,
    attn_own, attn_x, attn_got, attn_t, grads, ret_z, ret_x,
    dest_send, dest_recv, right_send, right_recv, left_send, left_recv,
    x_send, x_recv, x_own, ax_send, ax_recv, ax_own, az_send, az_recv, az_own,
    w_sem, pair_send, pair_recv, rs_send, rs_recv, rs_own, rz_send, rz_recv, rz_own, rx_send, rx_recv, rx_own,
):
    tok = cot_ref.shape[0]
    width = cot_ref.shape[1] // NC
    cols = width // NDP
    own_cols = wgrad_ref.shape[1]
    feats = w_ref.shape[0]
    half = width // 2
    me, my_d = lax.axis_index("tower"), lax.axis_index("dp")
    my_x, my_z = me // NZ, me % NZ
    my_half = my_z // PIECES
    my_y, my_core = my_d // CORES, my_d % CORES

    def at_z(k):
        return {"tower": my_x * NZ + (my_z + k + NZ) % NZ}

    def at_x(k):
        return {"tower": ((my_x + k) % NX) * NZ + my_z}

    def at_y(k):
        return {"dp": ((my_y + k) % NY) * CORES + my_core}

    other_core = {"dp": my_y * CORES + 1 - my_core}

    def remote(src, dst, send, recv, device):
        return pltpu.make_async_remote_copy(
            src_ref=src, dst_ref=dst, send_sem=send, recv_sem=recv,
            device_id=device, device_id_type=MESH,
        )

    def wait_bytes(ref, sem):
        pltpu.make_async_copy(ref, ref, sem).wait()

    def w_load(c, d):
        return pltpu.make_async_copy(
            w_ref.at[:, pl.ds(d * own_cols + c * cols, cols)],
            w_chunk.at[c % 2, :, pl.ds(d * cols, cols)],
            w_sem.at[c],
        )

    barrier = pltpu.get_barrier_semaphore()
    for k in range(1, NZ):
        pl.semaphore_signal(barrier, inc=1, device_id=at_z(k), device_id_type=MESH)
    for k in range(1, NX):
        pl.semaphore_signal(barrier, inc=1, device_id=at_x(k), device_id_type=MESH)
    for k in range(1, NY):
        pl.semaphore_signal(barrier, inc=1, device_id=at_y(k), device_id_type=MESH)
    pl.semaphore_signal(barrier, inc=1, device_id=other_core, device_id_type=MESH)

    def own_block(c):
        for d in range(NDP):
            ring[c, 0, :, d * cols:(d + 1) * cols] = cot_ref[
                :, d * own_cols + c * cols:d * own_cols + (c + 1) * cols
            ]

    own_block(0)
    own_block(1)
    pl.semaphore_wait(barrier, NZ - 1 + NX - 1 + NY)

    def ring_copy(c, s, right):
        off = -s if right else s
        src = ring.at[c, off % NZ]
        dst = ring.at[c, (off - 1 if right else off + 1) % NZ]
        if s == LAST - 1:
            part = pl.ds(0, half) if right else pl.ds(half, half)
            src, dst = src.at[:, part], dst.at[:, part]
        return remote(
            src, dst,
            (right_send if right else left_send).at[c, s],
            (right_recv if right else left_recv).at[c, s],
            at_z(1 if right else -1),
        )

    for c in range(2):
        ring_copy(c, 0, True).start()
        ring_copy(c, 0, False).start()
    for c in range(2):
        for d in range(NDP):
            w_load(c, d).start()
    for c in range(2, NC):
        own_block(c)

    mod = jnp.broadcast_to(mod_ref[...], (8, tok))
    kinds = [(mod == m).astype(F32) for m in range(3)]
    t_from = lax.broadcasted_iota(jnp.int32, (tok, tok), 0)
    t_to = lax.broadcasted_iota(jnp.int32, (tok, tok), 1)
    earlier = (t_from < t_to).astype(F32).astype(BF16)
    before = jnp.dot(jnp.concatenate(kinds, 0).astype(BF16), earlier, preferred_element_type=F32)
    order = sum(before[8 * m:8 * m + 8] * kinds[m] for m in range(3))
    serves = [gm_ref[g] for g in range(NGROUP)]
    how_many = jnp.ones_like(mod)
    for m in range(3):
        count = sum((s == m).astype(jnp.int32) for s in serves)
        how_many = jnp.where(mod == m, count, how_many)
    per = how_many.astype(F32)
    turn = (order.astype(jnp.int32) + me).astype(F32)
    target = (turn - jnp.floor((turn + 0.5) / per) * per).astype(jnp.int32)
    routed = jnp.zeros_like(mod)
    for g in range(NGROUP):
        rank = sum(((s == serves[g]).astype(jnp.int32) for s in serves[:g]), jnp.int32(0))
        routed = jnp.where((mod == serves[g]) & (target == rank), g, routed)
    dest = routed * CAP + jnp.floor((order + 0.5) / per).astype(jnp.int32)
    dests[0] = dest

    def dest_copy(k):
        return remote(dests.at[0], dests.at[NZ - k], dest_send.at[k], dest_recv.at[NZ - k], at_z(k))

    for k in range(1, NZ):
        dest_copy(k).start()

    slots = lax.broadcasted_iota(jnp.int32, (NGROUP * CAP, tok), 0)
    pick_own = jnp.where(slots == dest[0:1], 1.0, 0.0).astype(BF16)
    for p in range(PIECES):
        got = jnp.dot(pick_own, attn_ref[:, p * feats:(p + 1) * feats], preferred_element_type=F32)
        attn_own[:, :, :, p * feats:(p + 1) * feats] = got.astype(BF16).reshape(NX, HALVES, CAP, feats)

    def attn_x_copy(k):
        return remote(
            attn_own.at[(my_x + k) % NX], attn_x.at[my_x], ax_send.at[k], ax_recv.at[NX - k], at_x(k)
        )

    own_ax = pltpu.make_async_copy(attn_own.at[my_x], attn_x.at[my_x], ax_own)
    own_ax.start()
    for k in range(1, NX):
        attn_x_copy(k).start()

    def attn_z_src(k):
        z = (my_z + k) % NZ
        start = pl.multiple_of((z % PIECES) * feats, feats)
        return attn_x.at[:, z // PIECES, :, pl.ds(start, feats)]

    def attn_z_copy(k):
        return remote(
            attn_z_src(k), attn_got.at[:, my_z], az_send.at[k], az_recv.at[NZ - k], at_z(k)
        )

    def attn_along_z():
        own_ax.wait()
        for k in range(1, NX):
            attn_x_copy(k).wait_recv()
        pltpu.make_async_copy(attn_z_src(0), attn_got.at[:, my_z], az_own).start()
        for k in range(1, NZ):
            attn_z_copy(k).start()

    def attn_arrived():
        pltpu.make_async_copy(attn_z_src(0), attn_got.at[:, my_z], az_own).wait()
        for k in range(1, NZ):
            attn_z_copy(k).wait_recv()

        @pl.loop(0, feats // TILE)
        def _(j):
            at = pl.ds(pl.multiple_of(j * TILE, TILE), TILE)
            attn_t[at, :] = jnp.transpose(attn_got[:, :, :, at].reshape(NX * NZ * CAP, TILE))

    rows = lax.broadcasted_iota(jnp.int32, (NX * CAP, tok), 0)
    x_of = sum((rows >= CAP * k).astype(jnp.int32) for k in range(1, NX))
    wanted = rows + CAP * (HALVES - 1) * x_of + CAP * my_half

    def deliver(c, off):
        slot = off % NZ
        pick = jnp.where(wanted == dests[slot, 0:1, :], 1.0, 0.0).astype(BF16)
        got = jnp.dot(pick, ring[c, slot], preferred_element_type=F32).astype(BF16)
        for x in range(NX):
            staged[c, x, slot] = got[x * CAP:(x + 1) * CAP]
        lands = cot_got.at[c, my_x, (my_z + off + NZ) % NZ]
        for k in range(NX):
            src = staged.at[c, (my_x + k) % NX, slot]
            if k == 0:
                pltpu.make_async_copy(src, lands, x_own.at[c]).start()
            else:
                remote(src, lands, x_send.at[c, k], x_recv.at[c, NX - k], at_x(k)).start()

    def chunk_arrived(c):
        wait_bytes(staged.at[c, 0], x_own.at[c])
        for k in range(1, NX):
            wait_bytes(staged.at[c, k], x_recv.at[c, k])

    def x_sends_done(c):
        for k in range(1, NX):
            wait_bytes(staged.at[c, k], x_send.at[c, k])

    def input_grad(c):
        wait_bytes(w_chunk.at[c % 2], w_sem.at[c])

        @pl.loop(0, feats // TILE)
        def _(j):
            at = pl.ds(pl.multiple_of(j * TILE, TILE), TILE)
            term = lax.dot_general(
                cot_got[c].reshape(NX * NZ * CAP, width), w_chunk[c % 2, at, :],
                (((1,), (1,)), ((), ())), preferred_element_type=F32,
            )
            if c > 0:
                term += acc[:, at]
            if c < NC - 1:
                acc[:, at] = term
            else:
                grads[:, :, :, at] = term.astype(BF16).reshape(NX, NZ, CAP, TILE)

        if c + 2 < NC:
            for d in range(NDP):
                w_load(c + 2, d).start()

    def pair_copy(c):
        return remote(
            partial.at[c % 2, 1 - my_core], other.at[c], pair_send.at[c], pair_recv.at[c], other_core
        )

    def rs_copy(c, k):
        return remote(
            partial.at[c % 2, my_core, (my_y + k) % NY], terms.at[c, my_y],
            rs_send.at[c, k], rs_recv.at[c, NY - k], at_y(k),
        )

    def rs_own_copy(c):
        return pltpu.make_async_copy(
            partial.at[c % 2, my_core, my_y], terms.at[c, my_y], rs_own.at[c]
        )

    def weight_sends_done(c):
        pair_copy(c).wait_send()
        for k in range(1, NY):
            rs_copy(c, k).wait_send()
        rs_own_copy(c).wait()

    def weight_grad(c):
        if c >= 2:
            weight_sends_done(c - 2)

        @pl.loop(0, width // TILE)
        def _(j):
            at = pl.ds(pl.multiple_of(j * TILE, TILE), TILE)
            term = jnp.dot(
                attn_t[...], cot_got[c, :, :, :, at].reshape(NX * NZ * CAP, TILE),
                preferred_element_type=F32,
            ).astype(BF16)
            for i in range(CORES):
                partial[c % 2, i, j] = term[:, i * cols:(i + 1) * cols]

        pair_copy(c).start()

    def weight_pair(c):
        pair_copy(c).wait_recv()

        @pl.loop(0, feats // TILE)
        def _(j):
            at = pl.ds(pl.multiple_of(j * TILE, TILE), TILE)
            for y in range(NY):
                both = partial[c % 2, my_core, y, at, :].astype(F32) + other[c, y, at, :].astype(F32)
                partial[c % 2, my_core, y, at, :] = both.astype(BF16)

        rs_own_copy(c).start()
        for k in range(1, NY):
            rs_copy(c, k).start()

    def weight_grad_sum(c):
        if c >= NC - 2:
            rs_own_copy(c).wait()
        for k in range(1, NY):
            rs_copy(c, k).wait_recv()

        @pl.loop(0, feats // TILE)
        def _(j):
            at = pl.ds(pl.multiple_of(j * TILE, TILE), TILE)
            total = terms[c, 0, at, :].astype(F32)
            for y in range(1, NY):
                total += terms[c, y, at, :].astype(F32)
            wgrad_ref[at, c * cols:(c + 1) * cols] = total.astype(BF16)

    def ret_z_copy(k):
        return remote(
            grads.at[:, (my_z + k) % NZ], ret_z.at[my_z], rz_send.at[k], rz_recv.at[NZ - k], at_z(k)
        )

    def ring_step(c, s):
        if s > 0:
            ring_copy(c, s - 1, True).wait_recv()
            ring_copy(c, s - 1, False).wait_recv()
        if s < LAST and (c >= 2 or s > 0):
            ring_copy(c, s, True).start()
            ring_copy(c, s, False).start()
        if (c, s) == (0, 1):
            for k in range(1, NZ):
                dest_copy(k).wait_recv()
        if s in (0, LAST):
            deliver(c, s)
        else:
            deliver(c, -s)
            deliver(c, s)

    for c, s in ((0, 0), (1, 0), (0, 1), (1, 1), (0, 2)):
        ring_step(c, s)
    attn_along_z()
    for c, s in ((1, 2), (0, 3), (2, 0), (1, 3), (3, 0), (0, 4), (2, 1), (1, 4), (3, 1)):
        ring_step(c, s)
    chunk_arrived(0)
    input_grad(0)
    ring_step(2, 2)
    attn_arrived()
    weight_grad(0)
    ring_step(3, 2)
    chunk_arrived(1)
    input_grad(1)
    ring_step(2, 3)
    weight_grad(1)
    weight_pair(0)
    ring_step(3, 3)
    weight_pair(1)
    ring_step(2, 4)
    ring_step(3, 4)
    chunk_arrived(2)
    input_grad(2)
    chunk_arrived(3)
    input_grad(3)
    pltpu.make_async_copy(grads.at[:, my_z], ret_z.at[my_z], rz_own).start()
    for k in range(1, NZ):
        ret_z_copy(k).start()
    weight_grad(2)
    weight_grad(3)
    weight_pair(2)
    weight_pair(3)
    weight_grad_sum(0)
    weight_grad_sum(1)

    def ret_x_start(z):
        for k in range(NX):
            src, dst = ret_z.at[z, (my_x + k) % NX], ret_x.at[my_x, z]
            if k == 0:
                pltpu.make_async_copy(src, dst, rx_own).start()
            else:
                remote(src, dst, rx_send.at[k], rx_recv.at[NX - k], at_x(k)).start()

    pltpu.make_async_copy(grads.at[:, my_z], ret_z.at[my_z], rz_own).wait()
    ret_x_start(my_z)
    for k in (1, 7, 2, 6, 3, 5, 4):
        ret_z_copy(k).wait_recv()
        ret_x_start((my_z - k + NZ) % NZ)
    weight_grad_sum(2)
    weight_grad_sum(3)
    for k in range(NX):
        wait_bytes(ret_x.at[k], rx_own if k == 0 else rx_recv.at[k])

    back = jnp.where(slots == dests[0, 0:1, :], 1.0, 0.0).astype(BF16)
    for p in range(PIECES):
        pieces = jnp.concatenate(
            [ret_x[g // HALVES, (g % HALVES) * PIECES + p] for g in range(NGROUP)], 0
        )
        grad_ref[:, p * feats:(p + 1) * feats] = lax.dot_general(
            back, pieces, (((0,), (0,)), ((), ())), preferred_element_type=F32
        ).astype(BF16)

    for k in range(1, NZ):
        dest_copy(k).wait_send()
        attn_z_copy(k).wait_send()
        ret_z_copy(k).wait_send()
    for k in range(1, NX):
        attn_x_copy(k).wait_send()
        wait_bytes(ret_x.at[k], rx_send.at[k])
    for c in range(NC):
        for s in range(LAST):
            ring_copy(c, s, True).wait_send()
            ring_copy(c, s, False).wait_send()
        x_sends_done(c)
    for c in range(NC - 2, NC):
        pair_copy(c).wait_send()
        for k in range(1, NY):
            rs_copy(c, k).wait_send()


def backward(mod, gm, attn, cot, w):
    tok, model = cot.shape
    width = model // NC
    feats = w.shape[0]
    dma = pltpu.SemaphoreType.DMA
    vmem = pl.BlockSpec(memory_space=pltpu.VMEM)
    return pl.pallas_call(
        kernel,
        out_shape=(
            jax.ShapeDtypeStruct((tok, model), BF16),
            jax.ShapeDtypeStruct((feats, model // NDP), BF16),
        ),
        in_specs=[
            vmem, pl.BlockSpec(memory_space=pltpu.SMEM), vmem, vmem,
            pl.BlockSpec(memory_space=pl.ANY),
        ],
        out_specs=(vmem, vmem),
        scratch_shapes=[
            pltpu.VMEM((NC, NZ, tok, width), BF16),
            pltpu.VMEM((NZ, 8, tok), jnp.int32),
            pltpu.VMEM((NC, NX, NZ, CAP, width), BF16),
            pltpu.VMEM((NC, NX, NZ, CAP, width), BF16),
            pltpu.VMEM((2, feats, width), BF16),
            pltpu.VMEM((2, CORES, NY, feats, width // NDP), BF16),
            pltpu.VMEM((NC, NY, feats, width // NDP), BF16),
            pltpu.VMEM((NC, NY, feats, width // NDP), BF16),
            pltpu.VMEM((NX * NZ * CAP, feats), F32),
            pltpu.VMEM((NX, HALVES, CAP, model), BF16),
            pltpu.VMEM((NX, HALVES, CAP, model), BF16),
            pltpu.VMEM((NX, NZ, CAP, feats), BF16),
            pltpu.VMEM((feats, NX * NZ * CAP), BF16),
            pltpu.VMEM((NX, NZ, CAP, feats), BF16),
            pltpu.VMEM((NZ, NX, CAP, feats), BF16),
            pltpu.VMEM((NX, NZ, CAP, feats), BF16),
            dma((NZ,)), dma((NZ,)),
            dma((NC, LAST)), dma((NC, LAST)), dma((NC, LAST)), dma((NC, LAST)),
            dma((NC, NX)), dma((NC, NX)), dma((NC,)),
            dma((NX,)), dma((NX,)), dma,
            dma((NZ,)), dma((NZ,)), dma,
            dma((NC,)),
            dma((NC,)), dma((NC,)), dma((NC, NY)), dma((NC, NY)), dma((NC,)),
            dma((NZ,)), dma((NZ,)), dma,
            dma((NX,)), dma((NX,)), dma,
        ],
        compiler_params=pltpu.CompilerParams(
            collective_id=0, has_side_effects=True, vmem_limit_bytes=63 * 1024 * 1024
        ),
        name="moe_proj_backward",
    )(mod, gm, attn, cot, w)


def per_device(attn_out, out_cot, modality, group_modality, o_weight):
    return backward(modality.reshape(1, -1), group_modality, attn_out, out_cot, o_weight)


def solution(mesh):
    return jax.shard_map(
        per_device,
        mesh=mesh,
        in_specs=(
            P(("dp", "tower"), None),
            P(("dp", "tower"), None),
            P(("dp", "tower")),
            P(),
            P("tower", None),
        ),
        out_specs=(P(("dp", "tower"), None), P("tower", "dp")),
        check_vma=False,
    )
```

```python
import jax
import jax.numpy as jnp
from jax import lax
from jax.experimental import pallas as pl
from jax.experimental.pallas import tpu as pltpu
from jax.sharding import PartitionSpec as P

NGROUP = 8
CAP = 24
NX = 4
NZ = 8
HALVES = NGROUP // NX
PIECES = NZ // HALVES
NDP = 8
CORES = 2
NY = NDP // CORES
SOURCES = ((0, -1, 1), (-2, 2), (-3, 3), (4,))
NC = 4
LAST = NZ // 2
TILE = 256
MESH = pl.DeviceIdType.MESH
F32 = jnp.float32
BF16 = jnp.bfloat16


def kernel(
    mod_ref, gm_ref, attn_hbm, cot_hbm, w_ref, grad_ref, wgrad_ref,
    attn_ref, ring, dests, staged, cot_got, w_chunk, partial, other, terms, acc,
    attn_own, attn_x, attn_got, attn_t, grads, ret_z, ret_x,
    attn_in, cot_in, dest_send, dest_recv, right_send, right_recv, left_send, left_recv,
    x_send, x_recv, x_own, ax_send, ax_recv, ax_own, az_send, az_recv, az_own,
    w_sem, pair_send, pair_recv, rs_send, rs_recv, rs_own, rz_send, rz_recv, rz_own, rx_send, rx_recv, rx_own,
):
    tok = cot_hbm.shape[0]
    width = cot_hbm.shape[1] // NC
    cols = width // NDP
    own_cols = wgrad_ref.shape[1]
    feats = w_ref.shape[0]
    half = width // 2
    me, my_d = lax.axis_index("tower"), lax.axis_index("dp")
    my_x, my_z = me // NZ, me % NZ
    my_half = my_z // PIECES
    my_y, my_core = my_d // CORES, my_d % CORES

    def at_z(k):
        return {"tower": my_x * NZ + (my_z + k + NZ) % NZ}

    def at_x(k):
        return {"tower": ((my_x + k) % NX) * NZ + my_z}

    def at_y(k):
        return {"dp": ((my_y + k) % NY) * CORES + my_core}

    other_core = {"dp": my_y * CORES + 1 - my_core}

    def remote(src, dst, send, recv, device):
        return pltpu.make_async_remote_copy(
            src_ref=src, dst_ref=dst, send_sem=send, recv_sem=recv,
            device_id=device, device_id_type=MESH,
        )

    def wait_bytes(ref, sem):
        pltpu.make_async_copy(ref, ref, sem).wait()

    def w_load(c, d):
        return pltpu.make_async_copy(
            w_ref.at[:, pl.ds(d * own_cols + c * cols, cols)],
            w_chunk.at[c % 2, :, pl.ds(d * cols, cols)],
            w_sem.at[c],
        )

    def own_block(c):
        for d in range(NDP):
            pltpu.make_async_copy(
                cot_hbm.at[:, pl.ds(d * own_cols + c * cols, cols)],
                ring.at[c, 0, :, pl.ds(d * cols, cols)],
                cot_in.at[c],
            ).start()

    attn_load = pltpu.make_async_copy(attn_hbm, attn_ref, attn_in)
    barrier = pltpu.get_barrier_semaphore()
    for k in range(1, NZ):
        pl.semaphore_signal(barrier, inc=1, device_id=at_z(k), device_id_type=MESH)
    for k in range(1, NX):
        pl.semaphore_signal(barrier, inc=1, device_id=at_x(k), device_id_type=MESH)
    for k in range(1, NY):
        pl.semaphore_signal(barrier, inc=1, device_id=at_y(k), device_id_type=MESH)
    pl.semaphore_signal(barrier, inc=1, device_id=other_core, device_id_type=MESH)

    own_block(0)
    own_block(1)
    attn_load.start()
    pl.semaphore_wait(barrier, NZ - 1 + NX - 1 + NY)

    def ring_copy(c, s, right):
        off = -s if right else s
        src = ring.at[c, off % NZ]
        dst = ring.at[c, (off - 1 if right else off + 1) % NZ]
        if s == LAST - 1:
            part = pl.ds(0, half) if right else pl.ds(half, half)
            src, dst = src.at[:, part], dst.at[:, part]
        return remote(
            src, dst,
            (right_send if right else left_send).at[c, s],
            (right_recv if right else left_recv).at[c, s],
            at_z(1 if right else -1),
        )

    for c in range(2):
        wait_bytes(ring.at[c, 0], cot_in.at[c])
        ring_copy(c, 0, True).start()
        ring_copy(c, 0, False).start()
    for c in range(2, NC):
        own_block(c)
    for c in range(2):
        for d in range(NDP):
            w_load(c, d).start()

    mod = jnp.broadcast_to(mod_ref[...], (8, tok))
    kinds = [(mod == m).astype(F32) for m in range(3)]
    t_from = lax.broadcasted_iota(jnp.int32, (tok, tok), 0)
    t_to = lax.broadcasted_iota(jnp.int32, (tok, tok), 1)
    earlier = (t_from < t_to).astype(F32).astype(BF16)
    before = jnp.dot(jnp.concatenate(kinds, 0).astype(BF16), earlier, preferred_element_type=F32)
    order = sum(before[8 * m:8 * m + 8] * kinds[m] for m in range(3))
    serves = [gm_ref[g] for g in range(NGROUP)]
    how_many = jnp.ones_like(mod)
    for m in range(3):
        count = sum((s == m).astype(jnp.int32) for s in serves)
        how_many = jnp.where(mod == m, count, how_many)
    per = how_many.astype(F32)
    turn = (order.astype(jnp.int32) + me).astype(F32)
    target = (turn - jnp.floor((turn + 0.5) / per) * per).astype(jnp.int32)
    routed = jnp.zeros_like(mod)
    for g in range(NGROUP):
        rank = sum(((s == serves[g]).astype(jnp.int32) for s in serves[:g]), jnp.int32(0))
        routed = jnp.where((mod == serves[g]) & (target == rank), g, routed)
    dest = routed * CAP + jnp.floor((order + 0.5) / per).astype(jnp.int32)
    dests[0] = dest

    def dest_copy(k):
        return remote(dests.at[0], dests.at[NZ - k], dest_send.at[k], dest_recv.at[NZ - k], at_z(k))

    for k in range(1, NZ):
        dest_copy(k).start()

    slots = lax.broadcasted_iota(jnp.int32, (NGROUP * CAP, tok), 0)
    attn_load.wait()
    pick_own = jnp.where(slots == dest[0:1], 1.0, 0.0).astype(BF16)
    for p in range(PIECES):
        got = jnp.dot(pick_own, attn_ref[:, p * feats:(p + 1) * feats], preferred_element_type=F32)
        attn_own[:, :, :, p * feats:(p + 1) * feats] = got.astype(BF16).reshape(NX, HALVES, CAP, feats)

    def attn_x_copy(k):
        return remote(
            attn_own.at[(my_x + k) % NX], attn_x.at[my_x], ax_send.at[k], ax_recv.at[NX - k], at_x(k)
        )

    own_ax = pltpu.make_async_copy(attn_own.at[my_x], attn_x.at[my_x], ax_own)
    own_ax.start()
    for k in range(1, NX):
        attn_x_copy(k).start()

    def attn_z_src(k):
        z = (my_z + k) % NZ
        start = pl.multiple_of((z % PIECES) * feats, feats)
        return attn_x.at[:, z // PIECES, :, pl.ds(start, feats)]

    def attn_z_copy(k):
        return remote(
            attn_z_src(k), attn_got.at[:, my_z], az_send.at[k], az_recv.at[NZ - k], at_z(k)
        )

    def attn_along_z():
        own_ax.wait()
        for k in range(1, NX):
            attn_x_copy(k).wait_recv()
        pltpu.make_async_copy(attn_z_src(0), attn_got.at[:, my_z], az_own).start()
        for k in range(1, NZ):
            attn_z_copy(k).start()

    def attn_arrived():
        pltpu.make_async_copy(attn_z_src(0), attn_got.at[:, my_z], az_own).wait()
        for k in range(1, NZ):
            attn_z_copy(k).wait_recv()

        @pl.loop(0, feats // TILE)
        def _(j):
            at = pl.ds(pl.multiple_of(j * TILE, TILE), TILE)
            attn_t[at, :] = jnp.transpose(attn_got[:, :, :, at].reshape(NX * NZ * CAP, TILE))

    rows = lax.broadcasted_iota(jnp.int32, (NX * CAP, tok), 0)
    x_of = sum((rows >= CAP * k).astype(jnp.int32) for k in range(1, NX))
    wanted = rows + CAP * (HALVES - 1) * x_of + CAP * my_half

    def deliver(c, off):
        slot = off % NZ
        pick = jnp.where(wanted == dests[slot, 0:1, :], 1.0, 0.0).astype(BF16)
        got = jnp.dot(pick, ring[c, slot], preferred_element_type=F32).astype(BF16)
        for x in range(NX):
            staged[c, x, slot] = got[x * CAP:(x + 1) * CAP]
        part = abs(off) - 1 if off else 0
        lands = cot_got.at[c, my_x, (my_z + off + NZ) % NZ]
        for k in range(NX):
            src = staged.at[c, (my_x + k) % NX, slot]
            if k == 0:
                pltpu.make_async_copy(src, lands, x_own.at[c, part]).start()
            else:
                remote(
                    src, lands, x_send.at[c, k], x_recv.at[c, part, NX - k], at_x(k)
                ).start()

    def arrived(c, parts):
        for part in parts:
            count = len(SOURCES[part])
            wait_bytes(staged.at[c, 0, pl.ds(0, count)], x_own.at[c, part])
            for k in range(1, NX):
                wait_bytes(staged.at[c, k, pl.ds(0, count)], x_recv.at[c, part, k])

    def x_sends_done(c):
        for k in range(1, NX):
            wait_bytes(staged.at[c, k], x_send.at[c, k])

    def input_grad(c):
        wait_bytes(w_chunk.at[c % 2], w_sem.at[c])

        @pl.loop(0, feats // TILE)
        def _(j):
            at = pl.ds(pl.multiple_of(j * TILE, TILE), TILE)
            term = lax.dot_general(
                cot_got[c].reshape(NX * NZ * CAP, width), w_chunk[c % 2, at, :],
                (((1,), (1,)), ((), ())), preferred_element_type=F32,
            )
            term = term.reshape(NX, NZ, CAP, TILE)
            acc[:, :, :, at] = term if c == 0 else acc[:, :, :, at] + term

        for d in range(NDP):
            w_load(c + 2, d).start()

    def rows_grad(offsets):
        zs = [(my_z + off + NZ) % NZ for off in offsets]
        count = NX * CAP

        @pl.loop(0, feats // TILE)
        def _(j):
            at = pl.ds(pl.multiple_of(j * TILE, TILE), TILE)
            term = sum(
                lax.dot_general(
                    jnp.concatenate([cot_got[c, :, z].reshape(count, width) for z in zs], 0),
                    w_chunk[c % 2, at, :], (((1,), (1,)), ((), ())), preferred_element_type=F32,
                )
                for c in range(NC - 2, NC)
            )
            for i, z in enumerate(zs):
                total = term[i * count:(i + 1) * count].reshape(NX, CAP, TILE) + acc[:, z, :, at]
                grads[:, z, :, at] = total.astype(BF16)

        for off in offsets:
            if off == 0:
                pltpu.make_async_copy(grads.at[:, my_z], ret_z.at[my_z], rz_own).start()
            else:
                ret_z_copy(off % NZ).start()

    def pair_copy(c):
        return remote(
            partial.at[c % 2, 1 - my_core], other.at[c], pair_send.at[c], pair_recv.at[c], other_core
        )

    def rs_copy(c, k):
        return remote(
            partial.at[c % 2, my_core, (my_y + k) % NY], terms.at[c, my_y],
            rs_send.at[c, k], rs_recv.at[c, NY - k], at_y(k),
        )

    def rs_own_copy(c):
        return pltpu.make_async_copy(
            partial.at[c % 2, my_core, my_y], terms.at[c, my_y], rs_own.at[c]
        )

    def weight_sends_done(c):
        pair_copy(c).wait_send()
        for k in range(1, NY):
            rs_copy(c, k).wait_send()
        rs_own_copy(c).wait()

    def weight_grad(c):
        if c >= 2:
            weight_sends_done(c - 2)

        @pl.loop(0, width // TILE)
        def _(j):
            at = pl.ds(pl.multiple_of(j * TILE, TILE), TILE)
            term = jnp.dot(
                attn_t[...], cot_got[c, :, :, :, at].reshape(NX * NZ * CAP, TILE),
                preferred_element_type=F32,
            ).astype(BF16)
            for i in range(CORES):
                partial[c % 2, i, j] = term[:, i * cols:(i + 1) * cols]

        pair_copy(c).start()

    def weight_pair(c):
        pair_copy(c).wait_recv()

        @pl.loop(0, feats // TILE)
        def _(j):
            at = pl.ds(pl.multiple_of(j * TILE, TILE), TILE)
            for y in range(NY):
                both = partial[c % 2, my_core, y, at, :].astype(F32) + other[c, y, at, :].astype(F32)
                partial[c % 2, my_core, y, at, :] = both.astype(BF16)

        rs_own_copy(c).start()
        for k in range(1, NY):
            rs_copy(c, k).start()

    def weight_grad_sum(c):
        if c >= NC - 2:
            rs_own_copy(c).wait()
        for k in range(1, NY):
            rs_copy(c, k).wait_recv()

        @pl.loop(0, feats // TILE)
        def _(j):
            at = pl.ds(pl.multiple_of(j * TILE, TILE), TILE)
            total = terms[c, 0, at, :].astype(F32)
            for y in range(1, NY):
                total += terms[c, y, at, :].astype(F32)
            wgrad_ref[at, c * cols:(c + 1) * cols] = total.astype(BF16)

    def ret_z_copy(k):
        return remote(
            grads.at[:, (my_z + k) % NZ], ret_z.at[my_z], rz_send.at[k], rz_recv.at[NZ - k], at_z(k)
        )

    def ring_step(c, s):
        if c >= 2 and s == 0:
            wait_bytes(ring.at[c, 0], cot_in.at[c])
        if s > 0:
            ring_copy(c, s - 1, True).wait_recv()
            ring_copy(c, s - 1, False).wait_recv()
        if s < LAST and (c >= 2 or s > 0):
            ring_copy(c, s, True).start()
            ring_copy(c, s, False).start()
        if (c, s) == (0, 1):
            for k in range(1, NZ):
                dest_copy(k).wait_recv()
        if s in (0, LAST):
            deliver(c, s)
        else:
            deliver(c, -s)
            deliver(c, s)

    for c, s in ((0, 0), (1, 0), (0, 1), (1, 1), (0, 2)):
        ring_step(c, s)
    attn_along_z()
    for c, s in ((1, 2), (0, 3), (2, 0), (1, 3), (3, 0), (0, 4), (2, 1), (1, 4), (3, 1)):
        ring_step(c, s)
    every = range(len(SOURCES))
    arrived(0, every)
    input_grad(0)
    ring_step(2, 2)
    attn_arrived()
    weight_grad(0)
    ring_step(3, 2)
    arrived(1, every)
    input_grad(1)
    ring_step(2, 3)
    for c in range(NC - 2, NC):
        wait_bytes(w_chunk.at[c % 2], w_sem.at[c])
        arrived(c, (0,))
    rows_grad(SOURCES[0])
    ring_step(3, 3)
    weight_grad(1)
    weight_pair(0)
    ring_step(2, 4)
    for c in range(NC - 2, NC):
        arrived(c, (1,))
    rows_grad(SOURCES[1])
    weight_pair(1)
    ring_step(3, 4)
    arrived(2, (2, 3))
    weight_grad(2)
    arrived(3, (2, 3))
    rows_grad(SOURCES[2] + SOURCES[3])
    weight_pair(2)
    weight_grad(3)
    weight_grad_sum(0)
    weight_pair(3)
    weight_grad_sum(1)

    def ret_x_start(z):
        for k in range(NX):
            src, dst = ret_z.at[z, (my_x + k) % NX], ret_x.at[my_x, z]
            if k == 0:
                pltpu.make_async_copy(src, dst, rx_own).start()
            else:
                remote(src, dst, rx_send.at[k], rx_recv.at[NX - k], at_x(k)).start()

    pltpu.make_async_copy(grads.at[:, my_z], ret_z.at[my_z], rz_own).wait()
    ret_x_start(my_z)
    for k in (1, 7, 2, 6, 3, 5, 4):
        ret_z_copy(k).wait_recv()
        ret_x_start((my_z - k + NZ) % NZ)
    weight_grad_sum(2)
    weight_grad_sum(3)
    for k in range(NX):
        wait_bytes(ret_x.at[k], rx_own if k == 0 else rx_recv.at[k])

    back = jnp.where(slots == dests[0, 0:1, :], 1.0, 0.0).astype(BF16)
    for p in range(PIECES):
        pieces = jnp.concatenate(
            [ret_x[g // HALVES, (g % HALVES) * PIECES + p] for g in range(NGROUP)], 0
        )
        grad_ref[:, p * feats:(p + 1) * feats] = lax.dot_general(
            back, pieces, (((0,), (0,)), ((), ())), preferred_element_type=F32
        ).astype(BF16)

    for k in range(1, NZ):
        dest_copy(k).wait_send()
        attn_z_copy(k).wait_send()
        ret_z_copy(k).wait_send()
    for k in range(1, NX):
        attn_x_copy(k).wait_send()
        wait_bytes(ret_x.at[k], rx_send.at[k])
    for c in range(NC):
        for s in range(LAST):
            ring_copy(c, s, True).wait_send()
            ring_copy(c, s, False).wait_send()
        x_sends_done(c)
    for c in range(NC - 2, NC):
        pair_copy(c).wait_send()
        for k in range(1, NY):
            rs_copy(c, k).wait_send()


def backward(mod, gm, attn, cot, w):
    tok, model = cot.shape
    width = model // NC
    feats = w.shape[0]
    dma = pltpu.SemaphoreType.DMA
    vmem = pl.BlockSpec(memory_space=pltpu.VMEM)
    hbm = pl.BlockSpec(memory_space=pl.ANY)
    return pl.pallas_call(
        kernel,
        out_shape=(
            jax.ShapeDtypeStruct((tok, model), BF16),
            jax.ShapeDtypeStruct((feats, model // NDP), BF16),
        ),
        in_specs=[
            vmem, pl.BlockSpec(memory_space=pltpu.SMEM), hbm, hbm, hbm,
        ],
        out_specs=(vmem, vmem),
        scratch_shapes=[
            pltpu.VMEM((tok, model), BF16),
            pltpu.VMEM((NC, NZ, tok, width), BF16),
            pltpu.VMEM((NZ, 8, tok), jnp.int32),
            pltpu.VMEM((NC, NX, NZ, CAP, width), BF16),
            pltpu.VMEM((NC, NX, NZ, CAP, width), BF16),
            pltpu.VMEM((2, feats, width), BF16),
            pltpu.VMEM((2, CORES, NY, feats, width // NDP), BF16),
            pltpu.VMEM((NC, NY, feats, width // NDP), BF16),
            pltpu.VMEM((NC, NY, feats, width // NDP), BF16),
            pltpu.VMEM((NX, NZ, CAP, feats), F32),
            pltpu.VMEM((NX, HALVES, CAP, model), BF16),
            pltpu.VMEM((NX, HALVES, CAP, model), BF16),
            pltpu.VMEM((NX, NZ, CAP, feats), BF16),
            pltpu.VMEM((feats, NX * NZ * CAP), BF16),
            pltpu.VMEM((NX, NZ, CAP, feats), BF16),
            pltpu.VMEM((NZ, NX, CAP, feats), BF16),
            pltpu.VMEM((NX, NZ, CAP, feats), BF16),
            dma, dma((NC,)), dma((NZ,)), dma((NZ,)),
            dma((NC, LAST)), dma((NC, LAST)), dma((NC, LAST)), dma((NC, LAST)),
            dma((NC, NX)), dma((NC, LAST, NX)), dma((NC, LAST)),
            dma((NX,)), dma((NX,)), dma,
            dma((NZ,)), dma((NZ,)), dma,
            dma((NC,)),
            dma((NC,)), dma((NC,)), dma((NC, NY)), dma((NC, NY)), dma((NC,)),
            dma((NZ,)), dma((NZ,)), dma,
            dma((NX,)), dma((NX,)), dma,
        ],
        compiler_params=pltpu.CompilerParams(
            collective_id=0, has_side_effects=True, vmem_limit_bytes=63 * 1024 * 1024
        ),
        name="moe_proj_backward",
    )(mod, gm, attn, cot, w)


def per_device(attn_out, out_cot, modality, group_modality, o_weight):
    return backward(modality.reshape(1, -1), group_modality, attn_out, out_cot, o_weight)


def solution(mesh):
    return jax.shard_map(
        per_device,
        mesh=mesh,
        in_specs=(
            P(("dp", "tower"), None),
            P(("dp", "tower"), None),
            P(("dp", "tower")),
            P(),
            P("tower", None),
        ),
        out_specs=(P(("dp", "tower"), None), P("tower", "dp")),
        check_vma=False,
    )
```

```python
import jax
import jax.numpy as jnp
from jax import lax
from jax.experimental import pallas as pl
from jax.experimental.pallas import tpu as pltpu
from jax.sharding import PartitionSpec as P

NGROUP = 8
CAP = 24
NX = 4
NZ = 8
HALVES = NGROUP // NX
PIECES = NZ // HALVES
NDP = 8
CORES = 2
NY = NDP // CORES
SOURCES = ((0, -1, 1), (-2, 2), (-3, 3), (4,))
NC = 4
LAST = NZ // 2
TILE = 256
MESH = pl.DeviceIdType.MESH
F32 = jnp.float32
BF16 = jnp.bfloat16


def kernel(
    mod_ref, gm_ref, attn_hbm, cot_hbm, w_ref, grad_ref, wgrad_ref,
    attn_ref, ring, dests, staged, cot_got, w_chunk, partial, other, terms, acc,
    attn_own, attn_x, attn_got, attn_t, grads, ret_z, ret_x,
    attn_in, cot_in, dest_send, dest_recv, right_send, right_recv, left_send, left_recv,
    x_send, x_recv, x_own, ax_send, ax_recv, ax_own, az_send, az_recv, az_own,
    w_sem, pair_send, pair_recv, rs_send, rs_recv, rs_own, rz_send, rz_recv, rz_own, rx_send, rx_recv, rx_own,
):
    tok = cot_hbm.shape[0]
    width = cot_hbm.shape[1] // NC
    cols = width // NDP
    own_cols = wgrad_ref.shape[1]
    feats = w_ref.shape[0]
    half = width // 2
    me, my_d = lax.axis_index("tower"), lax.axis_index("dp")
    my_x, my_z = me // NZ, me % NZ
    my_half = my_z // PIECES
    my_y, my_core = my_d // CORES, my_d % CORES

    def at_z(k):
        return {"tower": my_x * NZ + (my_z + k + NZ) % NZ}

    def at_x(k):
        return {"tower": ((my_x + k) % NX) * NZ + my_z}

    def at_y(k):
        return {"dp": ((my_y + k) % NY) * CORES + my_core}

    other_core = {"dp": my_y * CORES + 1 - my_core}

    def remote(src, dst, send, recv, device):
        return pltpu.make_async_remote_copy(
            src_ref=src, dst_ref=dst, send_sem=send, recv_sem=recv,
            device_id=device, device_id_type=MESH,
        )

    def wait_bytes(ref, sem):
        pltpu.make_async_copy(ref, ref, sem).wait()

    def w_load(c, d):
        return pltpu.make_async_copy(
            w_ref.at[:, pl.ds(d * own_cols + c * cols, cols)],
            w_chunk.at[c % 2, :, pl.ds(d * cols, cols)],
            w_sem.at[c],
        )

    def own_block(c):
        for d in range(NDP):
            pltpu.make_async_copy(
                cot_hbm.at[:, pl.ds(d * own_cols + c * cols, cols)],
                ring.at[c, 0, :, pl.ds(d * cols, cols)],
                cot_in.at[c],
            ).start()

    attn_load = pltpu.make_async_copy(attn_hbm, attn_ref, attn_in)
    barrier = pltpu.get_barrier_semaphore()
    for k in range(1, NZ):
        pl.semaphore_signal(barrier, inc=1, device_id=at_z(k), device_id_type=MESH)
    for k in range(1, NX):
        pl.semaphore_signal(barrier, inc=1, device_id=at_x(k), device_id_type=MESH)
    for k in range(1, NY):
        pl.semaphore_signal(barrier, inc=1, device_id=at_y(k), device_id_type=MESH)
    pl.semaphore_signal(barrier, inc=1, device_id=other_core, device_id_type=MESH)

    own_block(0)
    own_block(1)
    attn_load.start()
    pl.semaphore_wait(barrier, NZ - 1 + NX - 1 + NY)

    def ring_copy(c, s, right):
        off = -s if right else s
        src = ring.at[c, off % NZ]
        dst = ring.at[c, (off - 1 if right else off + 1) % NZ]
        if s == LAST - 1:
            part = pl.ds(0, half) if right else pl.ds(half, half)
            src, dst = src.at[:, part], dst.at[:, part]
        return remote(
            src, dst,
            (right_send if right else left_send).at[c, s],
            (right_recv if right else left_recv).at[c, s],
            at_z(1 if right else -1),
        )

    for c in range(2):
        wait_bytes(ring.at[c, 0], cot_in.at[c])
        ring_copy(c, 0, True).start()
        ring_copy(c, 0, False).start()
    for c in range(2, NC):
        own_block(c)
    for c in range(2):
        for d in range(NDP):
            w_load(c, d).start()

    mod = jnp.broadcast_to(mod_ref[...], (8, tok))
    kinds = [(mod == m).astype(F32) for m in range(3)]
    t_from = lax.broadcasted_iota(jnp.int32, (tok, tok), 0)
    t_to = lax.broadcasted_iota(jnp.int32, (tok, tok), 1)
    earlier = (t_from < t_to).astype(F32).astype(BF16)
    before = jnp.dot(jnp.concatenate(kinds, 0).astype(BF16), earlier, preferred_element_type=F32)
    order = sum(before[8 * m:8 * m + 8] * kinds[m] for m in range(3))
    serves = [gm_ref[g] for g in range(NGROUP)]
    how_many = jnp.ones_like(mod)
    for m in range(3):
        count = sum((s == m).astype(jnp.int32) for s in serves)
        how_many = jnp.where(mod == m, count, how_many)
    per = how_many.astype(F32)
    turn = (order.astype(jnp.int32) + me).astype(F32)
    target = (turn - jnp.floor((turn + 0.5) / per) * per).astype(jnp.int32)
    routed = jnp.zeros_like(mod)
    for g in range(NGROUP):
        rank = sum(((s == serves[g]).astype(jnp.int32) for s in serves[:g]), jnp.int32(0))
        routed = jnp.where((mod == serves[g]) & (target == rank), g, routed)
    dest = routed * CAP + jnp.floor((order + 0.5) / per).astype(jnp.int32)
    dests[0] = dest

    def dest_copy(k):
        return remote(dests.at[0], dests.at[NZ - k], dest_send.at[k], dest_recv.at[NZ - k], at_z(k))

    for k in range(1, NZ):
        dest_copy(k).start()

    slots = lax.broadcasted_iota(jnp.int32, (NGROUP * CAP, tok), 0)
    attn_load.wait()
    pick_own = jnp.where(slots == dest[0:1], 1.0, 0.0).astype(BF16)
    for p in range(PIECES):
        got = jnp.dot(pick_own, attn_ref[:, p * feats:(p + 1) * feats], preferred_element_type=F32)
        attn_own[:, :, :, p * feats:(p + 1) * feats] = got.astype(BF16).reshape(NX, HALVES, CAP, feats)

    def attn_x_copy(k):
        return remote(
            attn_own.at[(my_x + k) % NX], attn_x.at[my_x], ax_send.at[k], ax_recv.at[NX - k], at_x(k)
        )

    own_ax = pltpu.make_async_copy(attn_own.at[my_x], attn_x.at[my_x], ax_own)
    own_ax.start()
    for k in range(1, NX):
        attn_x_copy(k).start()

    def attn_z_src(k):
        z = (my_z + k) % NZ
        start = pl.multiple_of((z % PIECES) * feats, feats)
        return attn_x.at[:, z // PIECES, :, pl.ds(start, feats)]

    def attn_z_copy(k):
        return remote(
            attn_z_src(k), attn_got.at[:, my_z], az_send.at[k], az_recv.at[NZ - k], at_z(k)
        )

    def attn_along_z():
        own_ax.wait()
        for k in range(1, NX):
            attn_x_copy(k).wait_recv()
        pltpu.make_async_copy(attn_z_src(0), attn_got.at[:, my_z], az_own).start()
        for k in range(1, NZ):
            attn_z_copy(k).start()

    def attn_arrived():
        pltpu.make_async_copy(attn_z_src(0), attn_got.at[:, my_z], az_own).wait()
        for k in range(1, NZ):
            attn_z_copy(k).wait_recv()

        @pl.loop(0, feats // TILE)
        def _(j):
            at = pl.ds(pl.multiple_of(j * TILE, TILE), TILE)
            attn_t[at, :] = jnp.transpose(attn_got[:, :, :, at].reshape(NX * NZ * CAP, TILE))

    rows = lax.broadcasted_iota(jnp.int32, (NX * CAP, tok), 0)
    x_of = sum((rows >= CAP * k).astype(jnp.int32) for k in range(1, NX))
    wanted = rows + CAP * (HALVES - 1) * x_of + CAP * my_half

    def deliver(c, off):
        slot = off % NZ
        pick = jnp.where(wanted == dests[slot, 0:1, :], 1.0, 0.0).astype(BF16)
        got = jnp.dot(pick, ring[c, slot], preferred_element_type=F32).astype(BF16)
        for x in range(NX):
            staged[c, x, slot] = got[x * CAP:(x + 1) * CAP]
        part = abs(off) - 1 if off else 0
        lands = cot_got.at[c, my_x, (my_z + off + NZ) % NZ]
        for k in range(NX):
            src = staged.at[c, (my_x + k) % NX, slot]
            if k == 0:
                pltpu.make_async_copy(src, lands, x_own.at[c, part]).start()
            else:
                remote(
                    src, lands, x_send.at[c, k], x_recv.at[c, part, NX - k], at_x(k)
                ).start()

    def arrived(c, parts):
        for part in parts:
            count = len(SOURCES[part])
            wait_bytes(staged.at[c, 0, pl.ds(0, count)], x_own.at[c, part])
            for k in range(1, NX):
                wait_bytes(staged.at[c, k, pl.ds(0, count)], x_recv.at[c, part, k])

    def x_sends_done(c):
        for k in range(1, NX):
            wait_bytes(staged.at[c, k], x_send.at[c, k])

    def input_grad(c):
        wait_bytes(w_chunk.at[c % 2], w_sem.at[c])

        @pl.loop(0, feats // TILE)
        def _(j):
            at = pl.ds(pl.multiple_of(j * TILE, TILE), TILE)
            term = lax.dot_general(
                cot_got[c].reshape(NX * NZ * CAP, width), w_chunk[c % 2, at, :],
                (((1,), (1,)), ((), ())), preferred_element_type=F32,
            )
            term = term.reshape(NX, NZ, CAP, TILE)
            acc[:, :, :, at] = term if c == 0 else acc[:, :, :, at] + term

        for d in range(NDP):
            w_load(c + 2, d).start()

    def rows_grad(offsets):
        zs = [(my_z + off + NZ) % NZ for off in offsets]
        count = NX * CAP

        @pl.loop(0, feats // TILE)
        def _(j):
            at = pl.ds(pl.multiple_of(j * TILE, TILE), TILE)
            term = sum(
                lax.dot_general(
                    jnp.concatenate([cot_got[c, :, z].reshape(count, width) for z in zs], 0),
                    w_chunk[c % 2, at, :], (((1,), (1,)), ((), ())), preferred_element_type=F32,
                )
                for c in range(NC - 2, NC)
            )
            for i, z in enumerate(zs):
                total = term[i * count:(i + 1) * count].reshape(NX, CAP, TILE) + acc[:, z, :, at]
                grads[:, z, :, at] = total.astype(BF16)

        for off in offsets:
            if off == 0:
                pltpu.make_async_copy(grads.at[:, my_z], ret_z.at[my_z], rz_own).start()
            else:
                ret_z_copy(off % NZ).start()

    def pair_copy(c):
        return remote(
            partial.at[c % 2, 1 - my_core], other.at[c], pair_send.at[c], pair_recv.at[c], other_core
        )

    def rs_copy(c, k):
        return remote(
            partial.at[c % 2, my_core, (my_y + k) % NY], terms.at[c, my_y],
            rs_send.at[c, k], rs_recv.at[c, NY - k], at_y(k),
        )

    def rs_own_copy(c):
        return pltpu.make_async_copy(
            partial.at[c % 2, my_core, my_y], terms.at[c, my_y], rs_own.at[c]
        )

    def weight_sends_done(c):
        pair_copy(c).wait_send()
        for k in range(1, NY):
            rs_copy(c, k).wait_send()
        rs_own_copy(c).wait()

    def weight_grad(c):
        if c >= 2:
            weight_sends_done(c - 2)

        @pl.loop(0, width // TILE)
        def _(j):
            at = pl.ds(pl.multiple_of(j * TILE, TILE), TILE)
            term = jnp.dot(
                attn_t[...], cot_got[c, :, :, :, at].reshape(NX * NZ * CAP, TILE),
                preferred_element_type=F32,
            ).astype(BF16)
            for i in range(CORES):
                partial[c % 2, i, j] = term[:, i * cols:(i + 1) * cols]

        pair_copy(c).start()

    def weight_pair(c):
        pair_copy(c).wait_recv()

        @pl.loop(0, feats // TILE)
        def _(j):
            at = pl.ds(pl.multiple_of(j * TILE, TILE), TILE)
            for y in range(NY):
                both = partial[c % 2, my_core, y, at, :].astype(F32) + other[c, y, at, :].astype(F32)
                partial[c % 2, my_core, y, at, :] = both.astype(BF16)

        rs_own_copy(c).start()
        for k in range(1, NY):
            rs_copy(c, k).start()

    def weight_grad_sum(c):
        if c >= NC - 2:
            rs_own_copy(c).wait()
        for k in range(1, NY):
            rs_copy(c, k).wait_recv()

        @pl.loop(0, feats // TILE)
        def _(j):
            at = pl.ds(pl.multiple_of(j * TILE, TILE), TILE)
            total = terms[c, 0, at, :].astype(F32)
            for y in range(1, NY):
                total += terms[c, y, at, :].astype(F32)
            wgrad_ref[at, c * cols:(c + 1) * cols] = total.astype(BF16)

    def ret_z_copy(k):
        return remote(
            grads.at[:, (my_z + k) % NZ], ret_z.at[my_z], rz_send.at[k], rz_recv.at[NZ - k], at_z(k)
        )

    def ring_step(c, s):
        if c >= 2 and s == 0:
            wait_bytes(ring.at[c, 0], cot_in.at[c])
        if s > 0:
            ring_copy(c, s - 1, True).wait_recv()
            ring_copy(c, s - 1, False).wait_recv()
        if s < LAST and (c >= 2 or s > 0):
            ring_copy(c, s, True).start()
            ring_copy(c, s, False).start()
        if (c, s) == (0, 1):
            for k in range(1, NZ):
                dest_copy(k).wait_recv()
        if s in (0, LAST):
            deliver(c, s)
        else:
            deliver(c, -s)
            deliver(c, s)

    for c, s in ((0, 0), (1, 0), (0, 1), (1, 1), (0, 2)):
        ring_step(c, s)
    attn_along_z()
    every = range(len(SOURCES))
    for c, s in ((1, 2), (0, 3), (2, 0), (1, 3), (3, 0), (0, 4), (2, 1), (1, 4)):
        ring_step(c, s)
    arrived(0, every)
    input_grad(0)
    ring_step(3, 1)
    arrived(1, every)
    input_grad(1)
    ring_step(2, 2)
    attn_arrived()
    weight_grad(0)
    ring_step(3, 2)
    weight_grad(1)
    weight_pair(0)
    ring_step(2, 3)
    for c in range(NC - 2, NC):
        wait_bytes(w_chunk.at[c % 2], w_sem.at[c])
        arrived(c, (0,))
    rows_grad(SOURCES[0])
    ring_step(3, 3)
    weight_pair(1)
    for c in range(NC - 2, NC):
        arrived(c, (1,))
    rows_grad(SOURCES[1])
    ring_step(2, 4)
    for c in range(NC - 2, NC):
        arrived(c, (2,))
    rows_grad(SOURCES[2])
    ring_step(3, 4)
    arrived(2, (3,))
    weight_grad(2)
    arrived(3, (3,))
    rows_grad(SOURCES[3])
    weight_pair(2)
    weight_grad(3)
    weight_pair(3)
    weight_grad_sum(0)
    weight_grad_sum(1)

    def ret_x_start(z):
        for k in range(NX):
            src, dst = ret_z.at[z, (my_x + k) % NX], ret_x.at[my_x, z]
            if k == 0:
                pltpu.make_async_copy(src, dst, rx_own).start()
            else:
                remote(src, dst, rx_send.at[k], rx_recv.at[NX - k], at_x(k)).start()

    pltpu.make_async_copy(grads.at[:, my_z], ret_z.at[my_z], rz_own).wait()
    ret_x_start(my_z)
    for k in (1, 7, 2, 6, 3, 5, 4):
        ret_z_copy(k).wait_recv()
        ret_x_start((my_z - k + NZ) % NZ)
    weight_grad_sum(2)
    weight_grad_sum(3)
    for k in range(NX):
        wait_bytes(ret_x.at[k], rx_own if k == 0 else rx_recv.at[k])

    back = jnp.where(slots == dests[0, 0:1, :], 1.0, 0.0).astype(BF16)
    for p in range(PIECES):
        pieces = jnp.concatenate(
            [ret_x[g // HALVES, (g % HALVES) * PIECES + p] for g in range(NGROUP)], 0
        )
        grad_ref[:, p * feats:(p + 1) * feats] = lax.dot_general(
            back, pieces, (((0,), (0,)), ((), ())), preferred_element_type=F32
        ).astype(BF16)

    for k in range(1, NZ):
        dest_copy(k).wait_send()
        attn_z_copy(k).wait_send()
        ret_z_copy(k).wait_send()
    for k in range(1, NX):
        attn_x_copy(k).wait_send()
        wait_bytes(ret_x.at[k], rx_send.at[k])
    for c in range(NC):
        for s in range(LAST):
            ring_copy(c, s, True).wait_send()
            ring_copy(c, s, False).wait_send()
        x_sends_done(c)
    for c in range(NC - 2, NC):
        pair_copy(c).wait_send()
        for k in range(1, NY):
            rs_copy(c, k).wait_send()


def backward(mod, gm, attn, cot, w):
    tok, model = cot.shape
    width = model // NC
    feats = w.shape[0]
    dma = pltpu.SemaphoreType.DMA
    vmem = pl.BlockSpec(memory_space=pltpu.VMEM)
    hbm = pl.BlockSpec(memory_space=pl.ANY)
    return pl.pallas_call(
        kernel,
        out_shape=(
            jax.ShapeDtypeStruct((tok, model), BF16),
            jax.ShapeDtypeStruct((feats, model // NDP), BF16),
        ),
        in_specs=[
            vmem, pl.BlockSpec(memory_space=pltpu.SMEM), hbm, hbm, hbm,
        ],
        out_specs=(vmem, vmem),
        scratch_shapes=[
            pltpu.VMEM((tok, model), BF16),
            pltpu.VMEM((NC, NZ, tok, width), BF16),
            pltpu.VMEM((NZ, 8, tok), jnp.int32),
            pltpu.VMEM((NC, NX, NZ, CAP, width), BF16),
            pltpu.VMEM((NC, NX, NZ, CAP, width), BF16),
            pltpu.VMEM((2, feats, width), BF16),
            pltpu.VMEM((2, CORES, NY, feats, width // NDP), BF16),
            pltpu.VMEM((NC, NY, feats, width // NDP), BF16),
            pltpu.VMEM((NC, NY, feats, width // NDP), BF16),
            pltpu.VMEM((NX, NZ, CAP, feats), F32),
            pltpu.VMEM((NX, HALVES, CAP, model), BF16),
            pltpu.VMEM((NX, HALVES, CAP, model), BF16),
            pltpu.VMEM((NX, NZ, CAP, feats), BF16),
            pltpu.VMEM((feats, NX * NZ * CAP), BF16),
            pltpu.VMEM((NX, NZ, CAP, feats), BF16),
            pltpu.VMEM((NZ, NX, CAP, feats), BF16),
            pltpu.VMEM((NX, NZ, CAP, feats), BF16),
            dma, dma((NC,)), dma((NZ,)), dma((NZ,)),
            dma((NC, LAST)), dma((NC, LAST)), dma((NC, LAST)), dma((NC, LAST)),
            dma((NC, NX)), dma((NC, LAST, NX)), dma((NC, LAST)),
            dma((NX,)), dma((NX,)), dma,
            dma((NZ,)), dma((NZ,)), dma,
            dma((NC,)),
            dma((NC,)), dma((NC,)), dma((NC, NY)), dma((NC, NY)), dma((NC,)),
            dma((NZ,)), dma((NZ,)), dma,
            dma((NX,)), dma((NX,)), dma,
        ],
        compiler_params=pltpu.CompilerParams(
            collective_id=0, has_side_effects=True, vmem_limit_bytes=63 * 1024 * 1024
        ),
        name="moe_proj_backward",
    )(mod, gm, attn, cot, w)


def hand_over(values):
    parts = 8

    def body(*refs):
        copies = []
        for i, value in enumerate(values):
            rows = value.shape[0] // parts
            for k in range(parts):
                at = pl.ds(k * rows, rows)
                copies.append(pltpu.make_async_copy(
                    refs[i].at[at], refs[len(values) + i].at[at], refs[-1].at[i, k]
                ))
        for copy in copies:
            copy.start()
        for copy in copies:
            copy.wait()

    hbm = pl.BlockSpec(memory_space=pl.ANY)
    return pl.pallas_call(
        body,
        out_shape=tuple(jax.ShapeDtypeStruct(v.shape, v.dtype) for v in values),
        in_specs=[hbm] * len(values),
        out_specs=(hbm,) * len(values),
        scratch_shapes=[pltpu.SemaphoreType.DMA((len(values), parts))],
        name="hand_over",
    )(*values)


def per_device(attn_out, out_cot, modality, group_modality, o_weight):
    return hand_over(
        backward(modality.reshape(1, -1), group_modality, attn_out, out_cot, o_weight)
    )


def solution(mesh):
    return jax.shard_map(
        per_device,
        mesh=mesh,
        in_specs=(
            P(("dp", "tower"), None),
            P(("dp", "tower"), None),
            P(("dp", "tower")),
            P(),
            P("tower", None),
        ),
        out_specs=(P(("dp", "tower"), None), P("tower", "dp")),
        check_vma=False,
    )
```

```python
import jax
import jax.numpy as jnp
from jax import lax
from jax.experimental import pallas as pl
from jax.experimental.pallas import tpu as pltpu
from jax.sharding import PartitionSpec as P

NGROUP = 8
CAP = 24
NX = 4
NZ = 8
HALVES = NGROUP // NX
PIECES = NZ // HALVES
NDP = 8
CORES = 2
NY = NDP // CORES
SOURCES = ((0, -1, 1), (-2, 2), (-3, 3), (4,))
NC = 4
LAST = NZ // 2
TILE = 256
MESH = pl.DeviceIdType.MESH
F32 = jnp.float32
BF16 = jnp.bfloat16


def kernel(
    mod_ref, gm_ref, attn_hbm, cot_hbm, w_ref, ret_x, dest_ref, wgrad_ref,
    attn_ref, ring, dests, staged, cot_got, w_chunk, partial, other, terms, acc,
    attn_own, attn_x, attn_got, attn_t, grads, ret_z,
    attn_in, cot_in, dest_send, dest_recv, right_send, right_recv, left_send, left_recv,
    x_send, x_recv, x_own, ax_send, ax_recv, ax_own, az_send, az_recv, az_own,
    w_sem, pair_send, pair_recv, rs_send, rs_recv, rs_own, rz_send, rz_recv, rz_own, rx_send, rx_recv, rx_own,
):
    tok = cot_hbm.shape[0]
    width = cot_hbm.shape[1] // NC
    cols = width // NDP
    own_cols = wgrad_ref.shape[1]
    feats = w_ref.shape[0]
    half = width // 2
    me, my_d = lax.axis_index("tower"), lax.axis_index("dp")
    my_x, my_z = me // NZ, me % NZ
    my_half = my_z // PIECES
    my_y, my_core = my_d // CORES, my_d % CORES

    def at_z(k):
        return {"tower": my_x * NZ + (my_z + k + NZ) % NZ}

    def at_x(k):
        return {"tower": ((my_x + k) % NX) * NZ + my_z}

    def at_y(k):
        return {"dp": ((my_y + k) % NY) * CORES + my_core}

    other_core = {"dp": my_y * CORES + 1 - my_core}

    def remote(src, dst, send, recv, device):
        return pltpu.make_async_remote_copy(
            src_ref=src, dst_ref=dst, send_sem=send, recv_sem=recv,
            device_id=device, device_id_type=MESH,
        )

    def wait_bytes(ref, sem):
        pltpu.make_async_copy(ref, ref, sem).wait()

    def w_load(c, d):
        return pltpu.make_async_copy(
            w_ref.at[:, pl.ds(d * own_cols + c * cols, cols)],
            w_chunk.at[c % 2, :, pl.ds(d * cols, cols)],
            w_sem.at[c],
        )

    def own_block(c):
        for d in range(NDP):
            pltpu.make_async_copy(
                cot_hbm.at[:, pl.ds(d * own_cols + c * cols, cols)],
                ring.at[c, 0, :, pl.ds(d * cols, cols)],
                cot_in.at[c],
            ).start()

    attn_load = pltpu.make_async_copy(attn_hbm, attn_ref, attn_in)
    barrier = pltpu.get_barrier_semaphore()
    for k in range(1, NZ):
        pl.semaphore_signal(barrier, inc=1, device_id=at_z(k), device_id_type=MESH)
    for k in range(1, NX):
        pl.semaphore_signal(barrier, inc=1, device_id=at_x(k), device_id_type=MESH)
    for k in range(1, NY):
        pl.semaphore_signal(barrier, inc=1, device_id=at_y(k), device_id_type=MESH)
    pl.semaphore_signal(barrier, inc=1, device_id=other_core, device_id_type=MESH)

    own_block(0)
    own_block(1)
    attn_load.start()
    pl.semaphore_wait(barrier, NZ - 1 + NX - 1 + NY)

    def ring_copy(c, s, right):
        off = -s if right else s
        src = ring.at[c, off % NZ]
        dst = ring.at[c, (off - 1 if right else off + 1) % NZ]
        if s == LAST - 1:
            part = pl.ds(0, half) if right else pl.ds(half, half)
            src, dst = src.at[:, part], dst.at[:, part]
        return remote(
            src, dst,
            (right_send if right else left_send).at[c, s],
            (right_recv if right else left_recv).at[c, s],
            at_z(1 if right else -1),
        )

    for c in range(2):
        wait_bytes(ring.at[c, 0], cot_in.at[c])
        ring_copy(c, 0, True).start()
        ring_copy(c, 0, False).start()
    for c in range(2, NC):
        own_block(c)
    for c in range(2):
        for d in range(NDP):
            w_load(c, d).start()

    mod = jnp.broadcast_to(mod_ref[...], (8, tok))
    kinds = [(mod == m).astype(F32) for m in range(3)]
    t_from = lax.broadcasted_iota(jnp.int32, (tok, tok), 0)
    t_to = lax.broadcasted_iota(jnp.int32, (tok, tok), 1)
    earlier = (t_from < t_to).astype(F32).astype(BF16)
    before = jnp.dot(jnp.concatenate(kinds, 0).astype(BF16), earlier, preferred_element_type=F32)
    order = sum(before[8 * m:8 * m + 8] * kinds[m] for m in range(3))
    serves = [gm_ref[g] for g in range(NGROUP)]
    how_many = jnp.ones_like(mod)
    for m in range(3):
        count = sum((s == m).astype(jnp.int32) for s in serves)
        how_many = jnp.where(mod == m, count, how_many)
    per = how_many.astype(F32)
    turn = (order.astype(jnp.int32) + me).astype(F32)
    target = (turn - jnp.floor((turn + 0.5) / per) * per).astype(jnp.int32)
    routed = jnp.zeros_like(mod)
    for g in range(NGROUP):
        rank = sum(((s == serves[g]).astype(jnp.int32) for s in serves[:g]), jnp.int32(0))
        routed = jnp.where((mod == serves[g]) & (target == rank), g, routed)
    dest = routed * CAP + jnp.floor((order + 0.5) / per).astype(jnp.int32)
    dests[0] = dest
    dest_ref[...] = dest

    def dest_copy(k):
        return remote(dests.at[0], dests.at[NZ - k], dest_send.at[k], dest_recv.at[NZ - k], at_z(k))

    for k in range(1, NZ):
        dest_copy(k).start()

    slots = lax.broadcasted_iota(jnp.int32, (NGROUP * CAP, tok), 0)
    attn_load.wait()
    pick_own = jnp.where(slots == dest[0:1], 1.0, 0.0).astype(BF16)
    for p in range(PIECES):
        got = jnp.dot(pick_own, attn_ref[:, p * feats:(p + 1) * feats], preferred_element_type=F32)
        attn_own[:, :, :, p * feats:(p + 1) * feats] = got.astype(BF16).reshape(NX, HALVES, CAP, feats)

    def attn_x_copy(k):
        return remote(
            attn_own.at[(my_x + k) % NX], attn_x.at[my_x], ax_send.at[k], ax_recv.at[NX - k], at_x(k)
        )

    own_ax = pltpu.make_async_copy(attn_own.at[my_x], attn_x.at[my_x], ax_own)
    own_ax.start()
    for k in range(1, NX):
        attn_x_copy(k).start()

    def attn_z_src(k):
        z = (my_z + k) % NZ
        start = pl.multiple_of((z % PIECES) * feats, feats)
        return attn_x.at[:, z // PIECES, :, pl.ds(start, feats)]

    def attn_z_copy(k):
        return remote(
            attn_z_src(k), attn_got.at[:, my_z], az_send.at[k], az_recv.at[NZ - k], at_z(k)
        )

    def attn_along_z():
        own_ax.wait()
        for k in range(1, NX):
            attn_x_copy(k).wait_recv()
        pltpu.make_async_copy(attn_z_src(0), attn_got.at[:, my_z], az_own).start()
        for k in range(1, NZ):
            attn_z_copy(k).start()

    def attn_arrived():
        pltpu.make_async_copy(attn_z_src(0), attn_got.at[:, my_z], az_own).wait()
        for k in range(1, NZ):
            attn_z_copy(k).wait_recv()

        @pl.loop(0, feats // TILE)
        def _(j):
            at = pl.ds(pl.multiple_of(j * TILE, TILE), TILE)
            attn_t[at, :] = jnp.transpose(attn_got[:, :, :, at].reshape(NX * NZ * CAP, TILE))

    rows = lax.broadcasted_iota(jnp.int32, (NX * CAP, tok), 0)
    x_of = sum((rows >= CAP * k).astype(jnp.int32) for k in range(1, NX))
    wanted = rows + CAP * (HALVES - 1) * x_of + CAP * my_half

    def deliver(c, off):
        slot = off % NZ
        pick = jnp.where(wanted == dests[slot, 0:1, :], 1.0, 0.0).astype(BF16)
        got = jnp.dot(pick, ring[c, slot], preferred_element_type=F32).astype(BF16)
        for x in range(NX):
            staged[c, x, slot] = got[x * CAP:(x + 1) * CAP]
        part = abs(off) - 1 if off else 0
        lands = cot_got.at[c, my_x, (my_z + off + NZ) % NZ]
        for k in range(NX):
            src = staged.at[c, (my_x + k) % NX, slot]
            if k == 0:
                pltpu.make_async_copy(src, lands, x_own.at[c, part]).start()
            else:
                remote(
                    src, lands, x_send.at[c, k], x_recv.at[c, part, NX - k], at_x(k)
                ).start()

    def arrived(c, parts):
        for part in parts:
            count = len(SOURCES[part])
            wait_bytes(staged.at[c, 0, pl.ds(0, count)], x_own.at[c, part])
            for k in range(1, NX):
                wait_bytes(staged.at[c, k, pl.ds(0, count)], x_recv.at[c, part, k])

    def x_sends_done(c):
        for k in range(1, NX):
            wait_bytes(staged.at[c, k], x_send.at[c, k])

    def input_grad(c):
        wait_bytes(w_chunk.at[c % 2], w_sem.at[c])

        @pl.loop(0, feats // TILE)
        def _(j):
            at = pl.ds(pl.multiple_of(j * TILE, TILE), TILE)
            term = lax.dot_general(
                cot_got[c].reshape(NX * NZ * CAP, width), w_chunk[c % 2, at, :],
                (((1,), (1,)), ((), ())), preferred_element_type=F32,
            )
            term = term.reshape(NX, NZ, CAP, TILE)
            acc[:, :, :, at] = term if c == 0 else acc[:, :, :, at] + term

        for d in range(NDP):
            w_load(c + 2, d).start()

    def rows_grad(offsets):
        zs = [(my_z + off + NZ) % NZ for off in offsets]
        count = NX * CAP

        @pl.loop(0, feats // TILE)
        def _(j):
            at = pl.ds(pl.multiple_of(j * TILE, TILE), TILE)
            term = sum(
                lax.dot_general(
                    jnp.concatenate([cot_got[c, :, z].reshape(count, width) for z in zs], 0),
                    w_chunk[c % 2, at, :], (((1,), (1,)), ((), ())), preferred_element_type=F32,
                )
                for c in range(NC - 2, NC)
            )
            for i, z in enumerate(zs):
                total = term[i * count:(i + 1) * count].reshape(NX, CAP, TILE) + acc[:, z, :, at]
                grads[:, z, :, at] = total.astype(BF16)

        for off in offsets:
            if off == 0:
                pltpu.make_async_copy(grads.at[:, my_z], ret_z.at[my_z], rz_own).start()
            else:
                ret_z_copy(off % NZ).start()

    def pair_copy(c):
        return remote(
            partial.at[c % 2, 1 - my_core], other.at[c], pair_send.at[c], pair_recv.at[c], other_core
        )

    def rs_copy(c, k):
        return remote(
            partial.at[c % 2, my_core, (my_y + k) % NY], terms.at[c, my_y],
            rs_send.at[c, k], rs_recv.at[c, NY - k], at_y(k),
        )

    def rs_own_copy(c):
        return pltpu.make_async_copy(
            partial.at[c % 2, my_core, my_y], terms.at[c, my_y], rs_own.at[c]
        )

    def weight_sends_done(c):
        pair_copy(c).wait_send()
        for k in range(1, NY):
            rs_copy(c, k).wait_send()
        rs_own_copy(c).wait()

    def weight_grad(c):
        if c >= 2:
            weight_sends_done(c - 2)

        @pl.loop(0, width // TILE)
        def _(j):
            at = pl.ds(pl.multiple_of(j * TILE, TILE), TILE)
            term = jnp.dot(
                attn_t[...], cot_got[c, :, :, :, at].reshape(NX * NZ * CAP, TILE),
                preferred_element_type=F32,
            ).astype(BF16)
            for i in range(CORES):
                partial[c % 2, i, j] = term[:, i * cols:(i + 1) * cols]

        pair_copy(c).start()

    def weight_pair(c):
        pair_copy(c).wait_recv()

        @pl.loop(0, feats // TILE)
        def _(j):
            at = pl.ds(pl.multiple_of(j * TILE, TILE), TILE)
            for y in range(NY):
                both = partial[c % 2, my_core, y, at, :].astype(F32) + other[c, y, at, :].astype(F32)
                partial[c % 2, my_core, y, at, :] = both.astype(BF16)

        rs_own_copy(c).start()
        for k in range(1, NY):
            rs_copy(c, k).start()

    def weight_grad_sum(c):
        if c >= NC - 2:
            rs_own_copy(c).wait()
        for k in range(1, NY):
            rs_copy(c, k).wait_recv()

        @pl.loop(0, feats // TILE)
        def _(j):
            at = pl.ds(pl.multiple_of(j * TILE, TILE), TILE)
            total = terms[c, 0, at, :].astype(F32)
            for y in range(1, NY):
                total += terms[c, y, at, :].astype(F32)
            wgrad_ref[at, c * cols:(c + 1) * cols] = total.astype(BF16)

    def ret_z_copy(k):
        return remote(
            grads.at[:, (my_z + k) % NZ], ret_z.at[my_z], rz_send.at[k], rz_recv.at[NZ - k], at_z(k)
        )

    def ring_step(c, s):
        if c >= 2 and s == 0:
            wait_bytes(ring.at[c, 0], cot_in.at[c])
        if s > 0:
            ring_copy(c, s - 1, True).wait_recv()
            ring_copy(c, s - 1, False).wait_recv()
        if s < LAST and (c >= 2 or s > 0):
            ring_copy(c, s, True).start()
            ring_copy(c, s, False).start()
        if (c, s) == (0, 1):
            for k in range(1, NZ):
                dest_copy(k).wait_recv()
        if s in (0, LAST):
            deliver(c, s)
        else:
            deliver(c, -s)
            deliver(c, s)

    for c, s in ((0, 0), (1, 0), (0, 1), (1, 1), (0, 2)):
        ring_step(c, s)
    attn_along_z()
    every = range(len(SOURCES))
    for c, s in ((1, 2), (0, 3), (2, 0), (1, 3), (3, 0), (0, 4), (2, 1), (1, 4)):
        ring_step(c, s)
    arrived(0, every)
    input_grad(0)
    ring_step(3, 1)
    arrived(1, every)
    input_grad(1)
    ring_step(2, 2)
    attn_arrived()
    weight_grad(0)
    ring_step(3, 2)
    weight_grad(1)
    weight_pair(0)
    ring_step(2, 3)
    for c in range(NC - 2, NC):
        wait_bytes(w_chunk.at[c % 2], w_sem.at[c])
        arrived(c, (0,))
    rows_grad(SOURCES[0])
    ring_step(3, 3)
    weight_pair(1)
    for c in range(NC - 2, NC):
        arrived(c, (1,))
    rows_grad(SOURCES[1])
    ring_step(2, 4)
    for c in range(NC - 2, NC):
        arrived(c, (2,))
    rows_grad(SOURCES[2])
    ring_step(3, 4)
    arrived(2, (3,))
    weight_grad(2)
    arrived(3, (3,))
    rows_grad(SOURCES[3])
    weight_pair(2)
    weight_grad(3)
    weight_pair(3)
    weight_grad_sum(0)
    weight_grad_sum(1)

    def ret_x_start(z):
        for k in range(NX):
            src, dst = ret_z.at[z, (my_x + k) % NX], ret_x.at[my_x, z]
            if k == 0:
                pltpu.make_async_copy(src, dst, rx_own).start()
            else:
                remote(src, dst, rx_send.at[k], rx_recv.at[NX - k], at_x(k)).start()

    pltpu.make_async_copy(grads.at[:, my_z], ret_z.at[my_z], rz_own).wait()
    ret_x_start(my_z)
    for k in (1, 7, 2, 6, 3, 5, 4):
        ret_z_copy(k).wait_recv()
        ret_x_start((my_z - k + NZ) % NZ)
    weight_grad_sum(2)
    weight_grad_sum(3)
    for k in range(NX):
        wait_bytes(ret_x.at[k], rx_own if k == 0 else rx_recv.at[k])

    for k in range(1, NZ):
        dest_copy(k).wait_send()
        attn_z_copy(k).wait_send()
        ret_z_copy(k).wait_send()
    for k in range(1, NX):
        attn_x_copy(k).wait_send()
        wait_bytes(ret_x.at[k], rx_send.at[k])
    for c in range(NC):
        for s in range(LAST):
            ring_copy(c, s, True).wait_send()
            ring_copy(c, s, False).wait_send()
        x_sends_done(c)
    for c in range(NC - 2, NC):
        pair_copy(c).wait_send()
        for k in range(1, NY):
            rs_copy(c, k).wait_send()


def backward(mod, gm, attn, cot, w):
    tok, model = cot.shape
    width = model // NC
    feats = w.shape[0]
    dma = pltpu.SemaphoreType.DMA
    vmem = pl.BlockSpec(memory_space=pltpu.VMEM)
    hbm = pl.BlockSpec(memory_space=pl.ANY)
    return pl.pallas_call(
        kernel,
        out_shape=(
            jax.ShapeDtypeStruct((NX, NZ, CAP, feats), BF16),
            jax.ShapeDtypeStruct((8, tok), jnp.int32),
            jax.ShapeDtypeStruct((feats, model // NDP), BF16),
        ),
        in_specs=[
            vmem, pl.BlockSpec(memory_space=pltpu.SMEM), hbm, hbm, hbm,
        ],
        out_specs=(hbm, vmem, vmem),
        scratch_shapes=[
            pltpu.VMEM((tok, model), BF16),
            pltpu.VMEM((NC, NZ, tok, width), BF16),
            pltpu.VMEM((NZ, 8, tok), jnp.int32),
            pltpu.VMEM((NC, NX, NZ, CAP, width), BF16),
            pltpu.VMEM((NC, NX, NZ, CAP, width), BF16),
            pltpu.VMEM((2, feats, width), BF16),
            pltpu.VMEM((2, CORES, NY, feats, width // NDP), BF16),
            pltpu.VMEM((NC, NY, feats, width // NDP), BF16),
            pltpu.VMEM((NC, NY, feats, width // NDP), BF16),
            pltpu.VMEM((NX, NZ, CAP, feats), F32),
            pltpu.VMEM((NX, HALVES, CAP, model), BF16),
            pltpu.VMEM((NX, HALVES, CAP, model), BF16),
            pltpu.VMEM((NX, NZ, CAP, feats), BF16),
            pltpu.VMEM((feats, NX * NZ * CAP), BF16),
            pltpu.VMEM((NX, NZ, CAP, feats), BF16),
            pltpu.VMEM((NZ, NX, CAP, feats), BF16),
            dma, dma((NC,)), dma((NZ,)), dma((NZ,)),
            dma((NC, LAST)), dma((NC, LAST)), dma((NC, LAST)), dma((NC, LAST)),
            dma((NC, NX)), dma((NC, LAST, NX)), dma((NC, LAST)),
            dma((NX,)), dma((NX,)), dma,
            dma((NZ,)), dma((NZ,)), dma,
            dma((NC,)),
            dma((NC,)), dma((NC,)), dma((NC, NY)), dma((NC, NY)), dma((NC,)),
            dma((NZ,)), dma((NZ,)), dma,
            dma((NX,)), dma((NX,)), dma,
        ],
        compiler_params=pltpu.CompilerParams(
            collective_id=0, has_side_effects=True, vmem_limit_bytes=63 * 1024 * 1024
        ),
        name="moe_proj_backward",
    )(mod, gm, attn, cot, w)


def finish_kernel(
    dest_ref, ret_hbm, w_hbm, grad_hbm, w_out, ret, grad, wgrad, ret_in, grad_out, w_in, w_sent,
):
    tok, feats = dest_ref.shape[1], ret.shape[3]
    parts = w_in.shape[0]
    rows = wgrad.shape[0] // parts

    def ret_load(p, h):
        at = h * PIECES + p
        return pltpu.make_async_copy(ret_hbm.at[:, at], ret.at[:, at], ret_in.at[at])

    def w_load(k):
        at = pl.ds(k * rows, rows)
        return pltpu.make_async_copy(w_hbm.at[at], wgrad.at[at], w_in.at[k])

    def w_store(k):
        at = pl.ds(k * rows, rows)
        return pltpu.make_async_copy(wgrad.at[at], w_out.at[at], w_sent.at[k])

    def grad_store(p):
        at = pl.ds(p * feats, feats)
        return pltpu.make_async_copy(grad.at[:, at], grad_hbm.at[:, at], grad_out.at[p])

    for p in range(PIECES):
        for h in range(HALVES):
            ret_load(p, h).start()
    for k in range(parts):
        w_load(k).start()
    slots = lax.broadcasted_iota(jnp.int32, (NGROUP * CAP, tok), 0)
    back = jnp.where(slots == dest_ref[0:1, :], 1.0, 0.0).T.astype(BF16)
    for p in range(PIECES):
        for h in range(HALVES):
            ret_load(p, h).wait()
        pieces = jnp.concatenate(
            [ret[g // HALVES, (g % HALVES) * PIECES + p] for g in range(NGROUP)], 0
        )
        grad[:, p * feats:(p + 1) * feats] = jnp.dot(
            back, pieces, preferred_element_type=F32
        ).astype(BF16)
        grad_store(p).start()
        w_load(p).wait()
        w_store(p).start()
    for p in range(PIECES):
        grad_store(p).wait()
        w_store(p).wait()


def finish(ret, dest, wgrad):
    tok, feats = dest.shape[1], ret.shape[3]
    dma = pltpu.SemaphoreType.DMA((PIECES,))
    vmem = pl.BlockSpec(memory_space=pltpu.VMEM)
    hbm = pl.BlockSpec(memory_space=pl.ANY)
    return pl.pallas_call(
        finish_kernel,
        out_shape=(
            jax.ShapeDtypeStruct((tok, PIECES * feats), BF16),
            jax.ShapeDtypeStruct(wgrad.shape, BF16),
        ),
        in_specs=[vmem, hbm, hbm],
        out_specs=(hbm, hbm),
        scratch_shapes=[
            pltpu.VMEM(ret.shape, BF16),
            pltpu.VMEM((tok, PIECES * feats), BF16),
            pltpu.VMEM(wgrad.shape, BF16),
            pltpu.SemaphoreType.DMA((NZ,)), dma, dma, dma,
        ],
        name="finish",
    )(dest, ret, wgrad)


def per_device(attn_out, out_cot, modality, group_modality, o_weight):
    ret, dest, wgrad = backward(
        modality.reshape(1, -1), group_modality, attn_out, out_cot, o_weight
    )
    return finish(ret, dest, wgrad)


def solution(mesh):
    return jax.shard_map(
        per_device,
        mesh=mesh,
        in_specs=(
            P(("dp", "tower"), None),
            P(("dp", "tower"), None),
            P(("dp", "tower")),
            P(),
            P("tower", None),
        ),
        out_specs=(P(("dp", "tower"), None), P("tower", "dp")),
        check_vma=False,
    )
```

```python
import jax
import jax.numpy as jnp
from jax import lax
from jax.experimental import pallas as pl
from jax.experimental.pallas import tpu as pltpu
from jax.sharding import PartitionSpec as P

NGROUP = 8
CAP = 24
NX = 4
NZ = 8
HALVES = NGROUP // NX
PIECES = NZ // HALVES
NDP = 8
CORES = 2
NY = NDP // CORES
ORDER = (0, -1, 1, -2, 2, -3, 3, 4)
PARTS = ((0, 3), (3, 2), (5, 2), (7, 1))
NC = 4
LAST = NZ // 2
TILE = 256
PLACE = {off % NZ: at for at, off in enumerate(ORDER)}
MESH = pl.DeviceIdType.MESH
F32 = jnp.float32
BF16 = jnp.bfloat16


def kernel(
    mod_ref, gm_ref, attn_hbm, cot_hbm, w_ref, ret_x, dest_ref, wgrad_ref,
    attn_ref, ring, dests, staged, cot_got, w_chunk, partial, other, terms, acc,
    attn_own, attn_x, attn_got, attn_t, grads, ret_z,
    attn_in, cot_in, dest_send, dest_recv, right_send, right_recv, left_send, left_recv,
    x_send, x_recv, x_own, ax_send, ax_recv, ax_own, az_send, az_recv, az_own,
    w_sem, pair_send, pair_recv, rs_send, rs_recv, rs_own, rz_send, rz_recv, rz_own, rx_send, rx_recv, rx_own,
):
    tok = cot_hbm.shape[0]
    width = cot_hbm.shape[1] // NC
    cols = width // NDP
    own_cols = wgrad_ref.shape[1]
    feats = w_ref.shape[0]
    half = width // 2
    me, my_d = lax.axis_index("tower"), lax.axis_index("dp")
    my_x, my_z = me // NZ, me % NZ
    my_half = my_z // PIECES
    my_y, my_core = my_d // CORES, my_d % CORES

    def at_z(k):
        return {"tower": my_x * NZ + (my_z + k + NZ) % NZ}

    def at_x(k):
        return {"tower": ((my_x + k) % NX) * NZ + my_z}

    def at_y(k):
        return {"dp": ((my_y + k) % NY) * CORES + my_core}

    other_core = {"dp": my_y * CORES + 1 - my_core}

    def remote(src, dst, send, recv, device):
        return pltpu.make_async_remote_copy(
            src_ref=src, dst_ref=dst, send_sem=send, recv_sem=recv,
            device_id=device, device_id_type=MESH,
        )

    def wait_bytes(ref, sem):
        pltpu.make_async_copy(ref, ref, sem).wait()

    def w_load(c, d):
        return pltpu.make_async_copy(
            w_ref.at[:, pl.ds(d * own_cols + c * cols, cols)],
            w_chunk.at[c % 2, :, pl.ds(d * cols, cols)],
            w_sem.at[c],
        )

    def own_block(c):
        for d in range(NDP):
            pltpu.make_async_copy(
                cot_hbm.at[:, pl.ds(d * own_cols + c * cols, cols)],
                ring.at[c, 0, :, pl.ds(d * cols, cols)],
                cot_in.at[c],
            ).start()

    attn_load = pltpu.make_async_copy(attn_hbm, attn_ref, attn_in)
    barrier = pltpu.get_barrier_semaphore()
    for k in range(1, NZ):
        pl.semaphore_signal(barrier, inc=1, device_id=at_z(k), device_id_type=MESH)
    for k in range(1, NX):
        pl.semaphore_signal(barrier, inc=1, device_id=at_x(k), device_id_type=MESH)
    for k in range(1, NY):
        pl.semaphore_signal(barrier, inc=1, device_id=at_y(k), device_id_type=MESH)
    pl.semaphore_signal(barrier, inc=1, device_id=other_core, device_id_type=MESH)

    own_block(0)
    own_block(1)
    attn_load.start()
    pl.semaphore_wait(barrier, NZ - 1 + NX - 1 + NY)

    def ring_copy(c, s, right):
        off = -s if right else s
        src = ring.at[c, off % NZ]
        dst = ring.at[c, (off - 1 if right else off + 1) % NZ]
        if s == LAST - 1:
            part = pl.ds(0, half) if right else pl.ds(half, half)
            src, dst = src.at[:, part], dst.at[:, part]
        return remote(
            src, dst,
            (right_send if right else left_send).at[c, s],
            (right_recv if right else left_recv).at[c, s],
            at_z(1 if right else -1),
        )

    for c in range(2):
        wait_bytes(ring.at[c, 0], cot_in.at[c])
        ring_copy(c, 0, True).start()
        ring_copy(c, 0, False).start()
    for c in range(2, NC):
        own_block(c)
    for c in range(2):
        for d in range(NDP):
            w_load(c, d).start()

    mod = jnp.broadcast_to(mod_ref[...], (8, tok))
    kinds = [(mod == m).astype(F32) for m in range(3)]
    t_from = lax.broadcasted_iota(jnp.int32, (tok, tok), 0)
    t_to = lax.broadcasted_iota(jnp.int32, (tok, tok), 1)
    earlier = (t_from < t_to).astype(F32).astype(BF16)
    before = jnp.dot(jnp.concatenate(kinds, 0).astype(BF16), earlier, preferred_element_type=F32)
    order = sum(before[8 * m:8 * m + 8] * kinds[m] for m in range(3))
    serves = [gm_ref[g] for g in range(NGROUP)]
    how_many = jnp.ones_like(mod)
    for m in range(3):
        count = sum((s == m).astype(jnp.int32) for s in serves)
        how_many = jnp.where(mod == m, count, how_many)
    per = how_many.astype(F32)
    turn = (order.astype(jnp.int32) + me).astype(F32)
    target = (turn - jnp.floor((turn + 0.5) / per) * per).astype(jnp.int32)
    routed = jnp.zeros_like(mod)
    for g in range(NGROUP):
        rank = sum(((s == serves[g]).astype(jnp.int32) for s in serves[:g]), jnp.int32(0))
        routed = jnp.where((mod == serves[g]) & (target == rank), g, routed)
    dest = routed * CAP + jnp.floor((order + 0.5) / per).astype(jnp.int32)
    dests[0] = dest
    dest_ref[...] = dest

    def dest_copy(k):
        return remote(dests.at[0], dests.at[NZ - k], dest_send.at[k], dest_recv.at[NZ - k], at_z(k))

    for k in range(1, NZ):
        dest_copy(k).start()

    slots = lax.broadcasted_iota(jnp.int32, (NGROUP * CAP, tok), 0)
    attn_load.wait()
    pick_own = jnp.where(slots == dest[0:1], 1.0, 0.0).astype(BF16)
    for p in range(PIECES):
        got = jnp.dot(pick_own, attn_ref[:, p * feats:(p + 1) * feats], preferred_element_type=F32)
        attn_own[:, :, :, p * feats:(p + 1) * feats] = got.astype(BF16).reshape(NX, HALVES, CAP, feats)

    def attn_x_copy(k):
        return remote(
            attn_own.at[(my_x + k) % NX], attn_x.at[my_x], ax_send.at[k], ax_recv.at[NX - k], at_x(k)
        )

    own_ax = pltpu.make_async_copy(attn_own.at[my_x], attn_x.at[my_x], ax_own)
    own_ax.start()
    for k in range(1, NX):
        attn_x_copy(k).start()

    def attn_z_src(k):
        z = (my_z + k) % NZ
        start = pl.multiple_of((z % PIECES) * feats, feats)
        return attn_x.at[:, z // PIECES, :, pl.ds(start, feats)]

    def attn_z_copy(k):
        return remote(
            attn_z_src(k), attn_got.at[:, PLACE[NZ - k]], az_send.at[k], az_recv.at[NZ - k], at_z(k)
        )

    def attn_along_z():
        own_ax.wait()
        for k in range(1, NX):
            attn_x_copy(k).wait_recv()
        pltpu.make_async_copy(attn_z_src(0), attn_got.at[:, 0], az_own).start()
        for k in range(1, NZ):
            attn_z_copy(k).start()

    def attn_arrived():
        pltpu.make_async_copy(attn_z_src(0), attn_got.at[:, 0], az_own).wait()
        for k in range(1, NZ):
            attn_z_copy(k).wait_recv()

        @pl.loop(0, feats // TILE)
        def _(j):
            at = pl.ds(pl.multiple_of(j * TILE, TILE), TILE)
            attn_t[at, :] = jnp.transpose(attn_got[:, :, :, at].reshape(NX * NZ * CAP, TILE))

    rows = lax.broadcasted_iota(jnp.int32, (NX * CAP, tok), 0)
    x_of = sum((rows >= CAP * k).astype(jnp.int32) for k in range(1, NX))
    wanted = rows + CAP * (HALVES - 1) * x_of + CAP * my_half

    def deliver(c, *offsets):
        at = pl.ds(PLACE[offsets[0] % NZ], len(offsets))
        for off in offsets:
            slot = off % NZ
            pick = jnp.where(wanted == dests[slot, 0:1, :], 1.0, 0.0).astype(BF16)
            got = jnp.dot(pick, ring[c, slot], preferred_element_type=F32).astype(BF16)
            for x in range(NX):
                staged[c, x, PLACE[slot]] = got[x * CAP:(x + 1) * CAP]
        part = max(abs(offsets[0]), 1) - 1
        lands = cot_got.at[c, my_x, at]
        for k in range(1, NX):
            src = staged.at[c, (my_x + k) % NX, at]
            remote(src, lands, x_send.at[c, k], x_recv.at[c, part, NX - k], at_x(k)).start()
        pltpu.make_async_copy(staged.at[c, my_x, at], lands, x_own.at[c, part]).start()

    def arrived(c, parts):
        for part in parts:
            count = PARTS[part][1]
            wait_bytes(staged.at[c, 0, pl.ds(0, count)], x_own.at[c, part])
            for k in range(1, NX):
                wait_bytes(staged.at[c, k, pl.ds(0, count)], x_recv.at[c, part, k])

    def x_sends_done(c):
        for k in range(1, NX):
            wait_bytes(staged.at[c, k], x_send.at[c, k])

    def input_grad(c):
        wait_bytes(w_chunk.at[c % 2], w_sem.at[c])

        @pl.loop(0, feats // TILE)
        def _(j):
            at = pl.ds(pl.multiple_of(j * TILE, TILE), TILE)
            term = lax.dot_general(
                cot_got[c].reshape(NX * NZ * CAP, width), w_chunk[c % 2, at, :],
                (((1,), (1,)), ((), ())), preferred_element_type=F32,
            )
            term = term.reshape(NX, NZ, CAP, TILE)
            acc[:, :, :, at] = term if c == 0 else acc[:, :, :, at] + term

        for d in range(NDP):
            w_load(c + 2, d).start()

    def rows_grad(part):
        first, count = PARTS[part]
        own = slice(first, first + count)

        @pl.loop(0, feats // TILE)
        def _(j):
            at = pl.ds(pl.multiple_of(j * TILE, TILE), TILE)
            term = sum(
                lax.dot_general(
                    cot_got[c, :, own].reshape(NX * count * CAP, width), w_chunk[c % 2, at, :],
                    (((1,), (1,)), ((), ())), preferred_element_type=F32,
                )
                for c in range(NC - 2, NC)
            )
            total = term.reshape(NX, count, CAP, TILE) + acc[:, own, :, at]
            grads[:, own, :, at] = total.astype(BF16)

        for off in ORDER[own]:
            if off == 0:
                pltpu.make_async_copy(grads.at[:, 0], ret_z.at[my_z], rz_own).start()
            else:
                ret_z_copy(off % NZ).start()

    def pair_copy(c):
        return remote(
            partial.at[c % 2, 1 - my_core], other.at[c], pair_send.at[c], pair_recv.at[c], other_core
        )

    def rs_copy(c, k):
        return remote(
            partial.at[c % 2, my_core, (my_y + k) % NY], terms.at[c, my_y],
            rs_send.at[c, k], rs_recv.at[c, NY - k], at_y(k),
        )

    def rs_own_copy(c):
        return pltpu.make_async_copy(
            partial.at[c % 2, my_core, my_y], terms.at[c, my_y], rs_own.at[c]
        )

    def weight_sends_done(c):
        pair_copy(c).wait_send()
        for k in range(1, NY):
            rs_copy(c, k).wait_send()
        rs_own_copy(c).wait()

    def weight_grad(c):
        if c >= 2:
            weight_sends_done(c - 2)

        @pl.loop(0, width // TILE)
        def _(j):
            at = pl.ds(pl.multiple_of(j * TILE, TILE), TILE)
            term = jnp.dot(
                attn_t[...], cot_got[c, :, :, :, at].reshape(NX * NZ * CAP, TILE),
                preferred_element_type=F32,
            ).astype(BF16)
            for i in range(CORES):
                partial[c % 2, i, j] = term[:, i * cols:(i + 1) * cols]

        pair_copy(c).start()

    def weight_pair(c):
        pair_copy(c).wait_recv()

        @pl.loop(0, feats // TILE)
        def _(j):
            at = pl.ds(pl.multiple_of(j * TILE, TILE), TILE)
            for y in range(NY):
                both = partial[c % 2, my_core, y, at, :].astype(F32) + other[c, y, at, :].astype(F32)
                partial[c % 2, my_core, y, at, :] = both.astype(BF16)

        rs_own_copy(c).start()
        for k in range(1, NY):
            rs_copy(c, k).start()

    def weight_grad_sum(c):
        if c >= NC - 2:
            rs_own_copy(c).wait()
        for k in range(1, NY):
            rs_copy(c, k).wait_recv()

        @pl.loop(0, feats // TILE)
        def _(j):
            at = pl.ds(pl.multiple_of(j * TILE, TILE), TILE)
            total = terms[c, 0, at, :].astype(F32)
            for y in range(1, NY):
                total += terms[c, y, at, :].astype(F32)
            wgrad_ref[at, c * cols:(c + 1) * cols] = total.astype(BF16)

    def ret_z_copy(k):
        return remote(
            grads.at[:, PLACE[k]], ret_z.at[my_z], rz_send.at[k], rz_recv.at[NZ - k], at_z(k)
        )

    def ring_step(c, s):
        if c >= 2 and s == 0:
            wait_bytes(ring.at[c, 0], cot_in.at[c])
        for right in (True, False):
            if s > 0:
                ring_copy(c, s - 1, right).wait_recv()
            if s < LAST and (c >= 2 or s > 0):
                ring_copy(c, s, right).start()
        if (c, s) == (0, 1):
            for k in range(1, NZ):
                dest_copy(k).wait_recv()
        if s in (0, LAST):
            deliver(c, s)
        else:
            deliver(c, -s, s)

    for c, s in ((0, 0), (1, 0), (0, 1), (1, 1), (0, 2)):
        ring_step(c, s)
    attn_along_z()
    every = range(len(PARTS))
    for c, s in ((1, 2), (0, 3), (2, 0), (1, 3), (3, 0), (0, 4), (2, 1), (1, 4)):
        ring_step(c, s)
    arrived(0, every)
    input_grad(0)
    ring_step(3, 1)
    arrived(1, every)
    input_grad(1)
    ring_step(2, 2)
    attn_arrived()
    weight_grad(0)
    ring_step(3, 2)
    weight_grad(1)
    weight_pair(0)
    ring_step(2, 3)
    for c in range(NC - 2, NC):
        wait_bytes(w_chunk.at[c % 2], w_sem.at[c])
        arrived(c, (0,))
    rows_grad(0)
    ring_step(3, 3)
    weight_pair(1)
    for c in range(NC - 2, NC):
        arrived(c, (1,))
    rows_grad(1)
    ring_step(2, 4)
    for c in range(NC - 2, NC):
        arrived(c, (2,))
    rows_grad(2)
    ring_step(3, 4)
    arrived(2, (3,))
    weight_grad(2)
    arrived(3, (3,))
    rows_grad(3)
    weight_pair(2)
    weight_grad(3)
    weight_pair(3)
    weight_grad_sum(0)
    weight_grad_sum(1)

    def ret_x_start(z):
        for k in range(NX):
            src, dst = ret_z.at[z, (my_x + k) % NX], ret_x.at[my_x, z]
            if k == 0:
                pltpu.make_async_copy(src, dst, rx_own).start()
            else:
                remote(src, dst, rx_send.at[k], rx_recv.at[NX - k], at_x(k)).start()

    pltpu.make_async_copy(grads.at[:, 0], ret_z.at[my_z], rz_own).wait()
    ret_x_start(my_z)
    for k in (1, 7, 2, 6, 3, 5, 4):
        ret_z_copy(k).wait_recv()
        ret_x_start((my_z - k + NZ) % NZ)
    weight_grad_sum(2)
    weight_grad_sum(3)
    for k in range(NX):
        wait_bytes(ret_x.at[k], rx_own if k == 0 else rx_recv.at[k])

    for k in range(1, NZ):
        dest_copy(k).wait_send()
        attn_z_copy(k).wait_send()
        ret_z_copy(k).wait_send()
    for k in range(1, NX):
        attn_x_copy(k).wait_send()
        wait_bytes(ret_x.at[k], rx_send.at[k])
    for c in range(NC):
        for s in range(LAST):
            ring_copy(c, s, True).wait_send()
            ring_copy(c, s, False).wait_send()
        x_sends_done(c)
    for c in range(NC - 2, NC):
        pair_copy(c).wait_send()
        for k in range(1, NY):
            rs_copy(c, k).wait_send()


def backward(mod, gm, attn, cot, w):
    tok, model = cot.shape
    width = model // NC
    feats = w.shape[0]
    dma = pltpu.SemaphoreType.DMA
    vmem = pl.BlockSpec(memory_space=pltpu.VMEM)
    hbm = pl.BlockSpec(memory_space=pl.ANY)
    return pl.pallas_call(
        kernel,
        out_shape=(
            jax.ShapeDtypeStruct((NX, NZ, CAP, feats), BF16),
            jax.ShapeDtypeStruct((8, tok), jnp.int32),
            jax.ShapeDtypeStruct((feats, model // NDP), BF16),
        ),
        in_specs=[
            vmem, pl.BlockSpec(memory_space=pltpu.SMEM), hbm, hbm, hbm,
        ],
        out_specs=(hbm, vmem, vmem),
        scratch_shapes=[
            pltpu.VMEM((tok, model), BF16),
            pltpu.VMEM((NC, NZ, tok, width), BF16),
            pltpu.VMEM((NZ, 8, tok), jnp.int32),
            pltpu.VMEM((NC, NX, NZ, CAP, width), BF16),
            pltpu.VMEM((NC, NX, NZ, CAP, width), BF16),
            pltpu.VMEM((2, feats, width), BF16),
            pltpu.VMEM((2, CORES, NY, feats, width // NDP), BF16),
            pltpu.VMEM((NC, NY, feats, width // NDP), BF16),
            pltpu.VMEM((NC, NY, feats, width // NDP), BF16),
            pltpu.VMEM((NX, NZ, CAP, feats), F32),
            pltpu.VMEM((NX, HALVES, CAP, model), BF16),
            pltpu.VMEM((NX, HALVES, CAP, model), BF16),
            pltpu.VMEM((NX, NZ, CAP, feats), BF16),
            pltpu.VMEM((feats, NX * NZ * CAP), BF16),
            pltpu.VMEM((NX, NZ, CAP, feats), BF16),
            pltpu.VMEM((NZ, NX, CAP, feats), BF16),
            dma, dma((NC,)), dma((NZ,)), dma((NZ,)),
            dma((NC, LAST)), dma((NC, LAST)), dma((NC, LAST)), dma((NC, LAST)),
            dma((NC, NX)), dma((NC, LAST, NX)), dma((NC, LAST)),
            dma((NX,)), dma((NX,)), dma,
            dma((NZ,)), dma((NZ,)), dma,
            dma((NC,)),
            dma((NC,)), dma((NC,)), dma((NC, NY)), dma((NC, NY)), dma((NC,)),
            dma((NZ,)), dma((NZ,)), dma,
            dma((NX,)), dma((NX,)), dma,
        ],
        compiler_params=pltpu.CompilerParams(
            collective_id=0, has_side_effects=True, vmem_limit_bytes=63 * 1024 * 1024
        ),
        name="moe_proj_backward",
    )(mod, gm, attn, cot, w)


def finish_kernel(
    dest_ref, ret_hbm, w_hbm, grad_hbm, w_out, ret, grad, wgrad, ret_in, grad_out, w_in, w_sent,
):
    tok, feats = dest_ref.shape[1], ret.shape[3]
    parts = w_in.shape[0]
    rows = wgrad.shape[0] // parts

    def ret_load(p, h):
        at = h * PIECES + p
        return pltpu.make_async_copy(ret_hbm.at[:, at], ret.at[:, at], ret_in.at[at])

    def w_load(k):
        at = pl.ds(k * rows, rows)
        return pltpu.make_async_copy(w_hbm.at[at], wgrad.at[at], w_in.at[k])

    def w_store(k):
        at = pl.ds(k * rows, rows)
        return pltpu.make_async_copy(wgrad.at[at], w_out.at[at], w_sent.at[k])

    def grad_store(p):
        at = pl.ds(p * feats, feats)
        return pltpu.make_async_copy(grad.at[:, at], grad_hbm.at[:, at], grad_out.at[p])

    for p in range(PIECES):
        for h in range(HALVES):
            ret_load(p, h).start()
    for k in range(parts):
        w_load(k).start()
    slots = lax.broadcasted_iota(jnp.int32, (NGROUP * CAP, tok), 0)
    back = jnp.where(slots == dest_ref[0:1, :], 1.0, 0.0).T.astype(BF16)
    for p in range(PIECES):
        for h in range(HALVES):
            ret_load(p, h).wait()
        pieces = jnp.concatenate(
            [ret[g // HALVES, (g % HALVES) * PIECES + p] for g in range(NGROUP)], 0
        )
        grad[:, p * feats:(p + 1) * feats] = jnp.dot(
            back, pieces, preferred_element_type=F32
        ).astype(BF16)
        grad_store(p).start()
        w_load(p).wait()
        w_store(p).start()
    for p in range(PIECES):
        grad_store(p).wait()
        w_store(p).wait()


def finish(ret, dest, wgrad):
    tok, feats = dest.shape[1], ret.shape[3]
    dma = pltpu.SemaphoreType.DMA((PIECES,))
    vmem = pl.BlockSpec(memory_space=pltpu.VMEM)
    hbm = pl.BlockSpec(memory_space=pl.ANY)
    return pl.pallas_call(
        finish_kernel,
        out_shape=(
            jax.ShapeDtypeStruct((tok, PIECES * feats), BF16),
            jax.ShapeDtypeStruct(wgrad.shape, BF16),
        ),
        in_specs=[vmem, hbm, hbm],
        out_specs=(hbm, hbm),
        scratch_shapes=[
            pltpu.VMEM(ret.shape, BF16),
            pltpu.VMEM((tok, PIECES * feats), BF16),
            pltpu.VMEM(wgrad.shape, BF16),
            pltpu.SemaphoreType.DMA((NZ,)), dma, dma, dma,
        ],
        name="finish",
    )(dest, ret, wgrad)


def per_device(attn_out, out_cot, modality, group_modality, o_weight):
    ret, dest, wgrad = backward(
        modality.reshape(1, -1), group_modality, attn_out, out_cot, o_weight
    )
    return finish(ret, dest, wgrad)


def solution(mesh):
    return jax.shard_map(
        per_device,
        mesh=mesh,
        in_specs=(
            P(("dp", "tower"), None),
            P(("dp", "tower"), None),
            P(("dp", "tower")),
            P(),
            P("tower", None),
        ),
        out_specs=(P(("dp", "tower"), None), P("tower", "dp")),
        check_vma=False,
    )
```

```python
import jax
import jax.numpy as jnp
from jax import lax
from jax.experimental import pallas as pl
from jax.experimental.pallas import tpu as pltpu
from jax.sharding import PartitionSpec as P

NGROUP = 8
CAP = 24
NX = 4
NZ = 8
HALVES = NGROUP // NX
PIECES = NZ // HALVES
NDP = 8
CORES = 2
NY = NDP // CORES
ORDER = (0, -1, 1, -2, 2, -3, 3, 4)
PARTS = ((0, 3), (3, 2), (5, 2), (7, 1))
NC = 4
LAST = NZ // 2
TILE = 256
PLACE = {off % NZ: at for at, off in enumerate(ORDER)}
MESH = pl.DeviceIdType.MESH
F32 = jnp.float32
BF16 = jnp.bfloat16


def kernel(
    mod_ref, gm_ref, attn_hbm, cot_hbm, w_ref, ret_x, dest_ref, wgrad_ref,
    attn_ref, ring, dests, staged, cot_got, w_chunk, partial, other, terms, acc,
    attn_own, attn_x, attn_got, attn_t, grads, ret_z,
    attn_in, cot_in, dest_send, dest_recv, right_send, right_recv, left_send, left_recv,
    x_send, x_recv, x_own, ax_send, ax_recv, ax_own, az_send, az_recv, az_own,
    w_sem, pair_send, pair_recv, rs_send, rs_recv, rs_own, rz_send, rz_recv, rz_own, rx_send, rx_recv, rx_own,
):
    tok = cot_hbm.shape[0]
    width = cot_hbm.shape[1] // NC
    cols = width // NDP
    own_cols = wgrad_ref.shape[1]
    feats = w_ref.shape[0]
    half = width // 2
    me, my_d = lax.axis_index("tower"), lax.axis_index("dp")
    my_x, my_z = me // NZ, me % NZ
    my_half = my_z // PIECES
    my_y, my_core = my_d // CORES, my_d % CORES

    def at_z(k):
        return {"tower": my_x * NZ + (my_z + k + NZ) % NZ}

    def at_x(k):
        return {"tower": ((my_x + k) % NX) * NZ + my_z}

    def at_y(k):
        return {"dp": ((my_y + k) % NY) * CORES + my_core}

    other_core = {"dp": my_y * CORES + 1 - my_core}

    def remote(src, dst, send, recv, device):
        return pltpu.make_async_remote_copy(
            src_ref=src, dst_ref=dst, send_sem=send, recv_sem=recv,
            device_id=device, device_id_type=MESH,
        )

    def wait_bytes(ref, sem):
        pltpu.make_async_copy(ref, ref, sem).wait()

    def w_load(c, d):
        return pltpu.make_async_copy(
            w_ref.at[:, pl.ds(d * own_cols + c * cols, cols)],
            w_chunk.at[c % 2, :, pl.ds(d * cols, cols)],
            w_sem.at[c],
        )

    def own_block(c):
        for d in range(NDP):
            pltpu.make_async_copy(
                cot_hbm.at[:, pl.ds(d * own_cols + c * cols, cols)],
                ring.at[c, 0, :, pl.ds(d * cols, cols)],
                cot_in.at[c],
            ).start()

    attn_load = pltpu.make_async_copy(attn_hbm, attn_ref, attn_in)
    barrier = pltpu.get_barrier_semaphore()
    for k in range(1, NZ):
        pl.semaphore_signal(barrier, inc=1, device_id=at_z(k), device_id_type=MESH)
    for k in range(1, NX):
        pl.semaphore_signal(barrier, inc=1, device_id=at_x(k), device_id_type=MESH)
    for k in range(1, NY):
        pl.semaphore_signal(barrier, inc=1, device_id=at_y(k), device_id_type=MESH)
    pl.semaphore_signal(barrier, inc=1, device_id=other_core, device_id_type=MESH)

    own_block(0)
    own_block(1)
    attn_load.start()
    pl.semaphore_wait(barrier, NZ - 1 + NX - 1 + NY)

    def ring_copy(c, s, right):
        off = -s if right else s
        src = ring.at[c, off % NZ]
        dst = ring.at[c, (off - 1 if right else off + 1) % NZ]
        if s == LAST - 1:
            part = pl.ds(0, half) if right else pl.ds(half, half)
            src, dst = src.at[:, part], dst.at[:, part]
        return remote(
            src, dst,
            (right_send if right else left_send).at[c, s],
            (right_recv if right else left_recv).at[c, s],
            at_z(1 if right else -1),
        )

    for c in range(2):
        wait_bytes(ring.at[c, 0], cot_in.at[c])
        ring_copy(c, 0, True).start()
        ring_copy(c, 0, False).start()
    for c in range(2, NC):
        own_block(c)
    for c in range(2):
        for d in range(NDP):
            w_load(c, d).start()

    mod = jnp.broadcast_to(mod_ref[...], (8, tok))
    kinds = [(mod == m).astype(F32) for m in range(3)]
    t_from = lax.broadcasted_iota(jnp.int32, (tok, tok), 0)
    t_to = lax.broadcasted_iota(jnp.int32, (tok, tok), 1)
    earlier = (t_from < t_to).astype(F32).astype(BF16)
    before = jnp.dot(jnp.concatenate(kinds, 0).astype(BF16), earlier, preferred_element_type=F32)
    order = sum(before[8 * m:8 * m + 8] * kinds[m] for m in range(3))
    serves = [gm_ref[g] for g in range(NGROUP)]
    how_many = jnp.ones_like(mod)
    for m in range(3):
        count = sum((s == m).astype(jnp.int32) for s in serves)
        how_many = jnp.where(mod == m, count, how_many)
    per = how_many.astype(F32)
    turn = (order.astype(jnp.int32) + me).astype(F32)
    target = (turn - jnp.floor((turn + 0.5) / per) * per).astype(jnp.int32)
    routed = jnp.zeros_like(mod)
    for g in range(NGROUP):
        rank = sum(((s == serves[g]).astype(jnp.int32) for s in serves[:g]), jnp.int32(0))
        routed = jnp.where((mod == serves[g]) & (target == rank), g, routed)
    dest = routed * CAP + jnp.floor((order + 0.5) / per).astype(jnp.int32)
    dests[0] = dest
    dest_ref[...] = dest

    def dest_copy(k):
        return remote(dests.at[0], dests.at[NZ - k], dest_send.at[k], dest_recv.at[NZ - k], at_z(k))

    for k in range(1, NZ):
        dest_copy(k).start()

    slots = lax.broadcasted_iota(jnp.int32, (NGROUP * CAP, tok), 0)
    attn_load.wait()
    pick_own = jnp.where(slots == dest[0:1], 1.0, 0.0).astype(BF16)
    for p in range(PIECES):
        got = jnp.dot(pick_own, attn_ref[:, p * feats:(p + 1) * feats], preferred_element_type=F32)
        attn_own[:, :, :, p * feats:(p + 1) * feats] = got.astype(BF16).reshape(NX, HALVES, CAP, feats)

    def attn_x_copy(k):
        return remote(
            attn_own.at[(my_x + k) % NX], attn_x.at[my_x], ax_send.at[k], ax_recv.at[NX - k], at_x(k)
        )

    own_ax = pltpu.make_async_copy(attn_own.at[my_x], attn_x.at[my_x], ax_own)
    own_ax.start()
    for k in range(1, NX):
        attn_x_copy(k).start()

    def attn_z_src(k):
        z = (my_z + k) % NZ
        start = pl.multiple_of((z % PIECES) * feats, feats)
        return attn_x.at[:, z // PIECES, :, pl.ds(start, feats)]

    def attn_z_copy(k):
        return remote(
            attn_z_src(k), attn_got.at[:, PLACE[NZ - k]], az_send.at[k], az_recv.at[NZ - k], at_z(k)
        )

    def attn_along_z():
        own_ax.wait()
        for k in range(1, NX):
            attn_x_copy(k).wait_recv()
        pltpu.make_async_copy(attn_z_src(0), attn_got.at[:, 0], az_own).start()
        for k in range(1, NZ):
            attn_z_copy(k).start()

    def attn_arrived():
        pltpu.make_async_copy(attn_z_src(0), attn_got.at[:, 0], az_own).wait()
        for k in range(1, NZ):
            attn_z_copy(k).wait_recv()

        @pl.loop(0, feats // TILE)
        def _(j):
            at = pl.ds(pl.multiple_of(j * TILE, TILE), TILE)
            attn_t[at, :] = jnp.transpose(attn_got[:, :, :, at].reshape(NX * NZ * CAP, TILE))

    rows = lax.broadcasted_iota(jnp.int32, (NX * CAP, tok), 0)
    x_of = sum((rows >= CAP * k).astype(jnp.int32) for k in range(1, NX))
    wanted = rows + CAP * (HALVES - 1) * x_of + CAP * my_half

    def deliver(c, *offsets):
        at = pl.ds(PLACE[offsets[0] % NZ], len(offsets))
        for off in offsets:
            slot = off % NZ
            pick = jnp.where(wanted == dests[slot, 0:1, :], 1.0, 0.0).astype(BF16)
            got = jnp.dot(pick, ring[c, slot], preferred_element_type=F32).astype(BF16)
            for x in range(NX):
                staged[c, x, PLACE[slot]] = got[x * CAP:(x + 1) * CAP]
        part = max(abs(offsets[0]), 1) - 1
        lands = cot_got.at[c, my_x, at]
        for k in range(1, NX):
            src = staged.at[c, (my_x + k) % NX, at]
            remote(src, lands, x_send.at[c, k], x_recv.at[c, part, NX - k], at_x(k)).start()
        pltpu.make_async_copy(staged.at[c, my_x, at], lands, x_own.at[c, part]).start()

    def arrived(c, parts):
        for part in parts:
            count = PARTS[part][1]
            wait_bytes(staged.at[c, 0, pl.ds(0, count)], x_own.at[c, part])
            for k in range(1, NX):
                wait_bytes(staged.at[c, k, pl.ds(0, count)], x_recv.at[c, part, k])

    def x_sends_done(c):
        for k in range(1, NX):
            wait_bytes(staged.at[c, k], x_send.at[c, k])

    def input_grad(c):
        wait_bytes(w_chunk.at[c % 2], w_sem.at[c])

        @pl.loop(0, feats // TILE)
        def _(j):
            at = pl.ds(pl.multiple_of(j * TILE, TILE), TILE)
            term = lax.dot_general(
                cot_got[c].reshape(NX * NZ * CAP, width), w_chunk[c % 2, at, :],
                (((1,), (1,)), ((), ())), preferred_element_type=F32,
            )
            term = term.reshape(NX, NZ, CAP, TILE)
            acc[:, :, :, at] = term if c == 0 else acc[:, :, :, at] + term

        for d in range(NDP):
            w_load(c + 2, d).start()

    def rows_grad(part):
        first, count = PARTS[part]
        own = slice(first, first + count)

        @pl.loop(0, feats // TILE)
        def _(j):
            at = pl.ds(pl.multiple_of(j * TILE, TILE), TILE)
            term = sum(
                lax.dot_general(
                    cot_got[c, :, own].reshape(NX * count * CAP, width), w_chunk[c % 2, at, :],
                    (((1,), (1,)), ((), ())), preferred_element_type=F32,
                )
                for c in range(NC - 2, NC)
            )
            total = term.reshape(NX, count, CAP, TILE) + acc[:, own, :, at]
            grads[:, own, :, at] = total.astype(BF16)

        for off in ORDER[own]:
            if off == 0:
                pltpu.make_async_copy(grads.at[:, 0], ret_z.at[my_z], rz_own).start()
            else:
                ret_z_copy(off % NZ).start()

    def pair_copy(c):
        return remote(
            partial.at[c % 2, 1 - my_core], other.at[c], pair_send.at[c], pair_recv.at[c], other_core
        )

    def rs_copy(c, k):
        return remote(
            partial.at[c % 2, my_core, (my_y + k) % NY], terms.at[c, my_y],
            rs_send.at[c, k], rs_recv.at[c, NY - k], at_y(k),
        )

    def rs_own_copy(c):
        return pltpu.make_async_copy(
            partial.at[c % 2, my_core, my_y], terms.at[c, my_y], rs_own.at[c]
        )

    def weight_sends_done(c):
        pair_copy(c).wait_send()
        for k in range(1, NY):
            rs_copy(c, k).wait_send()
        rs_own_copy(c).wait()

    def weight_grad(c):
        if c >= 2:
            weight_sends_done(c - 2)

        @pl.loop(0, width // TILE)
        def _(j):
            at = pl.ds(pl.multiple_of(j * TILE, TILE), TILE)
            term = jnp.dot(
                attn_t[...], cot_got[c, :, :, :, at].reshape(NX * NZ * CAP, TILE),
                preferred_element_type=F32,
            ).astype(BF16)
            for i in range(CORES):
                partial[c % 2, i, j] = term[:, i * cols:(i + 1) * cols]

        pair_copy(c).start()

    def weight_pair(c):
        pair_copy(c).wait_recv()

        @pl.loop(0, feats // TILE)
        def _(j):
            at = pl.ds(pl.multiple_of(j * TILE, TILE), TILE)
            for y in range(NY):
                both = partial[c % 2, my_core, y, at, :].astype(F32) + other[c, y, at, :].astype(F32)
                partial[c % 2, my_core, y, at, :] = both.astype(BF16)

        rs_own_copy(c).start()
        for k in range(1, NY):
            rs_copy(c, k).start()

    def weight_grad_sum(c):
        if c >= NC - 2:
            rs_own_copy(c).wait()
        for k in range(1, NY):
            rs_copy(c, k).wait_recv()

        @pl.loop(0, feats // TILE)
        def _(j):
            at = pl.ds(pl.multiple_of(j * TILE, TILE), TILE)
            total = terms[c, 0, at, :].astype(F32)
            for y in range(1, NY):
                total += terms[c, y, at, :].astype(F32)
            wgrad_ref[at, c * cols:(c + 1) * cols] = total.astype(BF16)

    def ret_z_copy(k):
        return remote(
            grads.at[:, PLACE[k]], ret_z.at[my_z], rz_send.at[k], rz_recv.at[NZ - k], at_z(k)
        )

    def ring_step(c, s):
        if c >= 2 and s == 0:
            wait_bytes(ring.at[c, 0], cot_in.at[c])
        for right in (True, False):
            if s > 0:
                ring_copy(c, s - 1, right).wait_recv()
            if s < LAST and (c >= 2 or s > 0):
                ring_copy(c, s, right).start()
        if (c, s) == (0, 1):
            for k in range(1, NZ):
                dest_copy(k).wait_recv()
        if s in (0, LAST):
            deliver(c, s)
        else:
            deliver(c, -s, s)

    for c, s in ((0, 0), (1, 0), (0, 1), (1, 1), (0, 2)):
        ring_step(c, s)
    attn_along_z()
    every = range(len(PARTS))
    for c, s in ((1, 2), (0, 3), (2, 0), (1, 3), (3, 0), (0, 4), (2, 1), (1, 4)):
        ring_step(c, s)
    arrived(0, every)
    input_grad(0)
    ring_step(3, 1)
    arrived(1, every)
    input_grad(1)
    ring_step(2, 2)
    attn_arrived()
    weight_grad(0)
    ring_step(3, 2)
    weight_grad(1)
    weight_pair(0)
    ring_step(2, 3)
    for c in range(NC - 2, NC):
        wait_bytes(w_chunk.at[c % 2], w_sem.at[c])
        arrived(c, (0,))
    rows_grad(0)
    ring_step(3, 3)
    weight_pair(1)
    for c in range(NC - 2, NC):
        arrived(c, (1,))
    rows_grad(1)
    ring_step(2, 4)
    for c in range(NC - 2, NC):
        arrived(c, (2,))
    rows_grad(2)
    ring_step(3, 4)
    arrived(2, (3,))
    weight_grad(2)
    arrived(3, (3,))
    rows_grad(3)
    weight_pair(2)
    weight_grad(3)
    weight_pair(3)
    weight_grad_sum(0)
    weight_grad_sum(1)

    def ret_x_start(z):
        for k in range(NX):
            src, dst = ret_z.at[z, (my_x + k) % NX], ret_x.at[my_x, z]
            if k == 0:
                pltpu.make_async_copy(src, dst, rx_own).start()
            else:
                remote(src, dst, rx_send.at[k], rx_recv.at[NX - k], at_x(k)).start()

    pltpu.make_async_copy(grads.at[:, 0], ret_z.at[my_z], rz_own).wait()
    ret_x_start(my_z)
    for k in (1, 7, 2, 6, 3, 5, 4):
        ret_z_copy(k).wait_recv()
        ret_x_start((my_z - k + NZ) % NZ)
    weight_grad_sum(2)
    weight_grad_sum(3)
    for k in range(NX):
        wait_bytes(ret_x.at[k], rx_own if k == 0 else rx_recv.at[k])

    for k in range(1, NZ):
        dest_copy(k).wait_send()
        attn_z_copy(k).wait_send()
        ret_z_copy(k).wait_send()
    for k in range(1, NX):
        attn_x_copy(k).wait_send()
        wait_bytes(ret_x.at[k], rx_send.at[k])
    for c in range(NC):
        for s in range(LAST):
            ring_copy(c, s, True).wait_send()
            ring_copy(c, s, False).wait_send()
        x_sends_done(c)
    for c in range(NC - 2, NC):
        pair_copy(c).wait_send()
        for k in range(1, NY):
            rs_copy(c, k).wait_send()


def backward(mod, gm, attn, cot, w):
    tok, model = cot.shape
    width = model // NC
    feats = w.shape[0]
    dma = pltpu.SemaphoreType.DMA
    vmem = pl.BlockSpec(memory_space=pltpu.VMEM)
    hbm = pl.BlockSpec(memory_space=pl.ANY)
    return pl.pallas_call(
        kernel,
        out_shape=(
            pltpu.VMEM((NX, NZ, CAP, feats), BF16),
            pltpu.VMEM((8, tok), jnp.int32),
            pltpu.VMEM((feats, model // NDP), BF16),
        ),
        in_specs=[
            vmem, pl.BlockSpec(memory_space=pltpu.SMEM), hbm, hbm, hbm,
        ],
        out_specs=(vmem, vmem, vmem),
        scratch_shapes=[
            pltpu.VMEM((tok, model), BF16),
            pltpu.VMEM((NC, NZ, tok, width), BF16),
            pltpu.VMEM((NZ, 8, tok), jnp.int32),
            pltpu.VMEM((NC, NX, NZ, CAP, width), BF16),
            pltpu.VMEM((NC, NX, NZ, CAP, width), BF16),
            pltpu.VMEM((2, feats, width), BF16),
            pltpu.VMEM((2, CORES, NY, feats, width // NDP), BF16),
            pltpu.VMEM((NC, NY, feats, width // NDP), BF16),
            pltpu.VMEM((NC, NY, feats, width // NDP), BF16),
            pltpu.VMEM((NX, NZ, CAP, feats), F32),
            pltpu.VMEM((NX, HALVES, CAP, model), BF16),
            pltpu.VMEM((NX, HALVES, CAP, model), BF16),
            pltpu.VMEM((NX, NZ, CAP, feats), BF16),
            pltpu.VMEM((feats, NX * NZ * CAP), BF16),
            pltpu.VMEM((NX, NZ, CAP, feats), BF16),
            pltpu.VMEM((NZ, NX, CAP, feats), BF16),
            dma, dma((NC,)), dma((NZ,)), dma((NZ,)),
            dma((NC, LAST)), dma((NC, LAST)), dma((NC, LAST)), dma((NC, LAST)),
            dma((NC, NX)), dma((NC, LAST, NX)), dma((NC, LAST)),
            dma((NX,)), dma((NX,)), dma,
            dma((NZ,)), dma((NZ,)), dma,
            dma((NC,)),
            dma((NC,)), dma((NC,)), dma((NC, NY)), dma((NC, NY)), dma((NC,)),
            dma((NZ,)), dma((NZ,)), dma,
            dma((NX,)), dma((NX,)), dma,
        ],
        compiler_params=pltpu.CompilerParams(
            collective_id=0, has_side_effects=True, vmem_limit_bytes=58 * 1024 * 1024
        ),
        name="moe_proj_backward",
    )(mod, gm, attn, cot, w)


def finish_kernel(dest_ref, ret, wgrad, grad_hbm, w_out, grad, grad_out, w_sent):
    tok, feats = dest_ref.shape[1], ret.shape[3]
    w_store = pltpu.make_async_copy(wgrad, w_out, w_sent)
    w_store.start()

    def grad_store(p):
        at = pl.ds(p * feats, feats)
        return pltpu.make_async_copy(grad.at[:, at], grad_hbm.at[:, at], grad_out.at[p])

    slots = lax.broadcasted_iota(jnp.int32, (NGROUP * CAP, tok), 0)
    back = jnp.where(slots == dest_ref[0:1, :], 1.0, 0.0).T.astype(BF16)
    for p in range(PIECES):
        pieces = jnp.concatenate(
            [ret[g // HALVES, (g % HALVES) * PIECES + p] for g in range(NGROUP)], 0
        )
        grad[:, p * feats:(p + 1) * feats] = jnp.dot(
            back, pieces, preferred_element_type=F32
        ).astype(BF16)
        grad_store(p).start()
    w_store.wait()
    for p in range(PIECES):
        grad_store(p).wait()


def finish(ret, dest, wgrad):
    tok, feats = dest.shape[1], ret.shape[3]
    vmem = pl.BlockSpec(memory_space=pltpu.VMEM)
    hbm = pl.BlockSpec(memory_space=pl.ANY)
    return pl.pallas_call(
        finish_kernel,
        out_shape=(
            jax.ShapeDtypeStruct((tok, PIECES * feats), BF16),
            jax.ShapeDtypeStruct(wgrad.shape, BF16),
        ),
        in_specs=[vmem, vmem, vmem],
        out_specs=(hbm, hbm),
        scratch_shapes=[
            pltpu.VMEM((tok, PIECES * feats), BF16),
            pltpu.SemaphoreType.DMA((PIECES,)), pltpu.SemaphoreType.DMA,
        ],
        compiler_params=pltpu.CompilerParams(vmem_limit_bytes=16 * 1024 * 1024),
        name="finish",
    )(dest, ret, wgrad)


def per_device(attn_out, out_cot, modality, group_modality, o_weight):
    ret, dest, wgrad = backward(
        modality.reshape(1, -1), group_modality, attn_out, out_cot, o_weight
    )
    return finish(ret, dest, wgrad)


def solution(mesh):
    return jax.shard_map(
        per_device,
        mesh=mesh,
        in_specs=(
            P(("dp", "tower"), None),
            P(("dp", "tower"), None),
            P(("dp", "tower")),
            P(),
            P("tower", None),
        ),
        out_specs=(P(("dp", "tower"), None), P("tower", "dp")),
        check_vma=False,
    )
```

```python
import jax
import jax.numpy as jnp
from jax import lax
from jax.experimental import pallas as pl
from jax.experimental.pallas import tpu as pltpu
from jax.sharding import PartitionSpec as P

NGROUP = 8
CAP = 24
NX = 4
NZ = 8
HALVES = NGROUP // NX
PIECES = NZ // HALVES
NDP = 8
CORES = 2
NY = NDP // CORES
ORDER = (0, -1, 1, -2, 2, -3, 3, 4)
PARTS = ((0, 3), (3, 2), (5, 2), (7, 1))
NC = 4
LAST = NZ // 2
TILE = 256
PLACE = {off % NZ: at for at, off in enumerate(ORDER)}
MESH = pl.DeviceIdType.MESH
F32 = jnp.float32
BF16 = jnp.bfloat16


def kernel(
    mod_ref, gm_ref, attn_hbm, cot_hbm, w_ref, ret_x, dest_ref, wgrad_ref,
    attn_ref, ring, dests, staged, cot_got, w_chunk, partial, other, terms, acc,
    attn_own, attn_x, attn_got, attn_t, grads, ret_z,
    attn_in, cot_in, dest_send, dest_recv, right_send, right_recv, left_send, left_recv,
    x_send, x_recv, x_own, ax_send, ax_recv, ax_own, az_send, az_recv, az_own,
    w_sem, pair_send, pair_recv, rs_send, rs_recv, rs_own, rz_send, rz_recv, rz_own, rx_send, rx_recv, rx_own,
):
    tok = cot_hbm.shape[0]
    width = cot_hbm.shape[1] // NC
    cols = width // NDP
    own_cols = wgrad_ref.shape[1]
    feats = w_ref.shape[0]
    half = width // 2
    me, my_d = lax.axis_index("tower"), lax.axis_index("dp")
    my_x, my_z = me // NZ, me % NZ
    my_half = my_z // PIECES
    my_y, my_core = my_d // CORES, my_d % CORES

    def at_z(k):
        return {"tower": my_x * NZ + (my_z + k + NZ) % NZ}

    def at_x(k):
        return {"tower": ((my_x + k) % NX) * NZ + my_z}

    def at_y(k):
        return {"dp": ((my_y + k) % NY) * CORES + my_core}

    other_core = {"dp": my_y * CORES + 1 - my_core}

    def remote(src, dst, send, recv, device):
        return pltpu.make_async_remote_copy(
            src_ref=src, dst_ref=dst, send_sem=send, recv_sem=recv,
            device_id=device, device_id_type=MESH,
        )

    def wait_bytes(ref, sem):
        pltpu.make_async_copy(ref, ref, sem).wait()

    def w_load(c, d):
        return pltpu.make_async_copy(
            w_ref.at[:, pl.ds(d * own_cols + c * cols, cols)],
            w_chunk.at[c % 2, :, pl.ds(d * cols, cols)],
            w_sem.at[c],
        )

    def own_block(c):
        for d in range(NDP):
            pltpu.make_async_copy(
                cot_hbm.at[:, pl.ds(d * own_cols + c * cols, cols)],
                ring.at[c, 0, :, pl.ds(d * cols, cols)],
                cot_in.at[c],
            ).start()

    attn_load = pltpu.make_async_copy(attn_hbm, attn_ref, attn_in)
    barrier = pltpu.get_barrier_semaphore()
    for k in range(1, NZ):
        pl.semaphore_signal(barrier, inc=1, device_id=at_z(k), device_id_type=MESH)
    for k in range(1, NX):
        pl.semaphore_signal(barrier, inc=1, device_id=at_x(k), device_id_type=MESH)
    for k in range(1, NY):
        pl.semaphore_signal(barrier, inc=1, device_id=at_y(k), device_id_type=MESH)
    pl.semaphore_signal(barrier, inc=1, device_id=other_core, device_id_type=MESH)

    own_block(0)
    own_block(1)
    attn_load.start()
    pl.semaphore_wait(barrier, NZ - 1 + NX - 1 + NY)

    def ring_copy(c, s, right):
        off = -s if right else s
        src = ring.at[c, off % NZ]
        dst = ring.at[c, (off - 1 if right else off + 1) % NZ]
        if s == LAST - 1:
            part = pl.ds(0, half) if right else pl.ds(half, half)
            src, dst = src.at[:, part], dst.at[:, part]
        return remote(
            src, dst,
            (right_send if right else left_send).at[c, s],
            (right_recv if right else left_recv).at[c, s],
            at_z(1 if right else -1),
        )

    for c in range(2):
        wait_bytes(ring.at[c, 0], cot_in.at[c])
        ring_copy(c, 0, True).start()
        ring_copy(c, 0, False).start()
    for c in range(2, NC):
        own_block(c)
    for c in range(2):
        for d in range(NDP):
            w_load(c, d).start()

    mod = jnp.broadcast_to(mod_ref[...], (8, tok))
    kinds = [(mod == m).astype(F32) for m in range(3)]
    t_from = lax.broadcasted_iota(jnp.int32, (tok, tok), 0)
    t_to = lax.broadcasted_iota(jnp.int32, (tok, tok), 1)
    earlier = (t_from < t_to).astype(F32).astype(BF16)
    before = jnp.dot(jnp.concatenate(kinds, 0).astype(BF16), earlier, preferred_element_type=F32)
    order = sum(before[8 * m:8 * m + 8] * kinds[m] for m in range(3))
    serves = [gm_ref[g] for g in range(NGROUP)]
    how_many = jnp.ones_like(mod)
    for m in range(3):
        count = sum((s == m).astype(jnp.int32) for s in serves)
        how_many = jnp.where(mod == m, count, how_many)
    per = how_many.astype(F32)
    turn = (order.astype(jnp.int32) + me).astype(F32)
    target = (turn - jnp.floor((turn + 0.5) / per) * per).astype(jnp.int32)
    routed = jnp.zeros_like(mod)
    for g in range(NGROUP):
        rank = sum(((s == serves[g]).astype(jnp.int32) for s in serves[:g]), jnp.int32(0))
        routed = jnp.where((mod == serves[g]) & (target == rank), g, routed)
    dest = routed * CAP + jnp.floor((order + 0.5) / per).astype(jnp.int32)
    dests[0] = dest
    dest_ref[...] = dest

    def dest_copy(k):
        return remote(dests.at[0], dests.at[NZ - k], dest_send.at[k], dest_recv.at[NZ - k], at_z(k))

    for k in range(1, NZ):
        dest_copy(k).start()

    slots = lax.broadcasted_iota(jnp.int32, (NGROUP * CAP, tok), 0)
    attn_load.wait()
    pick_own = jnp.where(slots == dest[0:1], 1.0, 0.0).astype(BF16)
    for p in range(PIECES):
        got = jnp.dot(pick_own, attn_ref[:, p * feats:(p + 1) * feats], preferred_element_type=F32)
        attn_own[:, :, :, p * feats:(p + 1) * feats] = got.astype(BF16).reshape(NX, HALVES, CAP, feats)

    def attn_x_copy(k):
        return remote(
            attn_own.at[(my_x + k) % NX], attn_x.at[my_x], ax_send.at[k], ax_recv.at[NX - k], at_x(k)
        )

    own_ax = pltpu.make_async_copy(attn_own.at[my_x], attn_x.at[my_x], ax_own)
    own_ax.start()
    for k in range(1, NX):
        attn_x_copy(k).start()

    def attn_z_src(k):
        z = (my_z + k) % NZ
        start = pl.multiple_of((z % PIECES) * feats, feats)
        return attn_x.at[:, z // PIECES, :, pl.ds(start, feats)]

    def attn_z_copy(k):
        return remote(
            attn_z_src(k), attn_got.at[:, PLACE[NZ - k]], az_send.at[k], az_recv.at[NZ - k], at_z(k)
        )

    def attn_along_z():
        own_ax.wait()
        for k in range(1, NX):
            attn_x_copy(k).wait_recv()
        pltpu.make_async_copy(attn_z_src(0), attn_got.at[:, 0], az_own).start()
        for k in range(1, NZ):
            attn_z_copy(k).start()

    def attn_arrived():
        pltpu.make_async_copy(attn_z_src(0), attn_got.at[:, 0], az_own).wait()
        for k in range(1, NZ):
            attn_z_copy(k).wait_recv()

        @pl.loop(0, feats // TILE)
        def _(j):
            at = pl.ds(pl.multiple_of(j * TILE, TILE), TILE)
            attn_t[at, :] = jnp.transpose(attn_got[:, :, :, at].reshape(NX * NZ * CAP, TILE))

    rows = lax.broadcasted_iota(jnp.int32, (NX * CAP, tok), 0)
    x_of = sum((rows >= CAP * k).astype(jnp.int32) for k in range(1, NX))
    wanted = rows + CAP * (HALVES - 1) * x_of + CAP * my_half

    def deliver(c, *offsets):
        at = pl.ds(PLACE[offsets[0] % NZ], len(offsets))
        for off in offsets:
            slot = off % NZ
            pick = jnp.where(wanted == dests[slot, 0:1, :], 1.0, 0.0).astype(BF16)
            got = jnp.dot(pick, ring[c, slot], preferred_element_type=F32).astype(BF16)
            for x in range(NX):
                staged[c, x, PLACE[slot]] = got[x * CAP:(x + 1) * CAP]
        part = max(abs(offsets[0]), 1) - 1
        lands = cot_got.at[c, my_x, at]
        for k in range(1, NX):
            src = staged.at[c, (my_x + k) % NX, at]
            remote(src, lands, x_send.at[c, k], x_recv.at[c, part, NX - k], at_x(k)).start()
        pltpu.make_async_copy(staged.at[c, my_x, at], lands, x_own.at[c, part]).start()

    def arrived(c, parts):
        for part in parts:
            count = PARTS[part][1]
            wait_bytes(staged.at[c, 0, pl.ds(0, count)], x_own.at[c, part])
            for k in range(1, NX):
                wait_bytes(staged.at[c, k, pl.ds(0, count)], x_recv.at[c, part, k])

    def x_sends_done(c):
        for k in range(1, NX):
            wait_bytes(staged.at[c, k], x_send.at[c, k])

    def input_grad(c):
        wait_bytes(w_chunk.at[c % 2], w_sem.at[c])

        @pl.loop(0, feats // TILE)
        def _(j):
            at = pl.ds(pl.multiple_of(j * TILE, TILE), TILE)
            term = lax.dot_general(
                cot_got[c].reshape(NX * NZ * CAP, width), w_chunk[c % 2, at, :],
                (((1,), (1,)), ((), ())), preferred_element_type=F32,
            )
            term = term.reshape(NX, NZ, CAP, TILE)
            acc[:, :, :, at] = term if c == 0 else acc[:, :, :, at] + term

        for d in range(NDP):
            w_load(c + 2, d).start()

    def rows_grad(part):
        first, count = PARTS[part]
        own = slice(first, first + count)

        @pl.loop(0, feats // TILE)
        def _(j):
            at = pl.ds(pl.multiple_of(j * TILE, TILE), TILE)
            term = sum(
                lax.dot_general(
                    cot_got[c, :, own].reshape(NX * count * CAP, width), w_chunk[c % 2, at, :],
                    (((1,), (1,)), ((), ())), preferred_element_type=F32,
                )
                for c in range(NC - 2, NC)
            )
            total = term.reshape(NX, count, CAP, TILE) + acc[:, own, :, at]
            grads[:, own, :, at] = total.astype(BF16)

        for off in ORDER[own]:
            if off == 0:
                pltpu.make_async_copy(grads.at[:, 0], ret_z.at[my_z], rz_own).start()
            else:
                ret_z_copy(off % NZ).start()

    def pair_copy(c):
        return remote(
            partial.at[c % 2, 1 - my_core], other.at[c], pair_send.at[c], pair_recv.at[c], other_core
        )

    def rs_copy(c, k):
        return remote(
            partial.at[c % 2, my_core, (my_y + k) % NY], terms.at[c, my_y],
            rs_send.at[c, k], rs_recv.at[c, NY - k], at_y(k),
        )

    def rs_own_copy(c):
        return pltpu.make_async_copy(
            partial.at[c % 2, my_core, my_y], terms.at[c, my_y], rs_own.at[c]
        )

    def weight_sends_done(c):
        pair_copy(c).wait_send()
        for k in range(1, NY):
            rs_copy(c, k).wait_send()
        rs_own_copy(c).wait()

    def weight_grad(c):
        if c >= 2:
            weight_sends_done(c - 2)

        @pl.loop(0, width // TILE)
        def _(j):
            at = pl.ds(pl.multiple_of(j * TILE, TILE), TILE)
            term = jnp.dot(
                attn_t[...], cot_got[c, :, :, :, at].reshape(NX * NZ * CAP, TILE),
                preferred_element_type=F32,
            ).astype(BF16)
            for i in range(CORES):
                partial[c % 2, i, j] = term[:, i * cols:(i + 1) * cols]

        pair_copy(c).start()

    def weight_pair(c):
        pair_copy(c).wait_recv()

        for k in (1, 2, 3, 0):
            y = (my_y + k) % NY

            @pl.loop(0, feats // TILE)
            def _(j):
                at = pl.ds(pl.multiple_of(j * TILE, TILE), TILE)
                both = partial[c % 2, my_core, y, at, :].astype(F32) + other[c, y, at, :].astype(F32)
                partial[c % 2, my_core, y, at, :] = both.astype(BF16)

            if k == 0:
                rs_own_copy(c).start()
            else:
                rs_copy(c, k).start()

    def weight_grad_sum(c):
        if c >= NC - 2:
            rs_own_copy(c).wait()
        for k in range(1, NY):
            rs_copy(c, k).wait_recv()

        @pl.loop(0, feats // TILE)
        def _(j):
            at = pl.ds(pl.multiple_of(j * TILE, TILE), TILE)
            total = terms[c, 0, at, :].astype(F32)
            for y in range(1, NY):
                total += terms[c, y, at, :].astype(F32)
            wgrad_ref[at, c * cols:(c + 1) * cols] = total.astype(BF16)

    def ret_z_copy(k):
        return remote(
            grads.at[:, PLACE[k]], ret_z.at[my_z], rz_send.at[k], rz_recv.at[NZ - k], at_z(k)
        )

    def ring_step(c, s):
        if c >= 2 and s == 0:
            wait_bytes(ring.at[c, 0], cot_in.at[c])
        for right in (True, False):
            if s > 0:
                ring_copy(c, s - 1, right).wait_recv()
            if s < LAST and (c >= 2 or s > 0):
                ring_copy(c, s, right).start()
        if (c, s) == (0, 1):
            for k in range(1, NZ):
                dest_copy(k).wait_recv()
        if s in (0, LAST):
            deliver(c, s)
        else:
            deliver(c, -s, s)

    for c, s in ((0, 0), (1, 0), (0, 1), (1, 1), (0, 2)):
        ring_step(c, s)
    attn_along_z()
    every = range(len(PARTS))
    for c, s in ((1, 2), (0, 3), (2, 0), (1, 3), (3, 0), (0, 4), (2, 1), (1, 4)):
        ring_step(c, s)
    arrived(0, every)
    input_grad(0)
    ring_step(3, 1)
    arrived(1, every)
    input_grad(1)
    ring_step(2, 2)
    attn_arrived()
    weight_grad(0)
    ring_step(3, 2)
    weight_grad(1)
    weight_pair(0)
    ring_step(2, 3)
    for c in range(NC - 2, NC):
        wait_bytes(w_chunk.at[c % 2], w_sem.at[c])
        arrived(c, (0,))
    rows_grad(0)
    ring_step(3, 3)
    weight_pair(1)
    ring_step(2, 4)
    for c in range(NC - 2, NC):
        arrived(c, (1,))
    rows_grad(1)
    arrived(2, (2, 3))
    weight_grad(2)
    arrived(3, (2,))
    rows_grad(2)
    ring_step(3, 4)
    weight_pair(2)
    arrived(3, (3,))
    weight_grad(3)
    rows_grad(3)
    weight_pair(3)
    weight_grad_sum(0)
    weight_grad_sum(1)

    def ret_x_start(z):
        for k in range(NX):
            src, dst = ret_z.at[z, (my_x + k) % NX], ret_x.at[my_x, z]
            if k == 0:
                pltpu.make_async_copy(src, dst, rx_own).start()
            else:
                remote(src, dst, rx_send.at[k], rx_recv.at[NX - k], at_x(k)).start()

    pltpu.make_async_copy(grads.at[:, 0], ret_z.at[my_z], rz_own).wait()
    ret_x_start(my_z)
    for k in (1, 7, 2, 6, 3, 5, 4):
        ret_z_copy(k).wait_recv()
        ret_x_start((my_z - k + NZ) % NZ)
    weight_grad_sum(2)
    weight_grad_sum(3)
    for k in range(NX):
        wait_bytes(ret_x.at[k], rx_own if k == 0 else rx_recv.at[k])

    for k in range(1, NZ):
        dest_copy(k).wait_send()
        attn_z_copy(k).wait_send()
        ret_z_copy(k).wait_send()
    for k in range(1, NX):
        attn_x_copy(k).wait_send()
        wait_bytes(ret_x.at[k], rx_send.at[k])
    for c in range(NC):
        for s in range(LAST):
            ring_copy(c, s, True).wait_send()
            ring_copy(c, s, False).wait_send()
        x_sends_done(c)
    for c in range(NC - 2, NC):
        pair_copy(c).wait_send()
        for k in range(1, NY):
            rs_copy(c, k).wait_send()


def backward(mod, gm, attn, cot, w):
    tok, model = cot.shape
    width = model // NC
    feats = w.shape[0]
    dma = pltpu.SemaphoreType.DMA
    vmem = pl.BlockSpec(memory_space=pltpu.VMEM)
    hbm = pl.BlockSpec(memory_space=pl.ANY)
    return pl.pallas_call(
        kernel,
        out_shape=(
            pltpu.VMEM((NX, NZ, CAP, feats), BF16),
            pltpu.VMEM((8, tok), jnp.int32),
            pltpu.VMEM((feats, model // NDP), BF16),
        ),
        in_specs=[
            vmem, pl.BlockSpec(memory_space=pltpu.SMEM), hbm, hbm, hbm,
        ],
        out_specs=(vmem, vmem, vmem),
        scratch_shapes=[
            pltpu.VMEM((tok, model), BF16),
            pltpu.VMEM((NC, NZ, tok, width), BF16),
            pltpu.VMEM((NZ, 8, tok), jnp.int32),
            pltpu.VMEM((NC, NX, NZ, CAP, width), BF16),
            pltpu.VMEM((NC, NX, NZ, CAP, width), BF16),
            pltpu.VMEM((2, feats, width), BF16),
            pltpu.VMEM((2, CORES, NY, feats, width // NDP), BF16),
            pltpu.VMEM((NC, NY, feats, width // NDP), BF16),
            pltpu.VMEM((NC, NY, feats, width // NDP), BF16),
            pltpu.VMEM((NX, NZ, CAP, feats), F32),
            pltpu.VMEM((NX, HALVES, CAP, model), BF16),
            pltpu.VMEM((NX, HALVES, CAP, model), BF16),
            pltpu.VMEM((NX, NZ, CAP, feats), BF16),
            pltpu.VMEM((feats, NX * NZ * CAP), BF16),
            pltpu.VMEM((NX, NZ, CAP, feats), BF16),
            pltpu.VMEM((NZ, NX, CAP, feats), BF16),
            dma, dma((NC,)), dma((NZ,)), dma((NZ,)),
            dma((NC, LAST)), dma((NC, LAST)), dma((NC, LAST)), dma((NC, LAST)),
            dma((NC, NX)), dma((NC, LAST, NX)), dma((NC, LAST)),
            dma((NX,)), dma((NX,)), dma,
            dma((NZ,)), dma((NZ,)), dma,
            dma((NC,)),
            dma((NC,)), dma((NC,)), dma((NC, NY)), dma((NC, NY)), dma((NC,)),
            dma((NZ,)), dma((NZ,)), dma,
            dma((NX,)), dma((NX,)), dma,
        ],
        compiler_params=pltpu.CompilerParams(
            collective_id=0, has_side_effects=True, vmem_limit_bytes=58 * 1024 * 1024
        ),
        name="moe_proj_backward",
    )(mod, gm, attn, cot, w)


def finish_kernel(dest_ref, ret, wgrad, grad_hbm, w_out, grad, grad_out, w_sent):
    tok, feats = dest_ref.shape[1], ret.shape[3]
    w_store = pltpu.make_async_copy(wgrad, w_out, w_sent)
    w_store.start()

    def grad_store(p):
        at = pl.ds(p * feats, feats)
        return pltpu.make_async_copy(grad.at[:, at], grad_hbm.at[:, at], grad_out.at[p])

    slots = lax.broadcasted_iota(jnp.int32, (NGROUP * CAP, tok), 0)
    back = jnp.where(slots == dest_ref[0:1, :], 1.0, 0.0).T.astype(BF16)
    for p in range(PIECES):
        pieces = jnp.concatenate(
            [ret[g // HALVES, (g % HALVES) * PIECES + p] for g in range(NGROUP)], 0
        )
        grad[:, p * feats:(p + 1) * feats] = jnp.dot(
            back, pieces, preferred_element_type=F32
        ).astype(BF16)
        grad_store(p).start()
    w_store.wait()
    for p in range(PIECES):
        grad_store(p).wait()


def finish(ret, dest, wgrad):
    tok, feats = dest.shape[1], ret.shape[3]
    vmem = pl.BlockSpec(memory_space=pltpu.VMEM)
    hbm = pl.BlockSpec(memory_space=pl.ANY)
    return pl.pallas_call(
        finish_kernel,
        out_shape=(
            jax.ShapeDtypeStruct((tok, PIECES * feats), BF16),
            jax.ShapeDtypeStruct(wgrad.shape, BF16),
        ),
        in_specs=[vmem, vmem, vmem],
        out_specs=(hbm, hbm),
        scratch_shapes=[
            pltpu.VMEM((tok, PIECES * feats), BF16),
            pltpu.SemaphoreType.DMA((PIECES,)), pltpu.SemaphoreType.DMA,
        ],
        compiler_params=pltpu.CompilerParams(vmem_limit_bytes=16 * 1024 * 1024),
        name="finish",
    )(dest, ret, wgrad)


def per_device(attn_out, out_cot, modality, group_modality, o_weight):
    ret, dest, wgrad = backward(
        modality.reshape(1, -1), group_modality, attn_out, out_cot, o_weight
    )
    return finish(ret, dest, wgrad)


def solution(mesh):
    return jax.shard_map(
        per_device,
        mesh=mesh,
        in_specs=(
            P(("dp", "tower"), None),
            P(("dp", "tower"), None),
            P(("dp", "tower")),
            P(),
            P("tower", None),
        ),
        out_specs=(P(("dp", "tower"), None), P("tower", "dp")),
        check_vma=False,
    )
```

```python
import jax
import jax.numpy as jnp
from jax import lax
from jax.experimental import pallas as pl
from jax.experimental.pallas import tpu as pltpu
from jax.sharding import PartitionSpec as P

NGROUP = 8
CAP = 24
NX = 4
NZ = 8
HALVES = NGROUP // NX
PIECES = NZ // HALVES
NDP = 8
CORES = 2
NY = NDP // CORES
ORDER = (0, -1, 1, -2, 2, -3, 3, 4)
PARTS = ((0, 3), (3, 2), (5, 2), (7, 1))
NC = 4
LAST = NZ // 2
TILE = 256
PLACE = {off % NZ: at for at, off in enumerate(ORDER)}
MESH = pl.DeviceIdType.MESH
F32 = jnp.float32
BF16 = jnp.bfloat16


def kernel(
    mod_ref, gm_ref, attn_hbm, cot_hbm, w_ref, ret_x, dest_ref, wgrad_ref,
    attn_ref, ring, dests, staged, cot_got, w_chunk, partial, other, terms, acc,
    attn_own, attn_x, attn_got, attn_t, grads, ret_z,
    attn_in, cot_in, dest_send, dest_recv, right_send, right_recv, left_send, left_recv,
    x_send, x_recv, x_own, ax_send, ax_recv, ax_own, az_send, az_recv, az_own,
    w_sem, pair_send, pair_recv, rs_send, rs_recv, rs_own, rz_send, rz_recv, rz_own, rx_send, rx_recv, rx_own,
):
    tok = cot_hbm.shape[0]
    width = cot_hbm.shape[1] // NC
    cols = width // NDP
    own_cols = wgrad_ref.shape[1]
    feats = w_ref.shape[0]
    half = width // 2
    me, my_d = lax.axis_index("tower"), lax.axis_index("dp")
    my_x, my_z = me // NZ, me % NZ
    my_half = my_z // PIECES
    my_y, my_core = my_d // CORES, my_d % CORES

    def at_z(k):
        return {"tower": my_x * NZ + (my_z + k + NZ) % NZ}

    def at_x(k):
        return {"tower": ((my_x + k) % NX) * NZ + my_z}

    def at_y(k):
        return {"dp": ((my_y + k) % NY) * CORES + my_core}

    other_core = {"dp": my_y * CORES + 1 - my_core}

    def remote(src, dst, send, recv, device):
        return pltpu.make_async_remote_copy(
            src_ref=src, dst_ref=dst, send_sem=send, recv_sem=recv,
            device_id=device, device_id_type=MESH,
        )

    def wait_bytes(ref, sem):
        pltpu.make_async_copy(ref, ref, sem).wait()

    def w_load(c, d):
        return pltpu.make_async_copy(
            w_ref.at[:, pl.ds(d * own_cols + c * cols, cols)],
            w_chunk.at[c % 2, :, pl.ds(d * cols, cols)],
            w_sem.at[c],
        )

    def own_block(c):
        for d in range(NDP):
            pltpu.make_async_copy(
                cot_hbm.at[:, pl.ds(d * own_cols + c * cols, cols)],
                ring.at[c, 0, :, pl.ds(d * cols, cols)],
                cot_in.at[c],
            ).start()

    attn_load = pltpu.make_async_copy(attn_hbm, attn_ref, attn_in)
    barrier = pltpu.get_barrier_semaphore()
    for k in range(1, NZ):
        pl.semaphore_signal(barrier, inc=1, device_id=at_z(k), device_id_type=MESH)
    for k in range(1, NX):
        pl.semaphore_signal(barrier, inc=1, device_id=at_x(k), device_id_type=MESH)
    for k in range(1, NY):
        pl.semaphore_signal(barrier, inc=1, device_id=at_y(k), device_id_type=MESH)
    pl.semaphore_signal(barrier, inc=1, device_id=other_core, device_id_type=MESH)

    for c in range(3):
        own_block(c)
    attn_load.start()
    pl.semaphore_wait(barrier, NZ - 1 + NX - 1 + NY)

    def ring_copy(c, s, right):
        off = -s if right else s
        src = ring.at[c, off % NZ]
        dst = ring.at[c, (off - 1 if right else off + 1) % NZ]
        if s == LAST - 1:
            part = pl.ds(0, half) if right else pl.ds(half, half)
            src, dst = src.at[:, part], dst.at[:, part]
        return remote(
            src, dst,
            (right_send if right else left_send).at[c, s],
            (right_recv if right else left_recv).at[c, s],
            at_z(1 if right else -1),
        )

    def ring_start(c):
        wait_bytes(ring.at[c, 0], cot_in.at[c])
        ring_copy(c, 0, True).start()
        ring_copy(c, 0, False).start()

    for c in range(3):
        ring_start(c)
    own_block(3)
    for c in range(2):
        for d in range(NDP):
            w_load(c, d).start()

    mod = jnp.broadcast_to(mod_ref[...], (8, tok))
    kinds = [(mod == m).astype(F32) for m in range(3)]
    t_from = lax.broadcasted_iota(jnp.int32, (tok, tok), 0)
    t_to = lax.broadcasted_iota(jnp.int32, (tok, tok), 1)
    earlier = (t_from < t_to).astype(F32).astype(BF16)
    before = jnp.dot(jnp.concatenate(kinds, 0).astype(BF16), earlier, preferred_element_type=F32)
    order = sum(before[8 * m:8 * m + 8] * kinds[m] for m in range(3))
    serves = [gm_ref[g] for g in range(NGROUP)]
    how_many = jnp.ones_like(mod)
    for m in range(3):
        count = sum((s == m).astype(jnp.int32) for s in serves)
        how_many = jnp.where(mod == m, count, how_many)
    per = how_many.astype(F32)
    turn = (order.astype(jnp.int32) + me).astype(F32)
    target = (turn - jnp.floor((turn + 0.5) / per) * per).astype(jnp.int32)
    routed = jnp.zeros_like(mod)
    for g in range(NGROUP):
        rank = sum(((s == serves[g]).astype(jnp.int32) for s in serves[:g]), jnp.int32(0))
        routed = jnp.where((mod == serves[g]) & (target == rank), g, routed)
    dest = routed * CAP + jnp.floor((order + 0.5) / per).astype(jnp.int32)
    dests[0] = dest
    dest_ref[...] = dest

    def dest_copy(k):
        return remote(dests.at[0], dests.at[NZ - k], dest_send.at[k], dest_recv.at[NZ - k], at_z(k))

    for k in range(1, NZ):
        dest_copy(k).start()

    slots = lax.broadcasted_iota(jnp.int32, (NGROUP * CAP, tok), 0)
    attn_load.wait()
    pick_own = jnp.where(slots == dest[0:1], 1.0, 0.0).astype(BF16)
    for p in range(PIECES):
        got = jnp.dot(pick_own, attn_ref[:, p * feats:(p + 1) * feats], preferred_element_type=F32)
        attn_own[:, :, :, p * feats:(p + 1) * feats] = got.astype(BF16).reshape(NX, HALVES, CAP, feats)

    def attn_x_copy(k):
        return remote(
            attn_own.at[(my_x + k) % NX], attn_x.at[my_x], ax_send.at[k], ax_recv.at[NX - k], at_x(k)
        )

    own_ax = pltpu.make_async_copy(attn_own.at[my_x], attn_x.at[my_x], ax_own)
    own_ax.start()
    for k in range(1, NX):
        attn_x_copy(k).start()

    def attn_z_src(k):
        z = (my_z + k) % NZ
        start = pl.multiple_of((z % PIECES) * feats, feats)
        return attn_x.at[:, z // PIECES, :, pl.ds(start, feats)]

    def attn_z_copy(k):
        return remote(
            attn_z_src(k), attn_got.at[:, PLACE[NZ - k]], az_send.at[k], az_recv.at[NZ - k], at_z(k)
        )

    def attn_along_z():
        own_ax.wait()
        for k in range(1, NX):
            attn_x_copy(k).wait_recv()
        pltpu.make_async_copy(attn_z_src(0), attn_got.at[:, 0], az_own).start()
        for k in range(1, NZ):
            attn_z_copy(k).start()

    def attn_arrived():
        pltpu.make_async_copy(attn_z_src(0), attn_got.at[:, 0], az_own).wait()
        for k in range(1, NZ):
            attn_z_copy(k).wait_recv()

        @pl.loop(0, feats // TILE)
        def _(j):
            at = pl.ds(pl.multiple_of(j * TILE, TILE), TILE)
            attn_t[at, :] = jnp.transpose(attn_got[:, :, :, at].reshape(NX * NZ * CAP, TILE))

    rows = lax.broadcasted_iota(jnp.int32, (NX * CAP, tok), 0)
    x_of = sum((rows >= CAP * k).astype(jnp.int32) for k in range(1, NX))
    wanted = rows + CAP * (HALVES - 1) * x_of + CAP * my_half

    def deliver(c, *offsets):
        at = pl.ds(PLACE[offsets[0] % NZ], len(offsets))
        for off in offsets:
            slot = off % NZ
            pick = jnp.where(wanted == dests[slot, 0:1, :], 1.0, 0.0).astype(BF16)
            got = jnp.dot(pick, ring[c, slot], preferred_element_type=F32).astype(BF16)
            for x in range(NX):
                staged[c, x, PLACE[slot]] = got[x * CAP:(x + 1) * CAP]
        part = max(abs(offsets[0]), 1) - 1
        lands = cot_got.at[c, my_x, at]
        for k in range(1, NX):
            src = staged.at[c, (my_x + k) % NX, at]
            remote(src, lands, x_send.at[c, k], x_recv.at[c, part, NX - k], at_x(k)).start()
        pltpu.make_async_copy(staged.at[c, my_x, at], lands, x_own.at[c, part]).start()

    def arrived(c, parts):
        for part in parts:
            count = PARTS[part][1]
            wait_bytes(staged.at[c, 0, pl.ds(0, count)], x_own.at[c, part])
            for k in range(1, NX):
                wait_bytes(staged.at[c, k, pl.ds(0, count)], x_recv.at[c, part, k])

    def x_sends_done(c):
        for k in range(1, NX):
            wait_bytes(staged.at[c, k], x_send.at[c, k])

    def input_grad(c):
        wait_bytes(w_chunk.at[c % 2], w_sem.at[c])

        @pl.loop(0, feats // TILE)
        def _(j):
            at = pl.ds(pl.multiple_of(j * TILE, TILE), TILE)
            term = lax.dot_general(
                cot_got[c].reshape(NX * NZ * CAP, width), w_chunk[c % 2, at, :],
                (((1,), (1,)), ((), ())), preferred_element_type=F32,
            )
            term = term.reshape(NX, NZ, CAP, TILE)
            acc[:, :, :, at] = term if c == 0 else acc[:, :, :, at] + term

        for d in range(NDP):
            w_load(c + 2, d).start()

    def rows_grad(part):
        first, count = PARTS[part]
        own = slice(first, first + count)

        @pl.loop(0, feats // TILE)
        def _(j):
            at = pl.ds(pl.multiple_of(j * TILE, TILE), TILE)
            term = sum(
                lax.dot_general(
                    cot_got[c, :, own].reshape(NX * count * CAP, width), w_chunk[c % 2, at, :],
                    (((1,), (1,)), ((), ())), preferred_element_type=F32,
                )
                for c in range(NC - 2, NC)
            )
            total = term.reshape(NX, count, CAP, TILE) + acc[:, own, :, at]
            grads[:, own, :, at] = total.astype(BF16)

        for off in ORDER[own]:
            if off == 0:
                pltpu.make_async_copy(grads.at[:, 0], ret_z.at[my_z], rz_own).start()
            else:
                ret_z_copy(off % NZ).start()

    def pair_copy(c):
        return remote(
            partial.at[c % 2, 1 - my_core], other.at[c], pair_send.at[c], pair_recv.at[c], other_core
        )

    def rs_copy(c, k):
        return remote(
            partial.at[c % 2, my_core, (my_y + k) % NY], terms.at[c, my_y],
            rs_send.at[c, k], rs_recv.at[c, NY - k], at_y(k),
        )

    def rs_own_copy(c):
        return pltpu.make_async_copy(
            partial.at[c % 2, my_core, my_y], terms.at[c, my_y], rs_own.at[c]
        )

    def weight_sends_done(c):
        pair_copy(c).wait_send()
        for k in range(1, NY):
            rs_copy(c, k).wait_send()
        rs_own_copy(c).wait()

    def weight_grad(c):
        if c >= 2:
            weight_sends_done(c - 2)

        @pl.loop(0, width // TILE)
        def _(j):
            at = pl.ds(pl.multiple_of(j * TILE, TILE), TILE)
            term = jnp.dot(
                attn_t[...], cot_got[c, :, :, :, at].reshape(NX * NZ * CAP, TILE),
                preferred_element_type=F32,
            ).astype(BF16)
            for i in range(CORES):
                partial[c % 2, i, j] = term[:, i * cols:(i + 1) * cols]

        pair_copy(c).start()

    def weight_pair(c):
        pair_copy(c).wait_recv()

        for k in (1, 2, 3, 0):
            y = (my_y + k) % NY

            @pl.loop(0, feats // TILE)
            def _(j):
                at = pl.ds(pl.multiple_of(j * TILE, TILE), TILE)
                both = partial[c % 2, my_core, y, at, :].astype(F32) + other[c, y, at, :].astype(F32)
                partial[c % 2, my_core, y, at, :] = both.astype(BF16)

            if k == 0:
                rs_own_copy(c).start()
            else:
                rs_copy(c, k).start()

    def weight_grad_sum(c):
        if c >= NC - 2:
            rs_own_copy(c).wait()
        for k in range(1, NY):
            rs_copy(c, k).wait_recv()

        @pl.loop(0, feats // TILE)
        def _(j):
            at = pl.ds(pl.multiple_of(j * TILE, TILE), TILE)
            total = terms[c, 0, at, :].astype(F32)
            for y in range(1, NY):
                total += terms[c, y, at, :].astype(F32)
            wgrad_ref[at, c * cols:(c + 1) * cols] = total.astype(BF16)

    def ret_z_copy(k):
        return remote(
            grads.at[:, PLACE[k]], ret_z.at[my_z], rz_send.at[k], rz_recv.at[NZ - k], at_z(k)
        )

    def ring_step(c, s):
        for right in (True, False):
            if s > 0:
                ring_copy(c, s - 1, right).wait_recv()
            if 0 < s < LAST:
                ring_copy(c, s, right).start()
        if (c, s) == (0, 1):
            for k in range(1, NZ):
                dest_copy(k).wait_recv()
        if s in (0, LAST):
            deliver(c, s)
        else:
            deliver(c, -s, s)

    for c, s in ((0, 0), (1, 0), (0, 1), (1, 1)):
        ring_step(c, s)
    ring_start(3)
    ring_step(0, 2)
    attn_along_z()
    every = range(len(PARTS))
    for c, s in ((1, 2), (0, 3), (2, 0), (1, 3), (3, 0), (0, 4), (2, 1), (1, 4)):
        ring_step(c, s)
    arrived(0, every)
    input_grad(0)
    ring_step(3, 1)
    arrived(1, every)
    input_grad(1)
    ring_step(2, 2)
    attn_arrived()
    weight_grad(0)
    ring_step(3, 2)
    weight_grad(1)
    weight_pair(0)
    ring_step(2, 3)
    for c in range(NC - 2, NC):
        wait_bytes(w_chunk.at[c % 2], w_sem.at[c])
        arrived(c, (0,))
    rows_grad(0)
    ring_step(3, 3)
    weight_pair(1)
    ring_step(2, 4)
    for c in range(NC - 2, NC):
        arrived(c, (1,))
    rows_grad(1)
    arrived(2, (2, 3))
    weight_grad(2)
    arrived(3, (2,))
    rows_grad(2)
    ring_step(3, 4)
    weight_pair(2)
    arrived(3, (3,))
    weight_grad(3)
    rows_grad(3)
    weight_pair(3)
    weight_grad_sum(0)
    weight_grad_sum(1)

    def ret_x_start(z):
        for k in range(NX):
            src, dst = ret_z.at[z, (my_x + k) % NX], ret_x.at[my_x, z]
            if k == 0:
                pltpu.make_async_copy(src, dst, rx_own).start()
            else:
                remote(src, dst, rx_send.at[k], rx_recv.at[NX - k], at_x(k)).start()

    pltpu.make_async_copy(grads.at[:, 0], ret_z.at[my_z], rz_own).wait()
    ret_x_start(my_z)
    for k in (1, 7, 2, 6, 3, 5, 4):
        ret_z_copy(k).wait_recv()
        ret_x_start((my_z - k + NZ) % NZ)
    weight_grad_sum(2)
    weight_grad_sum(3)
    for k in range(NX):
        wait_bytes(ret_x.at[k], rx_own if k == 0 else rx_recv.at[k])

    for k in range(1, NZ):
        dest_copy(k).wait_send()
        attn_z_copy(k).wait_send()
        ret_z_copy(k).wait_send()
    for k in range(1, NX):
        attn_x_copy(k).wait_send()
        wait_bytes(ret_x.at[k], rx_send.at[k])
    for c in range(NC):
        for s in range(LAST):
            ring_copy(c, s, True).wait_send()
            ring_copy(c, s, False).wait_send()
        x_sends_done(c)
    for c in range(NC - 2, NC):
        pair_copy(c).wait_send()
        for k in range(1, NY):
            rs_copy(c, k).wait_send()


def backward(mod, gm, attn, cot, w):
    tok, model = cot.shape
    width = model // NC
    feats = w.shape[0]
    dma = pltpu.SemaphoreType.DMA
    vmem = pl.BlockSpec(memory_space=pltpu.VMEM)
    hbm = pl.BlockSpec(memory_space=pl.ANY)
    return pl.pallas_call(
        kernel,
        out_shape=(
            pltpu.VMEM((NX, NZ, CAP, feats), BF16),
            pltpu.VMEM((8, tok), jnp.int32),
            pltpu.VMEM((feats, model // NDP), BF16),
        ),
        in_specs=[
            vmem, pl.BlockSpec(memory_space=pltpu.SMEM), hbm, hbm, hbm,
        ],
        out_specs=(vmem, vmem, vmem),
        scratch_shapes=[
            pltpu.VMEM((tok, model), BF16),
            pltpu.VMEM((NC, NZ, tok, width), BF16),
            pltpu.VMEM((NZ, 8, tok), jnp.int32),
            pltpu.VMEM((NC, NX, NZ, CAP, width), BF16),
            pltpu.VMEM((NC, NX, NZ, CAP, width), BF16),
            pltpu.VMEM((2, feats, width), BF16),
            pltpu.VMEM((2, CORES, NY, feats, width // NDP), BF16),
            pltpu.VMEM((NC, NY, feats, width // NDP), BF16),
            pltpu.VMEM((NC, NY, feats, width // NDP), BF16),
            pltpu.VMEM((NX, NZ, CAP, feats), F32),
            pltpu.VMEM((NX, HALVES, CAP, model), BF16),
            pltpu.VMEM((NX, HALVES, CAP, model), BF16),
            pltpu.VMEM((NX, NZ, CAP, feats), BF16),
            pltpu.VMEM((feats, NX * NZ * CAP), BF16),
            pltpu.VMEM((NX, NZ, CAP, feats), BF16),
            pltpu.VMEM((NZ, NX, CAP, feats), BF16),
            dma, dma((NC,)), dma((NZ,)), dma((NZ,)),
            dma((NC, LAST)), dma((NC, LAST)), dma((NC, LAST)), dma((NC, LAST)),
            dma((NC, NX)), dma((NC, LAST, NX)), dma((NC, LAST)),
            dma((NX,)), dma((NX,)), dma,
            dma((NZ,)), dma((NZ,)), dma,
            dma((NC,)),
            dma((NC,)), dma((NC,)), dma((NC, NY)), dma((NC, NY)), dma((NC,)),
            dma((NZ,)), dma((NZ,)), dma,
            dma((NX,)), dma((NX,)), dma,
        ],
        compiler_params=pltpu.CompilerParams(
            collective_id=0, has_side_effects=True, vmem_limit_bytes=58 * 1024 * 1024
        ),
        name="moe_proj_backward",
    )(mod, gm, attn, cot, w)


def finish_kernel(dest_ref, ret, wgrad, grad_hbm, w_out, grad, grad_out, w_sent):
    tok, feats = dest_ref.shape[1], ret.shape[3]
    w_store = pltpu.make_async_copy(wgrad, w_out, w_sent)
    w_store.start()

    def grad_store(p):
        at = pl.ds(p * feats, feats)
        return pltpu.make_async_copy(grad.at[:, at], grad_hbm.at[:, at], grad_out.at[p])

    slots = lax.broadcasted_iota(jnp.int32, (NGROUP * CAP, tok), 0)
    back = jnp.where(slots == dest_ref[0:1, :], 1.0, 0.0).T.astype(BF16)
    for p in range(PIECES):
        pieces = jnp.concatenate(
            [ret[g // HALVES, (g % HALVES) * PIECES + p] for g in range(NGROUP)], 0
        )
        grad[:, p * feats:(p + 1) * feats] = jnp.dot(
            back, pieces, preferred_element_type=F32
        ).astype(BF16)
        grad_store(p).start()
    w_store.wait()
    for p in range(PIECES):
        grad_store(p).wait()


def finish(ret, dest, wgrad):
    tok, feats = dest.shape[1], ret.shape[3]
    vmem = pl.BlockSpec(memory_space=pltpu.VMEM)
    hbm = pl.BlockSpec(memory_space=pl.ANY)
    return pl.pallas_call(
        finish_kernel,
        out_shape=(
            jax.ShapeDtypeStruct((tok, PIECES * feats), BF16),
            jax.ShapeDtypeStruct(wgrad.shape, BF16),
        ),
        in_specs=[vmem, vmem, vmem],
        out_specs=(hbm, hbm),
        scratch_shapes=[
            pltpu.VMEM((tok, PIECES * feats), BF16),
            pltpu.SemaphoreType.DMA((PIECES,)), pltpu.SemaphoreType.DMA,
        ],
        compiler_params=pltpu.CompilerParams(vmem_limit_bytes=16 * 1024 * 1024),
        name="finish",
    )(dest, ret, wgrad)


def per_device(attn_out, out_cot, modality, group_modality, o_weight):
    ret, dest, wgrad = backward(
        modality.reshape(1, -1), group_modality, attn_out, out_cot, o_weight
    )
    return finish(ret, dest, wgrad)


def solution(mesh):
    return jax.shard_map(
        per_device,
        mesh=mesh,
        in_specs=(
            P(("dp", "tower"), None),
            P(("dp", "tower"), None),
            P(("dp", "tower")),
            P(),
            P("tower", None),
        ),
        out_specs=(P(("dp", "tower"), None), P("tower", "dp")),
        check_vma=False,
    )
```

```python
import jax
import jax.numpy as jnp
from jax import lax
from jax.experimental import pallas as pl
from jax.experimental.pallas import tpu as pltpu
from jax.sharding import PartitionSpec as P

NGROUP = 8
CAP = 24
NX = 4
NZ = 8
HALVES = NGROUP // NX
PIECES = NZ // HALVES
NDP = 8
CORES = 2
NY = NDP // CORES
ORDER = (0, -1, 1, -2, 2, -3, 3, 4)
PARTS = ((0, 3), (3, 2), (5, 2), (7, 1))
NC = 4
LAST = NZ // 2
TILE = 256
PLACE = {off % NZ: at for at, off in enumerate(ORDER)}
MESH = pl.DeviceIdType.MESH
F32 = jnp.float32
BF16 = jnp.bfloat16


def kernel(
    mod_ref, gm_ref, attn_hbm, cot_hbm, w_ref, ret_x, dest_ref, wgrad_ref,
    attn_ref, ring, dests, staged, cot_got, w_chunk, partial, other, terms, acc,
    attn_own, attn_x, attn_got, attn_t, grads, ret_z,
    attn_in, cot_in, dest_send, dest_recv, right_send, right_recv, left_send, left_recv,
    x_send, x_recv, x_own, ax_send, ax_recv, ax_own, az_send, az_recv, az_own,
    w_sem, pair_send, pair_recv, rs_send, rs_recv, rs_own, rz_send, rz_recv, rz_own, rx_send, rx_recv, rx_own,
):
    tok = cot_hbm.shape[0]
    width = cot_hbm.shape[1] // NC
    cols = width // NDP
    own_cols = wgrad_ref.shape[1]
    feats = w_ref.shape[0]
    half = width // 2
    me, my_d = lax.axis_index("tower"), lax.axis_index("dp")
    my_x, my_z = me // NZ, me % NZ
    my_half = my_z // PIECES
    my_y, my_core = my_d // CORES, my_d % CORES

    def at_z(k):
        return {"tower": my_x * NZ + (my_z + k + NZ) % NZ}

    def at_x(k):
        return {"tower": ((my_x + k) % NX) * NZ + my_z}

    def at_y(k):
        return {"dp": ((my_y + k) % NY) * CORES + my_core}

    other_core = {"dp": my_y * CORES + 1 - my_core}

    def remote(src, dst, send, recv, device):
        return pltpu.make_async_remote_copy(
            src_ref=src, dst_ref=dst, send_sem=send, recv_sem=recv,
            device_id=device, device_id_type=MESH,
        )

    def wait_bytes(ref, sem):
        pltpu.make_async_copy(ref, ref, sem).wait()

    def w_load(c, d):
        return pltpu.make_async_copy(
            w_ref.at[:, pl.ds(d * own_cols + c * cols, cols)],
            w_chunk.at[c % 2, :, pl.ds(d * cols, cols)],
            w_sem.at[c],
        )

    def own_block(c):
        for d in range(NDP):
            pltpu.make_async_copy(
                cot_hbm.at[:, pl.ds(d * own_cols + c * cols, cols)],
                ring.at[c, 0, :, pl.ds(d * cols, cols)],
                cot_in.at[c],
            ).start()

    attn_load = pltpu.make_async_copy(attn_hbm, attn_ref, attn_in)
    barrier = pltpu.get_barrier_semaphore()
    for k in range(1, NZ):
        pl.semaphore_signal(barrier, inc=1, device_id=at_z(k), device_id_type=MESH)
    for k in range(1, NX):
        pl.semaphore_signal(barrier, inc=1, device_id=at_x(k), device_id_type=MESH)
    for k in range(1, NY):
        pl.semaphore_signal(barrier, inc=1, device_id=at_y(k), device_id_type=MESH)
    pl.semaphore_signal(barrier, inc=1, device_id=other_core, device_id_type=MESH)

    own_block(0)
    own_block(1)
    attn_load.start()
    pl.semaphore_wait(barrier, NZ - 1 + NX - 1 + NY)

    def ring_copy(c, s, right):
        off = -s if right else s
        src = ring.at[c, off % NZ]
        dst = ring.at[c, (off - 1 if right else off + 1) % NZ]
        if s == LAST - 1:
            part = pl.ds(0, half) if right else pl.ds(half, half)
            src, dst = src.at[:, part], dst.at[:, part]
        return remote(
            src, dst,
            (right_send if right else left_send).at[c, s],
            (right_recv if right else left_recv).at[c, s],
            at_z(1 if right else -1),
        )

    for c in range(2):
        wait_bytes(ring.at[c, 0], cot_in.at[c])
        ring_copy(c, 0, True).start()
        ring_copy(c, 0, False).start()
    for c in range(2, NC):
        own_block(c)
    for c in range(2):
        for d in range(NDP):
            w_load(c, d).start()

    mod = jnp.broadcast_to(mod_ref[...], (8, tok))
    kinds = [(mod == m).astype(F32) for m in range(3)]
    t_from = lax.broadcasted_iota(jnp.int32, (tok, tok), 0)
    t_to = lax.broadcasted_iota(jnp.int32, (tok, tok), 1)
    earlier = (t_from < t_to).astype(F32).astype(BF16)
    before = jnp.dot(jnp.concatenate(kinds, 0).astype(BF16), earlier, preferred_element_type=F32)
    order = sum(before[8 * m:8 * m + 8] * kinds[m] for m in range(3))
    serves = [gm_ref[g] for g in range(NGROUP)]
    how_many = jnp.ones_like(mod)
    for m in range(3):
        count = sum((s == m).astype(jnp.int32) for s in serves)
        how_many = jnp.where(mod == m, count, how_many)
    per = how_many.astype(F32)
    turn = (order.astype(jnp.int32) + me).astype(F32)
    target = (turn - jnp.floor((turn + 0.5) / per) * per).astype(jnp.int32)
    routed = jnp.zeros_like(mod)
    for g in range(NGROUP):
        rank = sum(((s == serves[g]).astype(jnp.int32) for s in serves[:g]), jnp.int32(0))
        routed = jnp.where((mod == serves[g]) & (target == rank), g, routed)
    dest = routed * CAP + jnp.floor((order + 0.5) / per).astype(jnp.int32)
    dests[0] = dest
    dest_ref[...] = dest

    def dest_copy(k):
        return remote(dests.at[0], dests.at[NZ - k], dest_send.at[k], dest_recv.at[NZ - k], at_z(k))

    for k in range(1, NZ):
        dest_copy(k).start()

    slots = lax.broadcasted_iota(jnp.int32, (NGROUP * CAP, tok), 0)
    attn_load.wait()
    pick_own = jnp.where(slots == dest[0:1], 1.0, 0.0).astype(BF16)
    for p in range(PIECES):
        got = jnp.dot(pick_own, attn_ref[:, p * feats:(p + 1) * feats], preferred_element_type=F32)
        attn_own[:, :, :, p * feats:(p + 1) * feats] = got.astype(BF16).reshape(NX, HALVES, CAP, feats)

    def attn_x_copy(k):
        return remote(
            attn_own.at[(my_x + k) % NX], attn_x.at[my_x], ax_send.at[k], ax_recv.at[NX - k], at_x(k)
        )

    own_ax = pltpu.make_async_copy(attn_own.at[my_x], attn_x.at[my_x], ax_own)
    own_ax.start()
    for k in range(1, NX):
        attn_x_copy(k).start()

    def attn_z_src(k):
        z = (my_z + k) % NZ
        start = pl.multiple_of((z % PIECES) * feats, feats)
        return attn_x.at[:, z // PIECES, :, pl.ds(start, feats)]

    def attn_z_copy(k):
        return remote(
            attn_z_src(k), attn_got.at[:, PLACE[NZ - k]], az_send.at[k], az_recv.at[NZ - k], at_z(k)
        )

    def attn_along_z():
        own_ax.wait()
        for k in range(1, NX):
            attn_x_copy(k).wait_recv()
        pltpu.make_async_copy(attn_z_src(0), attn_got.at[:, 0], az_own).start()
        for k in (3, 4, 5):
            attn_z_copy(k).start()

    def attn_arrived():
        pltpu.make_async_copy(attn_z_src(0), attn_got.at[:, 0], az_own).wait()
        for k in range(1, NZ):
            attn_z_copy(k).wait_recv()

        @pl.loop(0, feats // TILE)
        def _(j):
            at = pl.ds(pl.multiple_of(j * TILE, TILE), TILE)
            attn_t[at, :] = jnp.transpose(attn_got[:, :, :, at].reshape(NX * NZ * CAP, TILE))

    rows = lax.broadcasted_iota(jnp.int32, (NX * CAP, tok), 0)
    x_of = sum((rows >= CAP * k).astype(jnp.int32) for k in range(1, NX))
    wanted = rows + CAP * (HALVES - 1) * x_of + CAP * my_half

    def deliver(c, *offsets):
        at = pl.ds(PLACE[offsets[0] % NZ], len(offsets))
        for off in offsets:
            slot = off % NZ
            pick = jnp.where(wanted == dests[slot, 0:1, :], 1.0, 0.0).astype(BF16)
            got = jnp.dot(pick, ring[c, slot], preferred_element_type=F32).astype(BF16)
            for x in range(NX):
                staged[c, x, PLACE[slot]] = got[x * CAP:(x + 1) * CAP]
        part = max(abs(offsets[0]), 1) - 1
        lands = cot_got.at[c, my_x, at]
        for k in range(1, NX):
            src = staged.at[c, (my_x + k) % NX, at]
            remote(src, lands, x_send.at[c, k], x_recv.at[c, part, NX - k], at_x(k)).start()
        pltpu.make_async_copy(staged.at[c, my_x, at], lands, x_own.at[c, part]).start()

    def arrived(c, parts):
        for part in parts:
            count = PARTS[part][1]
            wait_bytes(staged.at[c, 0, pl.ds(0, count)], x_own.at[c, part])
            for k in range(1, NX):
                wait_bytes(staged.at[c, k, pl.ds(0, count)], x_recv.at[c, part, k])

    def x_sends_done(c):
        for k in range(1, NX):
            wait_bytes(staged.at[c, k], x_send.at[c, k])

    def input_grad(c):
        wait_bytes(w_chunk.at[c % 2], w_sem.at[c])

        @pl.loop(0, feats // TILE)
        def _(j):
            at = pl.ds(pl.multiple_of(j * TILE, TILE), TILE)
            term = lax.dot_general(
                cot_got[c].reshape(NX * NZ * CAP, width), w_chunk[c % 2, at, :],
                (((1,), (1,)), ((), ())), preferred_element_type=F32,
            )
            term = term.reshape(NX, NZ, CAP, TILE)
            acc[:, :, :, at] = term if c == 0 else acc[:, :, :, at] + term

        for d in range(NDP):
            w_load(c + 2, d).start()

    def rows_grad(part):
        first, count = PARTS[part]
        own = slice(first, first + count)

        @pl.loop(0, feats // TILE)
        def _(j):
            at = pl.ds(pl.multiple_of(j * TILE, TILE), TILE)
            term = sum(
                lax.dot_general(
                    cot_got[c, :, own].reshape(NX * count * CAP, width), w_chunk[c % 2, at, :],
                    (((1,), (1,)), ((), ())), preferred_element_type=F32,
                )
                for c in range(NC - 2, NC)
            )
            total = term.reshape(NX, count, CAP, TILE) + acc[:, own, :, at]
            grads[:, own, :, at] = total.astype(BF16)

        for off in ORDER[own]:
            if off == 0:
                pltpu.make_async_copy(grads.at[:, 0], ret_z.at[my_z], rz_own).start()
            else:
                ret_z_copy(off % NZ).start()

    def pair_copy(c):
        return remote(
            partial.at[c % 2, 1 - my_core], other.at[c], pair_send.at[c], pair_recv.at[c], other_core
        )

    def rs_copy(c, k):
        return remote(
            partial.at[c % 2, my_core, (my_y + k) % NY], terms.at[c, my_y],
            rs_send.at[c, k], rs_recv.at[c, NY - k], at_y(k),
        )

    def rs_own_copy(c):
        return pltpu.make_async_copy(
            partial.at[c % 2, my_core, my_y], terms.at[c, my_y], rs_own.at[c]
        )

    def weight_sends_done(c):
        pair_copy(c).wait_send()
        for k in range(1, NY):
            rs_copy(c, k).wait_send()
        rs_own_copy(c).wait()

    def weight_grad(c):
        if c >= 2:
            weight_sends_done(c - 2)

        @pl.loop(0, width // TILE)
        def _(j):
            at = pl.ds(pl.multiple_of(j * TILE, TILE), TILE)
            term = jnp.dot(
                attn_t[...], cot_got[c, :, :, :, at].reshape(NX * NZ * CAP, TILE),
                preferred_element_type=F32,
            ).astype(BF16)
            for i in range(CORES):
                partial[c % 2, i, j] = term[:, i * cols:(i + 1) * cols]

        pair_copy(c).start()

    def weight_pair(c):
        pair_copy(c).wait_recv()

        for k in (1, 2, 3, 0):
            y = (my_y + k) % NY

            @pl.loop(0, feats // TILE)
            def _(j):
                at = pl.ds(pl.multiple_of(j * TILE, TILE), TILE)
                both = partial[c % 2, my_core, y, at, :].astype(F32) + other[c, y, at, :].astype(F32)
                partial[c % 2, my_core, y, at, :] = both.astype(BF16)

            if k == 0:
                rs_own_copy(c).start()
            else:
                rs_copy(c, k).start()

    def weight_grad_sum(c):
        if c >= NC - 2:
            rs_own_copy(c).wait()
        for k in range(1, NY):
            rs_copy(c, k).wait_recv()

        @pl.loop(0, feats // TILE)
        def _(j):
            at = pl.ds(pl.multiple_of(j * TILE, TILE), TILE)
            total = terms[c, 0, at, :].astype(F32)
            for y in range(1, NY):
                total += terms[c, y, at, :].astype(F32)
            wgrad_ref[at, c * cols:(c + 1) * cols] = total.astype(BF16)

    def ret_z_copy(k):
        return remote(
            grads.at[:, PLACE[k]], ret_z.at[my_z], rz_send.at[k], rz_recv.at[NZ - k], at_z(k)
        )

    def ring_step(c, s):
        if c >= 2 and s == 0:
            wait_bytes(ring.at[c, 0], cot_in.at[c])
        for right in (True, False):
            if s > 0:
                ring_copy(c, s - 1, right).wait_recv()
            if s < LAST and (c >= 2 or s > 0):
                ring_copy(c, s, right).start()
        if (c, s) == (0, 1):
            for k in range(1, NZ):
                dest_copy(k).wait_recv()
        if s in (0, LAST):
            deliver(c, s)
        else:
            deliver(c, -s, s)

    for c, s in ((0, 0), (1, 0), (0, 1), (1, 1), (0, 2)):
        ring_step(c, s)
    attn_along_z()
    every = range(len(PARTS))
    for c, s in ((1, 2), (0, 3), (2, 0), (1, 3), (3, 0)):
        ring_step(c, s)
    for k in (1, 2, 6, 7):
        attn_z_copy(k).start()
    for c, s in ((0, 4), (2, 1), (1, 4)):
        ring_step(c, s)
    arrived(0, every)
    input_grad(0)
    ring_step(3, 1)
    arrived(1, every)
    input_grad(1)
    ring_step(2, 2)
    attn_arrived()
    weight_grad(0)
    ring_step(3, 2)
    weight_grad(1)
    weight_pair(0)
    ring_step(2, 3)
    for c in range(NC - 2, NC):
        wait_bytes(w_chunk.at[c % 2], w_sem.at[c])
        arrived(c, (0,))
    rows_grad(0)
    ring_step(3, 3)
    weight_pair(1)
    ring_step(2, 4)
    for c in range(NC - 2, NC):
        arrived(c, (1,))
    rows_grad(1)
    arrived(2, (2, 3))
    weight_grad(2)
    arrived(3, (2,))
    rows_grad(2)
    ring_step(3, 4)
    weight_pair(2)
    arrived(3, (3,))
    weight_grad(3)
    rows_grad(3)
    weight_pair(3)
    weight_grad_sum(0)
    weight_grad_sum(1)

    def ret_x_start(z):
        for k in range(NX):
            src, dst = ret_z.at[z, (my_x + k) % NX], ret_x.at[my_x, z]
            if k == 0:
                pltpu.make_async_copy(src, dst, rx_own).start()
            else:
                remote(src, dst, rx_send.at[k], rx_recv.at[NX - k], at_x(k)).start()

    pltpu.make_async_copy(grads.at[:, 0], ret_z.at[my_z], rz_own).wait()
    ret_x_start(my_z)
    for k in (1, 7, 2, 6, 3, 5, 4):
        ret_z_copy(k).wait_recv()
        ret_x_start((my_z - k + NZ) % NZ)
    weight_grad_sum(2)
    weight_grad_sum(3)
    for k in range(NX):
        wait_bytes(ret_x.at[k], rx_own if k == 0 else rx_recv.at[k])

    for k in range(1, NZ):
        dest_copy(k).wait_send()
        attn_z_copy(k).wait_send()
        ret_z_copy(k).wait_send()
    for k in range(1, NX):
        attn_x_copy(k).wait_send()
        wait_bytes(ret_x.at[k], rx_send.at[k])
    for c in range(NC):
        for s in range(LAST):
            ring_copy(c, s, True).wait_send()
            ring_copy(c, s, False).wait_send()
        x_sends_done(c)
    for c in range(NC - 2, NC):
        pair_copy(c).wait_send()
        for k in range(1, NY):
            rs_copy(c, k).wait_send()


def backward(mod, gm, attn, cot, w):
    tok, model = cot.shape
    width = model // NC
    feats = w.shape[0]
    dma = pltpu.SemaphoreType.DMA
    vmem = pl.BlockSpec(memory_space=pltpu.VMEM)
    hbm = pl.BlockSpec(memory_space=pl.ANY)
    return pl.pallas_call(
        kernel,
        out_shape=(
            pltpu.VMEM((NX, NZ, CAP, feats), BF16),
            pltpu.VMEM((8, tok), jnp.int32),
            pltpu.VMEM((feats, model // NDP), BF16),
        ),
        in_specs=[
            vmem, pl.BlockSpec(memory_space=pltpu.SMEM), hbm, hbm, hbm,
        ],
        out_specs=(vmem, vmem, vmem),
        scratch_shapes=[
            pltpu.VMEM((tok, model), BF16),
            pltpu.VMEM((NC, NZ, tok, width), BF16),
            pltpu.VMEM((NZ, 8, tok), jnp.int32),
            pltpu.VMEM((NC, NX, NZ, CAP, width), BF16),
            pltpu.VMEM((NC, NX, NZ, CAP, width), BF16),
            pltpu.VMEM((2, feats, width), BF16),
            pltpu.VMEM((2, CORES, NY, feats, width // NDP), BF16),
            pltpu.VMEM((NC, NY, feats, width // NDP), BF16),
            pltpu.VMEM((NC, NY, feats, width // NDP), BF16),
            pltpu.VMEM((NX, NZ, CAP, feats), F32),
            pltpu.VMEM((NX, HALVES, CAP, model), BF16),
            pltpu.VMEM((NX, HALVES, CAP, model), BF16),
            pltpu.VMEM((NX, NZ, CAP, feats), BF16),
            pltpu.VMEM((feats, NX * NZ * CAP), BF16),
            pltpu.VMEM((NX, NZ, CAP, feats), BF16),
            pltpu.VMEM((NZ, NX, CAP, feats), BF16),
            dma, dma((NC,)), dma((NZ,)), dma((NZ,)),
            dma((NC, LAST)), dma((NC, LAST)), dma((NC, LAST)), dma((NC, LAST)),
            dma((NC, NX)), dma((NC, LAST, NX)), dma((NC, LAST)),
            dma((NX,)), dma((NX,)), dma,
            dma((NZ,)), dma((NZ,)), dma,
            dma((NC,)),
            dma((NC,)), dma((NC,)), dma((NC, NY)), dma((NC, NY)), dma((NC,)),
            dma((NZ,)), dma((NZ,)), dma,
            dma((NX,)), dma((NX,)), dma,
        ],
        compiler_params=pltpu.CompilerParams(
            collective_id=0, has_side_effects=True, vmem_limit_bytes=58 * 1024 * 1024
        ),
        name="moe_proj_backward",
    )(mod, gm, attn, cot, w)


def finish_kernel(dest_ref, ret, wgrad, grad_hbm, w_out, grad, grad_out, w_sent):
    tok, feats = dest_ref.shape[1], ret.shape[3]
    w_store = pltpu.make_async_copy(wgrad, w_out, w_sent)
    w_store.start()

    def grad_store(p):
        at = pl.ds(p * feats, feats)
        return pltpu.make_async_copy(grad.at[:, at], grad_hbm.at[:, at], grad_out.at[p])

    slots = lax.broadcasted_iota(jnp.int32, (NGROUP * CAP, tok), 0)
    back = jnp.where(slots == dest_ref[0:1, :], 1.0, 0.0).T.astype(BF16)
    for p in range(PIECES):
        pieces = jnp.concatenate(
            [ret[g // HALVES, (g % HALVES) * PIECES + p] for g in range(NGROUP)], 0
        )
        grad[:, p * feats:(p + 1) * feats] = jnp.dot(
            back, pieces, preferred_element_type=F32
        ).astype(BF16)
        grad_store(p).start()
    w_store.wait()
    for p in range(PIECES):
        grad_store(p).wait()


def finish(ret, dest, wgrad):
    tok, feats = dest.shape[1], ret.shape[3]
    vmem = pl.BlockSpec(memory_space=pltpu.VMEM)
    hbm = pl.BlockSpec(memory_space=pl.ANY)
    return pl.pallas_call(
        finish_kernel,
        out_shape=(
            jax.ShapeDtypeStruct((tok, PIECES * feats), BF16),
            jax.ShapeDtypeStruct(wgrad.shape, BF16),
        ),
        in_specs=[vmem, vmem, vmem],
        out_specs=(hbm, hbm),
        scratch_shapes=[
            pltpu.VMEM((tok, PIECES * feats), BF16),
            pltpu.SemaphoreType.DMA((PIECES,)), pltpu.SemaphoreType.DMA,
        ],
        compiler_params=pltpu.CompilerParams(vmem_limit_bytes=16 * 1024 * 1024),
        name="finish",
    )(dest, ret, wgrad)


def per_device(attn_out, out_cot, modality, group_modality, o_weight):
    ret, dest, wgrad = backward(
        modality.reshape(1, -1), group_modality, attn_out, out_cot, o_weight
    )
    return finish(ret, dest, wgrad)


def solution(mesh):
    return jax.shard_map(
        per_device,
        mesh=mesh,
        in_specs=(
            P(("dp", "tower"), None),
            P(("dp", "tower"), None),
            P(("dp", "tower")),
            P(),
            P("tower", None),
        ),
        out_specs=(P(("dp", "tower"), None), P("tower", "dp")),
        check_vma=False,
    )
```
